32 devices in a mesh: rows: 8 (over z, y), seq: 4 (over x, core).
Axes of the slice: x: 2, y: 2, z: 4, core: 2. Of those that a mesh axis runs over, the one named last changes fastest.
Arguments:
- byte_ids: int32 [32, 2048], P('rows', 'seq'), may hold values from 0 to 255
- lengths: int32 [32], P('rows'), may hold values from 385 to 2048, as said below
- embed: float32 [256, 768], replicated, may hold values from -6 to 6
- conv_weight: float32 [4, 768], replicated, may hold values from -3 to 3
- conv_bias: float32 [768], replicated, may hold values from -3 to 3
- score_weight: float32 [768], replicated, may hold values from -0.4375 to 0.4375
- out_grad: float32 [32, 1024, 768], P('rows', 'seq'), may hold values from -6 to 6
Outputs:
- blocks_out: float32 [32, 1024, 768], P('rows', 'seq')
- embed_grad: float32 [256, 768], replicated
- convolution_tap_gradient: float32 [4, 768], replicated
- conv_bias_grad: float32 [768], replicated
- score_weight_grad: float32 [768], replicated
The draws below stay inside these ranges and needn't reach their ends.
Inputs may be any that keep to these rules, and one draw needn't show every extreme that they name: `lengths`: real bytes of each row; the first row has 2048.
All inputs are finite; a program needn't handle non-finite values.
Results may differ from the reference program's by a relative error of at most 0.0003.
Values sent between devices are 32-bit elements; how exact they have to be, the bound alone decides.
No kernel may reach another device: no remote copies, remote signals or barrier semaphores. Data moves between devices by JAX's collectives and lax.ppermute only.
A program may use at most 192 MiB of HBM per device.

```python
import jax
import jax.numpy as jnp
from jax import lax

D = 768
VOCAB = 256
KERNEL = 4
LMAX = 2048
HALF = 1024
ROWS = 32


def draw_lengths(key, part):
    bucket_key = jax.random.fold_in(key, 11)
    cut_key = jax.random.fold_in(key, 23)
    bucket = jax.random.randint(bucket_key, (ROWS,), 0, 3)
    base = jnp.right_shift(jnp.full((ROWS,), LMAX, jnp.int32), bucket.astype(jnp.int32))
    raw = jax.random.randint(cut_key, (ROWS,), 0, 1 << 30)
    cut = raw % (base // 4)
    lengths = (base - cut).astype(jnp.int32)
    return lengths.at[0].set(LMAX)


def set_ends(drawn, key, least, high):
    extent = drawn.shape
    place = [jax.random.randint(jax.random.fold_in(key, axis), (), 0, extent[axis]) for axis in range(len(extent))]
    drawn = drawn.at[tuple(place)].set(least)
    longest = extent.index(max(extent))
    place[longest] = (place[longest] + 1) % extent[longest]
    return drawn.at[tuple(place)].set(high)


def block_scale(key, dims, shards, smallest, largest):
    factor_of, own = 1.0, jax.random.fold_in(key, 6)
    for axis_at, blocks in shards:
        heights = jnp.exp(jax.random.uniform(jax.random.fold_in(own, axis_at), (blocks,), jnp.float32, smallest / len(shards), largest / len(shards)))
        factor_of = factor_of * jnp.repeat(heights, dims[axis_at] // blocks).reshape([-1 if axis == axis_at else 1 for axis in range(len(dims))])
    return factor_of


def gaussian(key, extent, scale, reach, split=(), held_as=jnp.bfloat16):
    values = jax.random.normal(key, extent, jnp.float32) * scale
    if len(split) > 0:
        values = block_scale(key, extent, split, -0.22, 0.18) * values
    return jnp.clip(values, min=-reach, max=reach).astype(held_as)


def setup_inputs(seed: int = 0) -> dict:
    keys = jax.random.split(jax.random.key(seed), 8)
    return {
        "byte_ids": set_ends(jax.random.randint(keys[0], (ROWS, LMAX), 0, VOCAB), jax.random.fold_in(keys[0], 1), 0, VOCAB - 1).astype(jnp.int32),
        "lengths": draw_lengths(jax.random.fold_in(keys[7], 71), 0),
        "embed": gaussian(keys[2], (VOCAB, D), 1.0, 6.0, (), jnp.float32),
        "conv_weight": gaussian(keys[3], (KERNEL, D), KERNEL ** -0.5, 3.0, (), jnp.float32),
        "conv_bias": gaussian(keys[4], (D,), 0.5, 3.0, (), jnp.float32),
        "score_weight": gaussian(keys[5], (D,), (D // 4) ** -0.5, 0.4375, (), jnp.float32),
        "out_grad": gaussian(keys[6], (ROWS, HALF, D), 1.0, 6.0, ((0, 8), (1, 4)), jnp.float32),
    }


eps_value = 1e-06
high_precision = lax.Precision.HIGHEST

@jax.custom_vjp
def low(v):
    return lax.optimization_barrier(v.astype(jnp.bfloat16)).astype(jnp.float32)

@jax.custom_vjp
def low_back(v):
    return v

def low_keep(v):
    return (low(v), None)

def low_pass(kept, grad):
    return (grad,)

def back_keep(v):
    return (v, None)

def back_low(kept, grad):
    return (low(grad),)
low.defvjp(low_keep, low_pass)
low_back.defvjp(back_keep, back_low)

def root_mean(total, count, width):
    return jnp.sqrt(total / (count * width) + eps_value)

def conv_rows(padded, conv_weight, conv_bias, width):
    total = conv_bias
    for tap in range(conv_weight.shape[0]):
        total = total + conv_weight[tap] * padded[:, tap:tap + width]
    return total

def pool_blocks(own, mask, ext, mask_ext, start):
    rows, width, feat = own.shape
    pooled = []
    for size in (1, 2, 3, 4):
        if size == 3:
            phase = (start + jnp.arange(width, dtype=jnp.int32)) % 3
            total = jnp.zeros_like(own)
            count = jnp.zeros_like(mask)
            for offset in range(-2, 3):
                inside = ((phase + offset >= 0) & (phase + offset < 3)).astype(jnp.float32)
                total = total + inside[None, :, None] * ext[:, 2 + offset:2 + offset + width]
                count = count + inside[None, :] * mask_ext[:, 2 + offset:2 + offset + width]
        else:
            total = jnp.repeat(own.reshape(rows, width // size, size, feat).sum(2), size, axis=1)
            count = jnp.repeat(mask.reshape(rows, width // size, size).sum(2), size, axis=1)
        pooled.append(total / jnp.maximum(count, 1.0)[:, :, None])
    return jnp.stack(pooled)

def mix_blocks(pooled, score_weight, mask):
    scores = jnp.einsum('brwd,d->brw', pooled, score_weight, precision=high_precision)
    probs = jax.nn.softmax(scores, axis=0)
    return lax.optimization_barrier(jnp.sum(probs[..., None] * pooled, axis=0)) * mask[..., None]

def halve(element_numbers, mask):
    rows, width, feat = element_numbers.shape
    total = element_numbers.reshape(rows, width // 2, 2, feat).sum(2)
    count = mask.reshape(rows, width // 2, 2).sum(2)
    return (total / jnp.maximum(count, 1.0)[..., None], mask[:, 0::2])

def forward(embed, conv_weight, conv_bias, score_weight, byte_ids, lengths):
    width = byte_ids.shape[1]
    feat = embed.shape[1]
    lead = conv_weight.shape[0] - 1
    places = jnp.arange(width, dtype=jnp.int32)
    mask = (places[None, :] < lengths[:, None]).astype(jnp.float32)
    count = jnp.sum(mask)
    emb = jnp.take(embed, byte_ids, axis=0) * mask[:, :, None]
    act = emb / root_mean(jnp.sum(emb * emb), count, feat)
    padded = jnp.pad(act, ((0, 0), (lead, 0), (0, 0)))
    conv = conv_rows(padded, conv_weight, conv_bias, width) * mask[:, :, None]
    normed = conv / root_mean(jnp.sum(conv * conv), count, feat)
    ext = jnp.pad(normed, ((0, 0), (2, 2), (0, 0)))
    mask_ext = jnp.pad(mask, ((0, 0), (2, 2)))
    pooled = pool_blocks(normed, mask, ext, mask_ext, 0)
    mixed = mix_blocks(pooled, score_weight, mask)
    hidden_result = mixed / root_mean(jnp.sum(mixed * mixed), count, feat)
    coarsened_sequences, down_mask = halve(hidden_result, mask)
    return coarsened_sequences / root_mean(jnp.sum(coarsened_sequences * coarsened_sequences), jnp.sum(down_mask), feat)

def reference(byte_ids, lengths, embed, conv_weight, conv_bias, score_weight, out_grad):

    def run(table, taps, bias, scorer):
        return forward(table, taps, bias, scorer, byte_ids, lengths)
    blocks_out, pull = jax.vjp(run, embed, conv_weight, conv_bias, score_weight)
    grads = pull(out_grad)
    return (blocks_out, grads[0], grads[1], grads[2], grads[3])
```

```python
import functools

import jax
import jax.numpy as jnp
from jax import lax
from jax.experimental import pallas as pl
from jax.experimental.pallas import tpu as pltpu
from jax.sharding import PartitionSpec as P

f32 = jnp.float32
EPS = 1e-06
HIGH = lax.Precision.HIGHEST
LANES = 128
RUNS = 8
OFF = 8
LEFT, RIGHT = 5, 2
NT = (((1,), (1,)), ((), ()))
TN = (((0,), (0,)), ((), ()))
AXES = ("rows", "seq")
VMEM = pl.BlockSpec(memory_space=pltpu.VMEM)
SMEM = pl.BlockSpec(memory_space=pltpu.SMEM)


def iota(shape, dim):
    return lax.broadcasted_iota(jnp.int32, shape, dim)


def shifted(x, by):
    return x if by == 0 else pltpu.roll(x, (-by) % LANES, 1)


def as_tiles(x):
    n, feat = x.shape
    return x.reshape(n // 8, 8, feat // LANES, LANES).transpose(0, 2, 1, 3).reshape(n * feat // LANES, LANES)


def from_tiles(x, feat):
    n = x.shape[0] * LANES // feat
    return x.reshape(n // 8, feat // LANES, 8, LANES).transpose(0, 2, 1, 3).reshape(n, feat)


def pair_rows(r, k, tile, half, tiles):
    first = ((r * RUNS * (half // 8) + k // 8) * tiles + tile) * 8 + k % 8
    return pl.ds(first, RUNS, stride=half // 8 * tiles * 8)


def prep_kernel(embed_ref, taps_ref, bias_ref, scorer_ref, split_ref, table_ref):
    embed = embed_ref[...]
    high = embed.astype(jnp.bfloat16)
    split_ref[0] = high
    split_ref[1] = (embed - high.astype(f32)).astype(jnp.bfloat16)
    taps = taps_ref[...]
    rows = jnp.concatenate([taps * scorer_ref[...], taps * bias_ref[...]], axis=0)
    table_ref[0:8, :] = lax.dot_general(rows, embed, NT, precision=HIGH, preferred_element_type=f32)
    table_ref[8:16, :] = lax.dot_general(
        jnp.ones_like(rows), embed * embed, NT, precision=HIGH, preferred_element_type=f32
    )


def stats_kernel(
    sizes, own_ref, left_ref, right_ref, len_ref, split_ref, table_ref, taps_ref, bias_ref, grad_ref,
    emb_ref, conv_ref, ids_ref, dots_ref, sums_ref,
):
    rows, width, run, feat, vocab, kernel = sizes
    tiles = feat // LANES
    start = lax.axis_index("seq") * width
    lane = iota((RUNS, LANES), 1)
    sub = iota((RUNS, LANES), 0)
    base = start + run * sub
    back = (OFF - run) % LANES

    for r in range(rows):
        own = own_ref[r * RUNS : (r + 1) * RUNS, :]
        before = pltpu.roll(pltpu.roll(own, 1, 0), back, 1)
        edge = pltpu.roll(jnp.broadcast_to(left_ref[r : r + 1, width - LANES : width], (RUNS, LANES)), OFF, 1)
        before = jnp.where(sub == 0, edge, before)
        after = pltpu.roll(pltpu.roll(own, RUNS - 1, 0), OFF + run, 1)
        edge = pltpu.roll(jnp.broadcast_to(right_ref[r : r + 1, 0:LANES], (RUNS, LANES)), OFF + run, 1)
        after = jnp.where(sub == RUNS - 1, edge, after)
        ids = jnp.where(lane < OFF, before, jnp.where(lane < OFF + run, pltpu.roll(own, OFF, 1), after))
        place = base + lane - OFF
        real = (place >= 0) & (place < len_ref[r])
        real = real & (lane >= OFF - LEFT) & (lane < OFF + run + RIGHT)
        ids_ref[r * RUNS : (r + 1) * RUNS, :] = jnp.where(real, ids, -1)

    group = 8
    vr = rows * RUNS
    for first in range(0, emb_ref.shape[0], group):
        marks = []
        for i in range(first, first + group):
            column = ids_ref[:, i + OFF - LEFT : i + OFF - LEFT + 1]
            marks.append((column == iota((vr, vocab), 1)).astype(f32))
        onehot = jnp.concatenate(marks, axis=0).astype(jnp.bfloat16)
        total = jnp.dot(onehot, split_ref[0], preferred_element_type=f32)
        total = total + jnp.dot(onehot, split_ref[1], preferred_element_type=f32)
        emb_ref[first : first + group] = total.reshape(group, vr, feat)

    def convolve(step, carry):
        r, tile = step // tiles, step % tiles
        at = (pl.ds(pl.multiple_of(r * RUNS, RUNS), RUNS), pl.ds(pl.multiple_of(tile * LANES, LANES), LANES))
        length = len_ref[r]
        taps = [jnp.broadcast_to(taps_ref[k : k + 1, at[1]], (RUNS, LANES)) for k in range(kernel)]
        window = [emb_ref[k, at[0], at[1]] for k in range(kernel - 1)]
        for j in range(-2, run + 2):
            window.append(emb_ref[j + LEFT, at[0], at[1]])
            total = taps[0] * window[0]
            for k in range(1, kernel):
                total = total + taps[k] * window[k]
            window = window[1:]
            real = base < length - j
            if j < 0:
                real = real & (base >= -j)
            conv_ref[j + 2, at[0], at[1]] = jnp.where(real, total, 0.0)
        return carry

    lax.fori_loop(0, rows * tiles, convolve, 0)

    dots_ref[...] = jnp.zeros_like(dots_ref)
    block = 4
    slices = run + 4

    def lagged(step, carry):
        r, first = step // (slices // block), step % (slices // block) * block
        at = pl.ds(pl.multiple_of(r * RUNS, RUNS), RUNS)
        acc = {}
        for tile in range(tiles):
            cols = slice(tile * LANES, (tile + 1) * LANES)
            u = [conv_ref[first + i, at, cols] for i in range(block + 5)]
            for i in range(block):
                for lag in range(6):
                    term = u[i] * u[i + lag]
                    acc[i, lag] = term if tile == 0 else acc[i, lag] + term
        for lag in range(6):
            value = dots_ref[lag, at, :]
            for i in range(block):
                here = lane == first + (i + OFF - 2)
                value = jnp.where(here, jnp.sum(acc[i, lag], axis=1, keepdims=True), value)
            dots_ref[lag, at, :] = value
        return carry

    for i in range(slices, slices + 8):
        conv_ref[i] = jnp.zeros_like(conv_ref[i])
    lax.fori_loop(0, rows * (slices // block), lagged, 0)

    half = run // 2

    def crossed(step, carry):
        r, first = step // (half // block), step % (half // block) * block
        at = pl.ds(pl.multiple_of(r * RUNS, RUNS), RUNS)
        acc = {}
        for tile in range(tiles):
            cols = slice(tile * LANES, (tile + 1) * LANES)
            u = [conv_ref[2 * first + i, at, cols] for i in range(2 * block + 4)]
            bias = jnp.broadcast_to(bias_ref[:, cols], (RUNS, LANES))
            for i in range(block):
                g = grad_ref[pair_rows(r, first + i, tile, half, tiles), :]
                terms = [g * u[2 * i + d] for d in range(6)] + [g * bias]
                for d in range(7):
                    acc[i, d] = terms[d] if tile == 0 else acc[i, d] + terms[d]
        for d in range(7):
            value = dots_ref[6 + d, at, :]
            for i in range(block):
                here = lane == 2 * first + (2 * i + OFF)
                value = jnp.where(here, jnp.sum(acc[i, d], axis=1, keepdims=True), value)
            dots_ref[6 + d, at, :] = value
        return carry

    lax.fori_loop(0, rows * (half // block), crossed, 0)

    def total_of(x):
        return jnp.sum(jnp.sum(x, axis=1, keepdims=True), axis=0, keepdims=True)

    sums = [jnp.zeros((1, 1), f32) for _ in range(5)]
    for r in range(rows):
        at = slice(r * RUNS, (r + 1) * RUNS)
        ids = ids_ref[at, :]
        real = ids >= 0
        low = jnp.where(real, ids, 0)

        def look(row):
            value = jnp.zeros((RUNS, LANES), f32)
            for part in range(vocab // LANES):
                entry = jnp.broadcast_to(
                    table_ref[row : row + 1, part * LANES : (part + 1) * LANES], (RUNS, LANES)
                )
                picked = jnp.take_along_axis(entry, low % LANES, axis=1)
                value = jnp.where(low // LANES == part, picked, value)
            return jnp.where(real, value, 0.0)

        scored = jnp.zeros((RUNS, LANES), f32)
        biased = jnp.zeros((RUNS, LANES), f32)
        for k in range(kernel):
            scored = scored + shifted(look(k), k - (kernel - 1))
            biased = biased + shifted(look(4 + k), k - (kernel - 1))
        inner = real & (lane >= OFF - 2)
        scored = jnp.where(inner, scored, 0.0)
        biased = jnp.where(inner, biased, 0.0)
        dots_ref[13, at, :] = scored
        dots_ref[14, at, :] = biased
        own = (real & (lane >= OFF) & (lane < OFF + run)).astype(f32)
        for i, x in enumerate((
            own * look(8), own, own * biased, own * dots_ref[0, at, :], own * (1 - lane % 2).astype(f32)
        )):
            sums[i] = sums[i] + total_of(x)
    sums_ref[...] = spread(sums, sums_ref.shape[0])


def spread(sums, count):
    lane = iota((1, LANES), 1)
    row = jnp.zeros((1, LANES), f32)
    for i, x in enumerate(sums):
        row = jnp.where(lane == i, x, row)
    return jnp.broadcast_to(row[None], (count, 1, LANES))


def picked(ref, number):
    row = jnp.sum(ref[...], axis=0)
    return [row[:, i : i + 1] for i in range(number)]


def scales(first_ref, bias, feat):
    emb_sum, count, cross, square, count4 = picked(first_ref, 5)
    one = jnp.sqrt(emb_sum / (count * feat) + EPS)
    bias_sum = jnp.sum(bias * bias, axis=1, keepdims=True)
    conv_sum = jnp.maximum(count * bias_sum + 2.0 * cross / one + square / (one * one), 0.0)
    two = jnp.sqrt(conv_sum / (count * feat) + EPS)
    return one, two, count, count4, bias_sum, cross


class Places:
    def __init__(self, ids, start, run):
        shape = ids.shape
        self.j = iota(shape, 1) - OFF
        sub = iota(shape, 0) % RUNS
        self.inside = (self.j >= 0) & (self.j < run)
        self.real = ((ids >= 0) & (self.j >= -2)).astype(f32)
        self.own = jnp.where(self.inside, self.real, 0.0)
        shown = self.j + OFF
        self.two, self.four = shown % 2, shown % 4
        self.three = (start + run * sub + shown + (3 * OFF - OFF)) % 3

    def holds(self, size, by):
        if size == 1:
            return jnp.ones_like(self.real) if by == 0 else None
        if abs(by) >= size:
            return None
        phase = {2: self.two, 3: self.three, 4: self.four}[size]
        return ((phase + by >= 0) & (phase + by < size)).astype(f32)

    def pooled(self, size, x):
        if size == 1:
            return x
        pair = x + jnp.where(self.two == 0, shifted(x, 1), shifted(x, -1))
        if size == 2:
            return pair
        if size == 4:
            return pair + jnp.where(self.four < 2, shifted(pair, 2), shifted(pair, -2))
        left, right = shifted(x, -1), shifted(x, 1)
        side = jnp.where(self.three == 0, shifted(x, 2), left)
        far = jnp.where(self.three == 2, shifted(x, -2), right)
        return x + side + far

    def both(self, x):
        return x + shifted(x, -1)


SIZES = (1, 2, 3, 4)
REACH = range(-3, 4)


def score_kernel(sizes, first_ref, ids_ref, dots_ref, bias_ref, scorer_ref, state_ref, sums_ref):
    rows, width, run, feat, vocab, kernel = sizes
    start = lax.axis_index("seq") * width
    bias = bias_ref[...]
    one, two, count, count4, bias_sum, cross = scales(first_ref, bias, feat)
    at = Places(ids_ref[...], start, run)
    real, own = at.real, at.own
    rate = 1.0 / (one * two)
    bias_score = jnp.sum(bias * scorer_ref[...], axis=1, keepdims=True) / two

    normed_score = real * bias_score + rate * dots_ref[13]
    counts = [jnp.maximum(at.pooled(b, real), 1.0) for b in SIZES]
    scores = [at.pooled(b, normed_score) / n for b, n in zip(SIZES, counts)]
    top = functools.reduce(jnp.maximum, scores)
    parts = [jnp.exp(s - top) for s in scores]
    whole = sum(parts)
    probs = [p / whole for p in parts]
    weights = [own * p / n for p, n in zip(probs, counts)]

    holds = {(b, d): at.holds(b, d) for b in SIZES for d in REACH}

    def blend(values):
        out = {}
        for d in REACH:
            terms = [v * holds[b, d] for b, v in zip(SIZES, values) if holds[b, d] is not None]
            out[d] = sum(terms)
        return out

    mixer = blend(weights)
    pair_count = jnp.maximum(at.pooled(2, real), 1.0)
    halver = {}
    even = at.two == 0
    for d in REACH:
        zero = jnp.zeros_like(real)
        ahead = shifted(mixer[d - 1], 1) if d - 1 >= -3 else zero
        behind = shifted(mixer[d + 1], -1) if d + 1 <= 3 else zero
        other = jnp.where(even, ahead, behind)
        halver[d] = jnp.where(at.inside, (mixer[d] + other) / pair_count, 0.0)

    bias_dot = dots_ref[14]
    normed_bias = real * (bias_sum / two) + rate * bias_dot
    lags = []
    for lag in range(6):
        later = shifted(real, lag)
        value = rate * rate * dots_ref[lag]
        value = value + (rate / two) * (bias_dot * later + real * shifted(bias_dot, lag))
        lags.append(value + (bias_sum / (two * two)) * (real * later))

    def gram(a, b):
        low, high = min(a, b), max(a, b)
        return shifted(lags[high - low], low) if high - low < 6 else None

    table = {(a, b): gram(a, b) for a in REACH for b in REACH if a <= b}

    def against(weighting):
        out = {}
        for a in REACH:
            out[a] = sum(
                weighting[b] * table[min(a, b), max(a, b)]
                for b in REACH if table[min(a, b), max(a, b)] is not None
            )
        return out

    with_mixed, with_half = against(mixer), against(halver)
    with_grad = {}
    grad_bias = dots_ref[12]
    cross_dots = {
        d: rate * dots_ref[6 + d + 2] + shifted(real, d) * (grad_bias / two) for d in range(-2, 4)
    }
    for d in REACH:
        here = cross_dots[d] if d >= -2 else jnp.zeros_like(real)
        before = shifted(cross_dots[d + 1], -1) if d + 1 <= 3 else jnp.zeros_like(real)
        with_grad[d] = jnp.where(even, here, before)

    def per_block(values, scale):
        out = []
        for b, n in zip(SIZES, counts):
            terms = [values[d] * holds[b, d] for d in REACH if holds[b, d] is not None]
            out.append(scale * sum(terms) / n)
        return out

    shared = own / pair_count
    bases = [per_block(with_grad, shared), per_block(with_half, shared), per_block(with_mixed, own)]

    def total_of(x):
        return jnp.sum(jnp.sum(x, axis=1, keepdims=True), axis=0, keepdims=True)

    first_of_pair = jnp.where(even & at.inside, 1.0, 0.0)
    mean_score = sum(p * s for p, s in zip(probs, scores))

    def bent(values):
        mean = sum(p * v for p, v in zip(probs, values))
        return total_of(own * (sum(p * s * v for p, s, v in zip(probs, scores, values)) - mean * mean_score))

    sums = [
        total_of(sum(own * mixer[d] * with_mixed[d] for d in REACH)),
        total_of(first_of_pair * sum(halver[d] * with_half[d] for d in REACH)),
        total_of(first_of_pair * sum(halver[d] * with_grad[d] for d in REACH)),
        bent(bases[0]), bent(bases[1]), bent(bases[2]),
        total_of(shared * at.both(grad_bias)),
        total_of(shared * sum(halver[d] * shifted(normed_bias, d) for d in REACH)),
        total_of(own * sum(mixer[d] * shifted(normed_bias, d) for d in REACH)),
    ]
    for i, b in enumerate(SIZES):
        state_ref[i] = weights[i]
        state_ref[4 + i] = probs[i]
        for f in range(3):
            state_ref[8 + 4 * f + i] = bases[f][i]
    sums_ref[...] = spread(sums, sums_ref.shape[0])


def back_kernel(
    sizes, first_ref, second_ref, ids_ref, state_ref, conv_ref, emb_ref, grad_ref, embed_ref, taps_ref, bias_ref,
    scorer_ref, out_ref, pay_ref, coef_ref, back_ref, acc_ref,
):
    rows, width, run, feat, vocab, kernel = sizes
    tiles = feat // LANES
    half = run // 2
    vr = rows * RUNS
    start = lax.axis_index("seq") * width
    bias = bias_ref[...]
    one, two, count, count4, bias_sum, cross = scales(first_ref, bias, feat)
    mixed_sum, half_sum, inner, bent_g, bent_h, bent_m, bias_g, bias_h, bias_m = picked(second_ref, 9)
    size, size4 = count * feat, count4 * feat
    three = jnp.sqrt(mixed_sum / size + EPS)
    four = jnp.sqrt(half_sum / (three * three) / size4 + EPS)
    fourth = (inner / three) / (four * four * four * size4)
    alpha = 1.0 / (three * four)
    beta = -fourth / (three * three)
    gamma = -(inner / four - fourth / three * half_sum) / (three * three * three * size)
    joint = alpha * (inner + bent_g) + beta * (half_sum + bent_h) + gamma * (mixed_sum + bent_m)
    rate = 1.0 / (one * two)
    normed_bias = count * bias_sum / two + rate * cross
    bias_back = (alpha * bias_g + beta * bias_h + gamma * bias_m - joint / size * normed_bias) / two
    inner_one = one * (joint * EPS / (two * two) - bias_back)
    first_coef = inner_one / (one * one * one * size)

    at = Places(ids_ref[...], start, run)
    probs = [state_ref[4 + i] for i in range(4)]
    weights = [state_ref[i] for i in range(4)]
    grads = [
        alpha * state_ref[8 + i] + beta * state_ref[12 + i] + gamma * state_ref[16 + i] for i in range(4)
    ]
    mean = sum(p * g for p, g in zip(probs, grads))
    spreading = jnp.zeros_like(probs[0])
    for i, b in enumerate(SIZES):
        bent = probs[i] * (grads[i] - mean)
        n = jnp.maximum(at.pooled(b, at.real), 1.0)
        spreading = spreading + at.pooled(b, jnp.where(at.inside, bent / n, 0.0))
    pair_real = at.pooled(2, at.real)
    pair_count = jnp.maximum(pair_real, 1.0)
    filled = (pair_real > 0).astype(f32)
    narrow = [rate * w for w in weights] + [rate * spreading, at.real]
    paired = [
        alpha / pair_count, alpha * filled, beta / (pair_count * pair_count), beta * filled / pair_count + gamma
    ]
    leak = jnp.sum(jnp.sum(spreading * at.real, axis=1, keepdims=True), axis=0, keepdims=True)

    for r in range(rows):
        sub = slice(r * RUNS, (r + 1) * RUNS)
        for j in range(-2, run + 2):
            which = range(6) if 0 <= j < run else (4, 5)
            for i in which:
                coef_ref[i, j + 2, sub, :] = jnp.broadcast_to(narrow[i][sub, j + OFF : j + OFF + 1], (RUNS, LANES))
        for k in range(half):
            for i in range(4):
                coef_ref[6 + i // 2, 2 * k + i % 2, sub, :] = jnp.broadcast_to(
                    paired[i][sub, 2 * k + OFF : 2 * k + OFF + 1], (RUNS, LANES)
                )

    acc_ref[...] = jnp.zeros_like(acc_ref)
    phase = (start + run * iota((RUNS, LANES), 0)) % 3
    at_phase = [phase == p for p in range(3)]

    def chosen(j, a, b, c):
        return jnp.where(at_phase[(0 - j) % 3], a, jnp.where(at_phase[(1 - j) % 3], b, c))

    full = (RUNS, LANES)
    alpha_all = jnp.broadcast_to(alpha, full)
    gamma_all = jnp.broadcast_to(gamma, full)
    fall = jnp.broadcast_to(rate * rate * joint / size, full)
    fall_bias = rate * joint / size / two

    def column(step, carry):
        r, tile = step // tiles, step % tiles
        sub = pl.ds(pl.multiple_of(r * RUNS, RUNS), RUNS)
        cols = pl.ds(pl.multiple_of(tile * LANES, LANES), LANES)
        taps = [jnp.broadcast_to(taps_ref[k : k + 1, cols], full) for k in range(kernel)]
        bias_row = bias_ref[:, cols]
        normed_row = jnp.broadcast_to(bias_row / two, full)
        fall_row = jnp.broadcast_to(bias_row * fall_bias, full)
        scorer = jnp.broadcast_to(scorer_ref[:, cols], full)
        zero = jnp.zeros(full, f32)

        def coef(i, j):
            return coef_ref[i, j, sub, :]

        u, triple, third, pairs, g_m, y3, gc = {}, {}, {}, {}, {}, {}, {}
        sums = [zero] * (kernel + 2)
        block = {}
        for j in range(-2, 2):
            u[j] = conv_ref[j + 2, sub, cols]
        triple[-2] = u[-2] + u[-1] + u[0]
        triple[-1] = u[-1] + u[0] + u[1]

        def window(j):
            near = [y3[i] for i in (j, j + 1, j + 2) if 0 <= i < run]
            return functools.reduce(lambda a, b: a + b, near) if near else zero

        def settle(s):
            nonlocal sums
            for j in (s, s - 1, s - 2):
                if j not in block:
                    block[j] = window(j)
            g = chosen(s, block[s], block[s - 1], block[s - 2])
            sigma = coef(4, s + 2)
            g = g + sigma * scorer
            if 0 <= s < run:
                g = g + lone[s]
                g = g - fall * u[s] - fall_row
            g = g * coef(5, s + 2)
            gc[s] = g
            for k in range(kernel):
                sums[k] = sums[k] + g * emb_ref[s - kernel + 1 + k + LEFT, sub, cols]
            sums[kernel] = sums[kernel] + g
            sums[kernel + 1] = sums[kernel + 1] + sigma * u[s]

        def finish(s):
            terms = [taps[k] * gc[s + kernel - 1 - k] for k in range(kernel) if s + kernel - 1 - k in gc]
            back_ref[s + LEFT, sub, cols] = functools.reduce(lambda a, b: a + b, terms)

        lone = {}
        settled = -2
        finished = -LEFT
        for quad in range(0, run, 4):
            for j in range(quad + 2, quad + 6):
                u[j] = conv_ref[j + 2, sub, cols]
            two_sums = [u[quad + 2 * p] + u[quad + 2 * p + 1] for p in range(2)]
            four_sum = two_sums[0] + two_sums[1]
            wide = zero
            for p in range(2):
                y = None
                xs = []
                for j in (quad + 2 * p, quad + 2 * p + 1):
                    triple[j] = u[j] + u[j + 1] + u[j + 2] if j % 2 else two_sums[p] + u[j + 2]
                    x = coef(0, j + 2) * u[j] + coef(1, j + 2) * two_sums[p]
                    x = x + coef(2, j + 2) * chosen(j, triple[j], triple[j - 1], triple[j - 2])
                    x = x + coef(3, j + 2) * four_sum
                    xs.append(x)
                y = xs[0] + xs[1]
                k = quad // 2 + p
                rowk = pair_rows(r, k, tile, half, tiles)
                scale_y = coef(6, 2 * k)
                out_ref[rowk, :] = scale_y * y + coef(6, 2 * k + 1) * normed_row
                q = scale_y * grad_ref[rowk, :] + coef(7, 2 * k) * y + coef(7, 2 * k + 1) * normed_row
                pair = zero
                for i, j in enumerate((quad + 2 * p, quad + 2 * p + 1)):
                    g = q + gamma_all * xs[i]
                    lone[j] = coef(0, j + 2) * g
                    y3[j] = coef(2, j + 2) * g
                    pair = coef(1, j + 2) * g if i == 0 else pair + coef(1, j + 2) * g
                    wide = coef(3, j + 2) * g if i + p == 0 else wide + coef(3, j + 2) * g
                for j in (quad + 2 * p, quad + 2 * p + 1):
                    lone[j] = lone[j] + pair
            for j in range(quad, quad + 4):
                lone[j] = lone[j] + wide
            last = quad + 3 - 2 if quad + 4 < run else run + 1
            while settled <= last:
                settle(settled)
                settled += 1
            done = settled - kernel if quad + 4 < run else run + RIGHT - 1
            while finished <= done:
                finish(finished)
                finished += 1
        for i in range(kernel + 2):
            acc_ref[i, :, cols] = acc_ref[i, :, cols] + sums[i]
        return carry

    lax.fori_loop(0, rows * tiles, column, 0)

    group = 8
    table = jnp.zeros((vocab, feat), f32)
    seen = jnp.zeros((vocab, LANES), f32)
    span = run + LEFT + RIGHT
    for first in range(0, emb_ref.shape[0], group):
        marks, inside = [], []
        for i in range(first, first + group):
            column_ids = ids_ref[:, i + OFF - LEFT : i + OFF - LEFT + 1]
            marks.append((column_ids == iota((vr, vocab), 1)).astype(f32))
            inside.append(jnp.full((vr, LANES), 1.0 if LEFT <= i < LEFT + run else 0.0, f32))
        onehot = jnp.concatenate(marks, axis=0).astype(jnp.bfloat16)
        if first + group > span:
            back_ref[span : first + group] = jnp.zeros((first + group - span, vr, feat), f32)
        value = back_ref[first : first + group].reshape(group * vr, feat)
        high = value.astype(jnp.bfloat16)
        low = (value - high.astype(f32)).astype(jnp.bfloat16)
        table = table + lax.dot_general(onehot, high, TN, preferred_element_type=f32)
        table = table + lax.dot_general(onehot, low, TN, preferred_element_type=f32)
        ones = jnp.concatenate(inside, axis=0).astype(jnp.bfloat16)
        seen = seen + lax.dot_general(onehot, ones, TN, preferred_element_type=f32)
    for tile in range(tiles):
        cols = slice(tile * LANES, (tile + 1) * LANES)
        pay_ref[:, cols] = table[:, cols] - first_coef * seen * embed_ref[:, cols]

    pay_ref[:, feat : feat + LANES] = jnp.zeros((vocab, LANES), f32)
    for i in range(kernel + 2):
        row = jnp.sum(acc_ref[i], axis=0, keepdims=True)
        if i == kernel:
            row = row * one
        if i == kernel + 1:
            row = row + bias * (leak / two)
        for tile in range(tiles):
            place = i * tiles + tile
            pay_ref[place : place + 1, feat : feat + LANES] = row[:, tile * LANES : (tile + 1) * LANES]


def exchanged(x, n):
    return lax.all_to_all(x, AXES, 0, 0, tiled=True)


def partner(x, axis, step):
    n = lax.axis_size(axis)
    return lax.ppermute(x, axis, [(i, i ^ step) for i in range(n)])


def summed_over_devices(x):
    steps = []
    step = 1
    while step < lax.axis_size("seq"):
        steps.append(step)
        step *= 2
    here = lax.axis_index("seq")
    for step in steps:
        side = (here // step) % 2
        parts = x.reshape(2, x.shape[0] // 2, x.shape[1])
        send = lax.dynamic_index_in_dim(parts, 1 - side, 0, False)
        keep = lax.dynamic_index_in_dim(parts, side, 0, False)
        x = keep + partner(send, "seq", step)
    n = lax.axis_size("rows")
    part = x.reshape(n, x.shape[0] // n, x.shape[1])
    part = jnp.sum(lax.all_to_all(part, "rows", 0, 0, tiled=True), axis=0)
    part = jnp.broadcast_to(part[None], (n,) + part.shape)
    x = lax.all_to_all(part, "rows", 0, 0, tiled=True).reshape(x.shape)
    for step in steps[::-1]:
        side = (here // step) % 2
        other = partner(x, "seq", step)
        x = jnp.where(side == 0, jnp.concatenate([x, other]), jnp.concatenate([other, x]))
    return x


def on_device(byte_ids, lengths, embed, conv_weight, conv_bias, score_weight, out_grad):
    rows, width = byte_ids.shape
    vocab, feat = embed.shape
    kernel = conv_weight.shape[0]
    run = width // RUNS
    half = width // 2
    vr = rows * RUNS
    sizes = (rows, width, run, feat, vocab, kernel)
    count = lax.axis_size("seq")
    devices = count * lax.axis_size("rows")
    span = -(-(run + LEFT + RIGHT) // 8) * 8
    struct = jax.ShapeDtypeStruct
    params = pltpu.CompilerParams(vmem_limit_bytes=60 * 1024 * 1024)

    up = [(i, i + 1) for i in range(count - 1)]
    left = lax.ppermute(byte_ids, "seq", up)
    right = lax.ppermute(byte_ids, "seq", [(j, i) for i, j in up])
    own = jnp.pad(byte_ids.reshape(vr, run), ((0, 0), (0, LANES - run)))
    bias = conv_bias.reshape(1, feat)
    scorer = score_weight.reshape(1, feat)
    grad = as_tiles(out_grad.reshape(rows * half, feat))

    split, table = pl.pallas_call(
        prep_kernel,
        out_shape=(struct((2, vocab, feat), jnp.bfloat16), struct((16, vocab), f32)),
        in_specs=[VMEM] * 4, out_specs=(VMEM, VMEM), compiler_params=params, name="prep",
    )(embed, conv_weight, bias, scorer)

    emb, conv, ids, dots, first = pl.pallas_call(
        functools.partial(stats_kernel, sizes),
        out_shape=(
            struct((span, vr, feat), f32), struct((run + 12, vr, feat), f32), struct((vr, LANES), jnp.int32),
            struct((15, vr, LANES), f32), struct((devices, 1, LANES), f32),
        ),
        in_specs=[VMEM, VMEM, VMEM, SMEM] + [VMEM] * 5, out_specs=(VMEM,) * 5, compiler_params=params, name="stats",
    )(own, left, right, lengths, split, table, conv_weight, bias, grad)
    first = exchanged(first, devices)

    state, second = pl.pallas_call(
        functools.partial(score_kernel, sizes),
        out_shape=(struct((20, vr, LANES), f32), struct((devices, 1, LANES), f32)),
        in_specs=[VMEM] * 5, out_specs=(VMEM, VMEM), compiler_params=params, name="score",
    )(first, ids, dots, bias, scorer)
    second = exchanged(second, devices)

    blocks, pay = pl.pallas_call(
        functools.partial(back_kernel, sizes),
        out_shape=(struct((rows * half * feat // LANES, LANES), f32), struct((vocab, feat + LANES), f32)),
        in_specs=[VMEM] * 11, out_specs=(VMEM, VMEM), compiler_params=params, name="back",
        scratch_shapes=[
            pltpu.VMEM((8, run + 4, vr, LANES), f32), pltpu.VMEM((span, vr, feat), f32),
            pltpu.VMEM((kernel + 2, RUNS, feat), f32),
        ],
    )(first, second, ids, state, conv, emb, grad, embed, conv_weight, bias, scorer)

    pay = summed_over_devices(pay)
    tiles = feat // LANES
    extra = pay[: (kernel + 2) * tiles, feat:].reshape(kernel + 2, feat)
    return (
        from_tiles(blocks, feat).reshape(rows, half, feat), pay[:, :feat], extra[:kernel], extra[kernel], extra[kernel + 1]
    )


def solution(mesh):
    placed = (P("rows", "seq"), P("rows"), P(), P(), P(), P(), P("rows", "seq", None))
    return jax.shard_map(
        on_device,
        mesh=mesh,
        in_specs=placed,
        out_specs=(P("rows", "seq", None), P(), P(), P(), P()),
        check_vma=False,
    )
```

```python
import functools

import jax
import jax.numpy as jnp
from jax import lax
from jax.experimental import pallas as pl
from jax.experimental.pallas import tpu as pltpu
from jax.sharding import PartitionSpec as P

f32 = jnp.float32
EPS = 1e-06
LANES = 128
WIDE = 256
RUNS = 8
OFF = 8
LEFT, RIGHT = 5, 2
NT = (((1,), (1,)), ((), ()))
AXES = ("rows", "seq")
VMEM = pl.BlockSpec(memory_space=pltpu.VMEM)
HBM = pl.BlockSpec(memory_space=pltpu.HBM)


def iota(shape, dim):
    return lax.broadcasted_iota(jnp.int32, shape, dim)


def shifted(x, by):
    return x if by == 0 else pltpu.roll(x, (-by) % LANES, 1)


BIAS, SCORER = 4, 5
IDS, WEIGHTS, SEEN = 15, 16, 18


def stats_kernel(
    sizes, own_hbm, left_hbm, right_hbm, len_hbm, embed_hbm, taps_hbm, bias_hbm, scorer_hbm, grad_hbm,
    emb_hbm, conv_hbm, cot_hbm, mark_hbm, pack_ref, sums_ref,
    own_ref, left_ref, right_ref, len_ref, embed_ref, taps_ref, bias_ref, scorer_ref, grad_ref,
    split_ref, table_ref, rows_ref, mark_ref, turn_ref, spot_ref, line_ref, seen_ref, order_ref, run_ref, *rest,
):
    rows, width, run, feat, vocab, kernel = sizes
    pairs = feat // WIDE
    emb_ref, conv_ref = rest[:pairs], rest[pairs : 2 * pairs]
    cot_ref, sems = rest[2 * pairs :]
    half = run // 2
    vr = rows * RUNS
    span = mark_ref.shape[0] // vr
    sources = (own_hbm, left_hbm, right_hbm, len_hbm, embed_hbm, taps_hbm, bias_hbm, scorer_hbm, grad_hbm)
    targets = (own_ref, left_ref, right_ref, len_ref, embed_ref, taps_ref, bias_ref, scorer_ref, grad_ref)
    fetch = [pltpu.make_async_copy(a, b, sems.at[0, i]) for i, (a, b) in enumerate(zip(sources, targets))]
    for copy in fetch:
        copy.start()
    start = lax.axis_index("seq") * width
    lane = iota((RUNS, LANES), 1)
    sub = iota((RUNS, LANES), 0)
    base = start + run * sub
    back = (OFF - run) % LANES

    for copy in fetch[:4]:
        copy.wait()
    for r in range(rows):
        for s in range(RUNS):
            line = own_ref[r : r + 1, s * run // LANES * LANES : (s * run // LANES + 1) * LANES]
            shift = -(s * run % LANES) % LANES
            line = jnp.broadcast_to(line, (RUNS, LANES))
            line = pltpu.roll(line, shift, 1) if shift else line
            run_ref[r * RUNS + s : r * RUNS + s + 1, :] = line[0:1]
    for r in range(rows):
        own = run_ref[r * RUNS : (r + 1) * RUNS, :]
        before = pltpu.roll(pltpu.roll(own, 1, 0), back, 1)
        edge = pltpu.roll(jnp.broadcast_to(left_ref[r : r + 1, width - LANES : width], (RUNS, LANES)), OFF, 1)
        before = jnp.where(sub == 0, edge, before)
        after = pltpu.roll(pltpu.roll(own, RUNS - 1, 0), OFF + run, 1)
        edge = pltpu.roll(jnp.broadcast_to(right_ref[r : r + 1, 0:LANES], (RUNS, LANES)), OFF + run, 1)
        after = jnp.where(sub == RUNS - 1, edge, after)
        ids = jnp.where(lane < OFF, before, jnp.where(lane < OFF + run, pltpu.roll(own, OFF, 1), after))
        place = base + lane - OFF
        real = (place >= 0) & (place < len_ref[r])
        real = real & (lane >= OFF - LEFT) & (lane < OFF + run + RIGHT)
        pack_ref[IDS, r * RUNS : (r + 1) * RUNS, :] = jnp.where(real, ids, -1).astype(f32)

    group = LANES // (rows * RUNS)
    ids = pack_ref[IDS].astype(jnp.bfloat16)
    eye = (iota((LANES, LANES), 0) == iota((LANES, LANES), 1)).astype(f32).astype(jnp.bfloat16)
    turned = lax.dot_general(eye, ids, NT, preferred_element_type=f32).astype(jnp.bfloat16)
    lined = jnp.zeros((line_ref.shape[0], LANES), f32)
    for i in range(group):
        shape = (line_ref.shape[0], LANES)
        take = (iota(shape, 1) == iota(shape, 0) * group + (i + OFF - LEFT)).astype(f32).astype(jnp.bfloat16)
        put = (iota((vr, LANES), 1) == iota((vr, LANES), 0) + i * vr).astype(f32).astype(jnp.bfloat16)
        some = jnp.dot(take, turned, preferred_element_type=f32).astype(jnp.bfloat16)
        lined = lined + jnp.dot(some, put, preferred_element_type=f32)
    line_ref[...] = lined

    def mark(step, carry):
        for r in range(rows):
            ids = pack_ref[IDS, r * RUNS : (r + 1) * RUNS, :].astype(jnp.int32)
            for i in range(group):
                where = jnp.full((RUNS, LANES), step * group + (i + OFF - LEFT), jnp.int32)
                byte = jnp.take_along_axis(ids, where, axis=1)
                for part in range(vocab // LANES):
                    spot_ref[i, r * RUNS : (r + 1) * RUNS, part * LANES : (part + 1) * LANES] = jnp.where(
                        byte == lane + part * LANES, 1.0, 0.0
                    )
        at = pl.ds(pl.multiple_of(step * LANES, LANES), LANES)
        mark_ref[at, :] = spot_ref[...].reshape(LANES, vocab).astype(jnp.bfloat16)
        bytes_here = jnp.broadcast_to(line_ref[pl.ds(step, 1), :], (vocab, LANES))
        column = jnp.where(bytes_here == iota((vocab, LANES), 0).astype(f32), 1.0, 0.0)
        turn_ref[:, at] = column.astype(jnp.bfloat16)
        line = step * group + iota((1, LANES), 1) // vr
        inside = ((line >= LEFT) & (line < LEFT + run)).astype(f32)
        seen_ref[...] = seen_ref[...] + column * inside
        return carry

    seen_ref[...] = jnp.zeros_like(seen_ref)
    lax.fori_loop(0, span // group, mark, 0)
    for i in range(vocab // vr):
        seen = jnp.sum(seen_ref[i * vr : (i + 1) * vr, :], axis=1, keepdims=True)
        pack_ref[SEEN + i] = jnp.broadcast_to(seen, (vr, LANES))
    keep_mark = pltpu.make_async_copy(turn_ref, mark_hbm, sems.at[1, 0])
    keep_mark.start()
    for copy in fetch[4:8]:
        copy.wait()
    embed = embed_ref[...]
    high, low = in_two(embed)
    split_ref[0] = high
    split_ref[1] = low

    taps = taps_ref[...]
    bias = bias_ref[...].reshape(1, feat)
    scorer = scorer_ref[...].reshape(1, feat)
    rows_ref[0:kernel, :] = taps
    rows_ref[BIAS : BIAS + 1, :] = bias
    rows_ref[SCORER : SCORER + 1, :] = scorer
    rows_ref[SCORER + 1 : 8, :] = jnp.zeros((7 - SCORER, feat), f32)
    for tile in range(feat // LANES):
        at = slice(tile % 4 * 8, tile % 4 * 8 + 8)
        pack_ref[WEIGHTS + tile // 4, at, :] = rows_ref[:, tile * LANES : (tile + 1) * LANES]

    def inner(a, b):
        return lax.dot_general(a, b, NT, preferred_element_type=f32)

    scaled = in_two(jnp.concatenate([taps * scorer, taps * bias], axis=0))
    ones = jnp.ones((8, feat), jnp.bfloat16)
    squares = in_two(embed * embed)
    table_ref[0:8, :] = inner(scaled[0], high) + (inner(scaled[0], low) + inner(scaled[1], high))
    table_ref[8:16, :] = inner(ones, squares[0]) + inner(ones, squares[1])

    steps = rows * (WIDE // LANES)
    lines = span // steps

    def embedding(pair, step):
        at = pl.ds(pl.multiple_of(step * (lines * vr), 16), lines * vr)
        cols = slice(pair * WIDE, (pair + 1) * WIDE)
        total = jnp.dot(mark_ref[at, :], split_ref[0, :, cols], preferred_element_type=f32)
        total = total + jnp.dot(mark_ref[at, :], split_ref[1, :, cols], preferred_element_type=f32)
        emb_ref[pair][pl.ds(step * lines, lines)] = total.reshape(lines, vr, WIDE)

    def convolution(pair, step):
        r, tile = step // (WIDE // LANES), step % (WIDE // LANES)
        at = (pl.ds(pl.multiple_of(r * RUNS, RUNS), RUNS), pl.ds(pl.multiple_of(tile * LANES, LANES), LANES))
        cols = pl.ds(pl.multiple_of(pair * WIDE + tile * LANES, LANES), LANES)
        length = len_ref[r]
        taps = [jnp.broadcast_to(rows_ref[k : k + 1, cols], (RUNS, LANES)) for k in range(kernel)]
        window = [emb_ref[pair][k, at[0], at[1]] for k in range(kernel - 1)]
        for j in range(-2, run + 2):
            window.append(emb_ref[pair][j + LEFT, at[0], at[1]])
            total = taps[0] * window[0]
            for k in range(1, kernel):
                total = total + taps[k] * window[k]
            window = window[1:]
            real = base < length - j
            if j < 0:
                real = real & (base >= -j)
            conv_ref[pair][j + 2, at[0], at[1]] = jnp.where(real, total, 0.0)

    size = RUNS * half
    order = iota((size, size), 0)
    order = (iota((size, size), 1) == order % RUNS * half + order // RUNS).astype(f32)
    order_ref[...] = order.astype(jnp.bfloat16)

    def reorder(r):
        order = order_ref[...]
        at = pl.ds(pl.multiple_of(r * RUNS, RUNS), RUNS)
        for pair in range(pairs):
            cols = slice(pair * WIDE, (pair + 1) * WIDE)
            parts = in_two(grad_ref[pl.ds(pl.multiple_of(r * size, 8), size), cols])
            moved = jnp.dot(order, parts[0], preferred_element_type=f32)
            moved = moved + jnp.dot(order, parts[1], preferred_element_type=f32)
            cot_ref[:, at, cols] = moved.reshape(half, RUNS, WIDE)

    keeps = [keep_mark]
    for stage in range(pairs + 1):

        def both(step, carry):
            if stage < pairs:
                embedding(stage, step)
            if stage > 0:
                convolution(stage - 1, step)
            return carry

        lax.fori_loop(0, steps, both, 0)
        if stage < pairs:
            cols = pl.ds(stage * WIDE, WIDE)
            keeps.append(pltpu.make_async_copy(emb_ref[stage], emb_hbm.at[:, :, cols], sems.at[1, 1 + stage]))
            keeps[-1].start()
        if stage > 0:
            cols = pl.ds((stage - 1) * WIDE, WIDE)
            keeps.append(
                pltpu.make_async_copy(conv_ref[stage - 1], conv_hbm.at[:, :, cols], sems.at[2, stage - 1])
            )
            keeps[-1].start()

    block = 4
    slices = run + 4
    zero = jnp.zeros((RUNS, LANES), f32)
    tile_at = [(t * LANES // WIDE, slice(t * LANES % WIDE, t * LANES % WIDE + LANES)) for t in range(feat // LANES)]

    def lagged(r, carry):
        at = pl.ds(pl.multiple_of(r * RUNS, RUNS), RUNS)
        values = [zero] * 6
        for first in range(0, slices, block):
            acc = {}
            for tile, (pair, cols) in enumerate(tile_at):
                u = [conv_ref[pair][first + i, at, cols] for i in range(min(block + 5, slices - first))]
                for i in range(block):
                    for lag in range(min(6, slices - first - i)):
                        term = u[i] * u[i + lag]
                        acc[i, lag] = term if tile == 0 else acc[i, lag] + term
            for i, lag in acc:
                here = lane == first + (i + OFF - 2)
                values[lag] = jnp.where(here, jnp.sum(acc[i, lag], axis=1, keepdims=True), values[lag])
        for lag in range(6):
            pack_ref[lag, at, :] = values[lag]
        reorder(r)
        return carry

    fetch[8].wait()
    lax.fori_loop(0, rows, lagged, 0)
    keeps.append(pltpu.make_async_copy(cot_ref, cot_hbm, sems.at[3, 0]))
    keeps[-1].start()
    def crossed(r, carry):
        at = pl.ds(pl.multiple_of(r * RUNS, RUNS), RUNS)
        values = [zero] * 7
        for first in range(0, half, block):
            acc = {}
            for tile, (pair, cols) in enumerate(tile_at):
                u = [conv_ref[pair][2 * first + i, at, cols] for i in range(2 * block + 4)]
                bias = jnp.broadcast_to(rows_ref[BIAS : BIAS + 1, tile * LANES : (tile + 1) * LANES], (RUNS, LANES))
                for i in range(block):
                    g = cot_ref[first + i, at, tile * LANES : (tile + 1) * LANES]
                    terms = [g * u[2 * i + d] for d in range(6)] + [g * bias]
                    for d in range(7):
                        acc[i, d] = terms[d] if tile == 0 else acc[i, d] + terms[d]
            for i, d in acc:
                here = lane == 2 * first + (2 * i + OFF)
                values[d] = jnp.where(here, jnp.sum(acc[i, d], axis=1, keepdims=True), values[d])
        for d in range(7):
            pack_ref[6 + d, at, :] = values[d]
        return carry

    lax.fori_loop(0, rows, crossed, 0)

    def total_of(x):
        return jnp.sum(jnp.sum(x, axis=1, keepdims=True), axis=0, keepdims=True)

    def lookups(r, sums):
        at = pl.ds(pl.multiple_of(r * RUNS, RUNS), RUNS)
        ids = pack_ref[IDS, at, :].astype(jnp.int32)
        real = ids >= 0
        low = jnp.where(real, ids, 0)

        def look(row):
            value = jnp.zeros((RUNS, LANES), f32)
            for part in range(vocab // LANES):
                entry = jnp.broadcast_to(
                    table_ref[row : row + 1, part * LANES : (part + 1) * LANES], (RUNS, LANES)
                )
                taken = jnp.take_along_axis(entry, low % LANES, axis=1)
                value = jnp.where(low // LANES == part, taken, value)
            return jnp.where(real, value, 0.0)

        scored = jnp.zeros((RUNS, LANES), f32)
        biased = jnp.zeros((RUNS, LANES), f32)
        for k in range(kernel):
            scored = scored + shifted(look(k), k - (kernel - 1))
            biased = biased + shifted(look(4 + k), k - (kernel - 1))
        inner_real = real & (lane >= OFF - 2)
        scored = jnp.where(inner_real, scored, 0.0)
        biased = jnp.where(inner_real, biased, 0.0)
        pack_ref[13, at, :] = scored
        pack_ref[14, at, :] = biased
        own = (real & (lane >= OFF) & (lane < OFF + run)).astype(f32)
        new = (own * look(8), own, own * biased, own * pack_ref[0, at, :], own * (1 - lane % 2).astype(f32))
        return tuple(a + b for a, b in zip(sums, new))

    sums = lax.fori_loop(0, rows, lookups, (zero,) * 5)
    sums_ref[...] = spread([total_of(x) for x in sums], sums_ref.shape[0])
    for copy in keeps:
        copy.wait()


def in_two(x):
    high = x.astype(jnp.bfloat16)
    return high, (x - high.astype(f32)).astype(jnp.bfloat16)


def unpack_rows(pack_ref, rows_ref):
    for tile in range(rows_ref.shape[1] // LANES):
        at = slice(tile % 4 * 8, tile % 4 * 8 + 8)
        rows_ref[:, tile * LANES : (tile + 1) * LANES] = pack_ref[WEIGHTS + tile // 4, at, :]


def spread(sums, count):
    lane = iota((1, LANES), 1)
    row = jnp.zeros((1, LANES), f32)
    for i, x in enumerate(sums):
        row = jnp.where(lane == i, x, row)
    return jnp.broadcast_to(row[None], (count, 1, LANES))


def picked(ref, number):
    row = jnp.sum(ref[...], axis=0)
    return [row[:, i : i + 1] for i in range(number)]


def scales(first_ref, bias, feat):
    emb_sum, count, cross, square, count4 = picked(first_ref, 5)
    one = jnp.sqrt(emb_sum / (count * feat) + EPS)
    bias_sum = jnp.sum(bias * bias, axis=1, keepdims=True)
    conv_sum = jnp.maximum(count * bias_sum + 2.0 * cross / one + square / (one * one), 0.0)
    two = jnp.sqrt(conv_sum / (count * feat) + EPS)
    return one, two, count, count4, bias_sum, cross


class Places:
    def __init__(self, ids, start, run):
        shape = ids.shape
        self.j = iota(shape, 1) - OFF
        sub = iota(shape, 0) % RUNS
        self.inside = (self.j >= 0) & (self.j < run)
        self.real = ((ids >= 0) & (self.j >= -2)).astype(f32)
        self.own = jnp.where(self.inside, self.real, 0.0)
        shown = self.j + OFF
        self.two, self.four = shown % 2, shown % 4
        self.three = (start + run * sub + shown + (3 * OFF - OFF)) % 3

    def holds(self, size, by):
        if size == 1:
            return jnp.ones_like(self.real) if by == 0 else None
        if abs(by) >= size:
            return None
        phase = {2: self.two, 3: self.three, 4: self.four}[size]
        return ((phase + by >= 0) & (phase + by < size)).astype(f32)

    def pooled(self, size, x):
        if size == 1:
            return x
        pair = x + jnp.where(self.two == 0, shifted(x, 1), shifted(x, -1))
        if size == 2:
            return pair
        if size == 4:
            return pair + jnp.where(self.four < 2, shifted(pair, 2), shifted(pair, -2))
        left, right = shifted(x, -1), shifted(x, 1)
        side = jnp.where(self.three == 0, shifted(x, 2), left)
        far = jnp.where(self.three == 2, shifted(x, -2), right)
        return x + side + far

    def both(self, x):
        return x + shifted(x, -1)


SIZES = (1, 2, 3, 4)
REACH = range(-3, 4)


def score_kernel(sizes, first_ref, dots_ref, state_ref, sums_ref, rows_ref):
    rows, width, run, feat, vocab, kernel = sizes
    start = lax.axis_index("seq") * width
    unpack_rows(dots_ref, rows_ref)
    bias = rows_ref[BIAS : BIAS + 1, :]
    one, two, count, count4, bias_sum, cross = scales(first_ref, bias, feat)
    at = Places(dots_ref[IDS], start, run)
    real, own = at.real, at.own
    rate = 1.0 / (one * two)
    bias_score = jnp.sum(bias * rows_ref[SCORER : SCORER + 1, :], axis=1, keepdims=True) / two

    normed_score = real * bias_score + rate * dots_ref[13]
    counts = [jnp.maximum(at.pooled(b, real), 1.0) for b in SIZES]
    scores = [at.pooled(b, normed_score) / n for b, n in zip(SIZES, counts)]
    top = functools.reduce(jnp.maximum, scores)
    parts = [jnp.exp(s - top) for s in scores]
    whole = sum(parts)
    probs = [p / whole for p in parts]
    weights = [own * p / n for p, n in zip(probs, counts)]

    holds = {(b, d): at.holds(b, d) for b in SIZES for d in REACH}

    def blend(values):
        out = {}
        for d in REACH:
            terms = [v * holds[b, d] for b, v in zip(SIZES, values) if holds[b, d] is not None]
            out[d] = sum(terms)
        return out

    mixer = blend(weights)
    pair_count = jnp.maximum(at.pooled(2, real), 1.0)
    halver = {}
    even = at.two == 0
    for d in REACH:
        zero = jnp.zeros_like(real)
        ahead = shifted(mixer[d - 1], 1) if d - 1 >= -3 else zero
        behind = shifted(mixer[d + 1], -1) if d + 1 <= 3 else zero
        other = jnp.where(even, ahead, behind)
        halver[d] = jnp.where(at.inside, (mixer[d] + other) / pair_count, 0.0)

    bias_dot = dots_ref[14]
    normed_bias = real * (bias_sum / two) + rate * bias_dot
    lags = []
    for lag in range(6):
        later = shifted(real, lag)
        value = rate * rate * dots_ref[lag]
        value = value + (rate / two) * (bias_dot * later + real * shifted(bias_dot, lag))
        lags.append(value + (bias_sum / (two * two)) * (real * later))

    def gram(a, b):
        low, high = min(a, b), max(a, b)
        return shifted(lags[high - low], low) if high - low < 6 else None

    table = {(a, b): gram(a, b) for a in REACH for b in REACH if a <= b}

    def against(weighting):
        out = {}
        for a in REACH:
            out[a] = sum(
                weighting[b] * table[min(a, b), max(a, b)]
                for b in REACH if table[min(a, b), max(a, b)] is not None
            )
        return out

    with_mixed, with_half = against(mixer), against(halver)
    with_grad = {}
    grad_bias = dots_ref[12]
    cross_dots = {
        d: rate * dots_ref[6 + d + 2] + shifted(real, d) * (grad_bias / two) for d in range(-2, 4)
    }
    for d in REACH:
        here = cross_dots[d] if d >= -2 else jnp.zeros_like(real)
        before = shifted(cross_dots[d + 1], -1) if d + 1 <= 3 else jnp.zeros_like(real)
        with_grad[d] = jnp.where(even, here, before)

    def per_block(values, scale):
        out = []
        for b, n in zip(SIZES, counts):
            terms = [values[d] * holds[b, d] for d in REACH if holds[b, d] is not None]
            out.append(scale * sum(terms) / n)
        return out

    shared = own / pair_count
    bases = [per_block(with_grad, shared), per_block(with_half, shared), per_block(with_mixed, own)]

    def total_of(x):
        return jnp.sum(jnp.sum(x, axis=1, keepdims=True), axis=0, keepdims=True)

    first_of_pair = jnp.where(even & at.inside, 1.0, 0.0)
    mean_score = sum(p * s for p, s in zip(probs, scores))

    def bent(values):
        mean = sum(p * v for p, v in zip(probs, values))
        return total_of(own * (sum(p * s * v for p, s, v in zip(probs, scores, values)) - mean * mean_score))

    sums = [
        total_of(sum(own * mixer[d] * with_mixed[d] for d in REACH)),
        total_of(first_of_pair * sum(halver[d] * with_half[d] for d in REACH)),
        total_of(first_of_pair * sum(halver[d] * with_grad[d] for d in REACH)),
        bent(bases[0]), bent(bases[1]), bent(bases[2]),
        total_of(shared * at.both(grad_bias)),
        total_of(shared * sum(halver[d] * shifted(normed_bias, d) for d in REACH)),
        total_of(own * sum(mixer[d] * shifted(normed_bias, d) for d in REACH)),
    ]
    for i, b in enumerate(SIZES):
        state_ref[i] = weights[i]
        state_ref[4 + i] = probs[i]
        for f in range(3):
            state_ref[8 + 4 * f + i] = bases[f][i]
    sums_ref[...] = spread(sums, sums_ref.shape[0])


def back_kernel(
    sizes, first_hbm, second_hbm, pack_hbm, state_hbm, mark_hbm, embed_hbm, conv_hbm, emb_hbm, cot_hbm,
    out_hbm, keep_hbm, send_hbm,
    first_ref, second_ref, pack_ref, state_ref, mark_ref, embed_ref, rows_ref, turn_ref, out_ref, order_ref,
    narrow_ref, acc_ref, pay_ref, conv_ref, emb_ref, cot_ref, back_ref, sems,
):
    rows, width, run, feat, vocab, kernel = sizes
    tiles = feat // LANES
    per = WIDE // LANES
    units = rows * (feat // WIDE)
    half = run // 2
    vr = rows * RUNS

    def fetches(unit):
        sub = pl.ds(pl.multiple_of(unit % rows * RUNS, RUNS), RUNS)
        cols = pl.ds(pl.multiple_of(unit // rows * WIDE, LANES), WIDE)
        return [
            pltpu.make_async_copy(a.at[:, sub, cols], b.at[:, sub, cols], sems.at[i, unit])
            for i, (a, b) in enumerate(((conv_hbm, conv_ref), (cot_hbm, cot_ref), (emb_hbm, emb_ref)))
        ]

    size = RUNS * half

    def stored(unit):
        some = pl.ds(pl.multiple_of(unit % rows * size, 8), size)
        cols = pl.ds(pl.multiple_of(unit // rows * WIDE, LANES), WIDE)
        return pltpu.make_async_copy(out_ref.at[some, cols], out_hbm.at[some, cols], sems.at[3, unit])

    def restore(unit):
        some = pl.ds(pl.multiple_of(unit % rows * size, 8), size)
        cols = pl.ds(pl.multiple_of(unit // rows * WIDE, LANES), WIDE)
        high, low = in_two(turn_ref[...].reshape(size, WIDE))
        moved = jnp.dot(order_ref[...], high, preferred_element_type=f32)
        out_ref[some, cols] = moved + jnp.dot(order_ref[...], low, preferred_element_type=f32)

    sources = (first_hbm, second_hbm, pack_hbm, state_hbm, mark_hbm, embed_hbm)
    targets = (first_ref, second_ref, pack_ref, state_ref, mark_ref, embed_ref)
    small = [pltpu.make_async_copy(a, b, sems.at[4, i]) for i, (a, b) in enumerate(zip(sources, targets))]
    ahead = 3
    for copy in small[:4]:
        copy.start()
    for unit in range(ahead):
        for copy in fetches(unit):
            copy.start()
    for copy in small[4:]:
        copy.start()
    for copy in small[:4]:
        copy.wait()

    start = lax.axis_index("seq") * width
    unpack_rows(pack_ref, rows_ref)
    bias = rows_ref[BIAS : BIAS + 1, :]
    one, two, count, count4, bias_sum, cross = scales(first_ref, bias, feat)
    mixed_sum, half_sum, inner, bent_g, bent_h, bent_m, bias_g, bias_h, bias_m = picked(second_ref, 9)
    volume, volume4 = count * feat, count4 * feat
    three = jnp.sqrt(mixed_sum / volume + EPS)
    four = jnp.sqrt(half_sum / (three * three) / volume4 + EPS)
    fourth = (inner / three) / (four * four * four * volume4)
    alpha = 1.0 / (three * four)
    beta = -fourth / (three * three)
    gamma = -(inner / four - fourth / three * half_sum) / (three * three * three * volume)
    joint = alpha * (inner + bent_g) + beta * (half_sum + bent_h) + gamma * (mixed_sum + bent_m)
    rate = 1.0 / (one * two)
    normed_bias = count * bias_sum / two + rate * cross
    bias_back = (alpha * bias_g + beta * bias_h + gamma * bias_m - joint / volume * normed_bias) / two
    inner_one = one * (joint * EPS / (two * two) - bias_back)
    first_coef = inner_one / (one * one * one * volume)

    at = Places(pack_ref[IDS], start, run)
    probs = [state_ref[4 + i] for i in range(4)]
    weights = [state_ref[i] for i in range(4)]
    grads = [
        alpha * state_ref[8 + i] + beta * state_ref[12 + i] + gamma * state_ref[16 + i] for i in range(4)
    ]
    mean = sum(p * g for p, g in zip(probs, grads))
    spreading = jnp.zeros_like(probs[0])
    for i, b in enumerate(SIZES):
        bent = probs[i] * (grads[i] - mean)
        n = jnp.maximum(at.pooled(b, at.real), 1.0)
        spreading = spreading + at.pooled(b, jnp.where(at.inside, bent / n, 0.0))
    pair_real = at.pooled(2, at.real)
    pair_count = jnp.maximum(pair_real, 1.0)
    filled = (pair_real > 0).astype(f32)
    narrow = [rate * w for w in weights] + [rate * spreading, at.real]
    paired = [
        alpha / pair_count, alpha * filled, beta / (pair_count * pair_count), beta * filled / pair_count + gamma
    ]
    leak = jnp.sum(jnp.sum(spreading * at.real, axis=1, keepdims=True), axis=0, keepdims=True)

    for i, x in enumerate(narrow + paired):
        narrow_ref[i] = x
    order = iota((size, size), 0)
    order = (iota((size, size), 1) == order % half * RUNS + order // half).astype(f32)
    order_ref[...] = order.astype(jnp.bfloat16)
    turn_ref[...] = jnp.zeros_like(turn_ref)
    acc_ref[...] = jnp.zeros_like(acc_ref)
    phase = (start + run * iota((RUNS, LANES), 0)) % 3
    at_phase = [phase == p for p in range(3)]

    def chosen(j, a, b, c):
        return jnp.where(at_phase[(0 - j) % 3], a, jnp.where(at_phase[(1 - j) % 3], b, c))

    full = (RUNS, LANES)
    alpha_all = jnp.broadcast_to(alpha, full)
    gamma_all = jnp.broadcast_to(gamma, full)
    fall = jnp.broadcast_to(rate * rate * joint / volume, full)
    fall_bias = rate * joint / volume / two

    def column(r, tile, near, factor):
        sub = pl.ds(pl.multiple_of(r * RUNS, RUNS), RUNS)
        cols = pl.ds(pl.multiple_of(tile * LANES, LANES), LANES)
        taps = [jnp.broadcast_to(rows_ref[k : k + 1, cols], full) for k in range(kernel)]
        bias_row = rows_ref[BIAS : BIAS + 1, cols]
        normed_row = jnp.broadcast_to(bias_row / two, full)
        fall_row = jnp.broadcast_to(bias_row * fall_bias, full)
        scorer = jnp.broadcast_to(rows_ref[SCORER : SCORER + 1, cols], full)
        zero = jnp.zeros(full, f32)

        u, triple, y3, gc = {}, {}, {}, {}
        sums = [zero] * (kernel + 2)
        block = {}
        for j in range(-2, 2):
            u[j] = conv_ref[j + 2, sub, cols]
        triple[-2] = u[-2] + u[-1] + u[0]
        triple[-1] = u[-1] + u[0] + u[1]

        def window(j):
            near = [y3[i] for i in (j, j + 1, j + 2) if 0 <= i < run]
            return functools.reduce(lambda a, b: a + b, near) if near else zero

        def settle(s):
            nonlocal sums
            for j in (s, s - 1, s - 2):
                if j not in block:
                    block[j] = window(j)
            g = chosen(s, block[s], block[s - 1], block[s - 2])
            sigma = factor(4, s)
            g = g + sigma * scorer
            if 0 <= s < run:
                g = g + lone[s]
                g = g - fall * u[s] - fall_row
            g = g * factor(5, s)
            gc[s] = g
            for k in range(kernel):
                sums[k] = sums[k] + g * emb_ref[s - kernel + 1 + k + LEFT, sub, cols]
            sums[kernel] = sums[kernel] + g
            sums[kernel + 1] = sums[kernel + 1] + sigma * u[s]

        def finish(s):
            terms = [taps[k] * gc[s + kernel - 1 - k] for k in range(kernel) if s + kernel - 1 - k in gc]
            back_ref[s + LEFT, sub, cols] = functools.reduce(lambda a, b: a + b, terms)

        lone = {}
        settled = -2
        finished = -LEFT
        for quad in range(0, run, 4):
            for j in range(quad + 2, quad + 6):
                u[j] = conv_ref[j + 2, sub, cols]
            two_sums = [u[quad + 2 * p] + u[quad + 2 * p + 1] for p in range(2)]
            four_sum = two_sums[0] + two_sums[1]
            wide = zero
            for p in range(2):
                y = None
                xs = []
                for j in (quad + 2 * p, quad + 2 * p + 1):
                    triple[j] = u[j] + u[j + 1] + u[j + 2] if j % 2 else two_sums[p] + u[j + 2]
                    x = factor(0, j) * u[j] + factor(1, j) * two_sums[p]
                    x = x + factor(2, j) * chosen(j, triple[j], triple[j - 1], triple[j - 2])
                    x = x + factor(3, j) * four_sum
                    xs.append(x)
                y = xs[0] + xs[1]
                k = quad // 2 + p
                scale_y = factor(6, 2 * k)
                turn_ref[k, :, near] = scale_y * y + factor(7, 2 * k) * normed_row
                q = scale_y * cot_ref[k, sub, cols] + factor(8, 2 * k) * y + factor(9, 2 * k) * normed_row
                pair = zero
                for i, j in enumerate((quad + 2 * p, quad + 2 * p + 1)):
                    g = q + gamma_all * xs[i]
                    lone[j] = factor(0, j) * g
                    y3[j] = factor(2, j) * g
                    pair = factor(1, j) * g if i == 0 else pair + factor(1, j) * g
                    wide = factor(3, j) * g if i + p == 0 else wide + factor(3, j) * g
                for j in (quad + 2 * p, quad + 2 * p + 1):
                    lone[j] = lone[j] + pair
            for j in range(quad, quad + 4):
                lone[j] = lone[j] + wide
            last = quad + 3 - 2 if quad + 4 < run else run + 1
            while settled <= last:
                settle(settled)
                settled += 1
            done = settled - kernel if quad + 4 < run else run + RIGHT - 1
            while finished <= done:
                finish(finished)
                finished += 1
            yield
        for i in range(kernel + 2):
            acc_ref[i, :, cols] = acc_ref[i, :, cols] + sums[i]

    def some_columns(unit, carry):
        for copy in fetches(unit):
            copy.wait()

        @pl.when(unit + ahead < units)
        def _():
            for copy in fetches(unit + ahead):
                copy.start()

        r = unit % rows
        made = {}

        def factor(i, j):
            if (i, j) not in made:
                sub = pl.ds(pl.multiple_of(r * RUNS, RUNS), RUNS)
                made[i, j] = jnp.broadcast_to(narrow_ref[i, sub, j + OFF : j + OFF + 1], full)
            return made[i, j]

        last = jnp.maximum(unit - 1, 0)
        restore(last)
        parts = []
        for i in range(per):
            near = slice(i * LANES, (i + 1) * LANES)
            parts.append(column(r, unit // rows * per + i, near, factor))
        for _ in zip(*parts, strict=True):
            pass

        @pl.when(unit > 0)
        def _():
            stored(last).start()

        return carry

    lax.fori_loop(0, units, some_columns, 0)
    restore(units - 1)
    stored(units - 1).start()

    positions = mark_ref.shape[1]
    edge = run + LEFT + RIGHT
    back_ref[edge:] = jnp.zeros((back_ref.shape[0] - edge, vr, feat), f32)
    for copy in small[4:]:
        copy.wait()
    total_tiles = pay_ref.shape[0]

    def gather(pair, carry):
        cols = pl.ds(pl.multiple_of(pair * WIDE, LANES), WIDE)
        high, low = in_two(back_ref[:, :, cols].reshape(positions, WIDE))
        total = jnp.dot(mark_ref[...], high, preferred_element_type=f32)
        total = total + jnp.dot(mark_ref[...], low, preferred_element_type=f32)
        for v in range(vocab // 8):
            seen = first_coef * pack_ref[SEEN + v * 8 // vr, v * 8 % vr : v * 8 % vr + 8, :]
            for i in range(per):
                wide = pl.ds(pl.multiple_of(pair * WIDE + i * LANES, LANES), LANES)
                part = total[v * 8 : v * 8 + 8, i * LANES : (i + 1) * LANES]
                pay_ref[v * tiles + pair * per + i] = part - seen * embed_ref[v * 8 : v * 8 + 8, wide]
        return carry

    lax.fori_loop(0, feat // WIDE, gather, 0)

    end = vocab // 8 * tiles
    pay_ref[end:] = jnp.zeros((total_tiles - end, 8, LANES), f32)
    for i in range(kernel + 2):
        row = jnp.sum(acc_ref[i], axis=0, keepdims=True)
        if i == kernel:
            row = row * one
        if i == kernel + 1:
            row = row + bias * (leak / two)
        for tile in range(tiles):
            place = i * tiles + tile
            pay_ref[end + place // 8, place % 8 : place % 8 + 1, :] = row[:, tile * LANES : (tile + 1) * LANES]
    core = lax.axis_index("seq") % 2
    part = total_tiles // 2
    halves = [
        pltpu.make_async_copy(pay_ref.at[pl.ds(core * part, part)], keep_hbm, sems.at[0, 0]),
        pltpu.make_async_copy(pay_ref.at[pl.ds((1 - core) * part, part)], send_hbm, sems.at[1, 0]),
    ]
    for copy in halves:
        copy.start()
    for unit in range(units):
        stored(unit).wait()
    for copy in halves:
        copy.wait()


def exchanged(x):
    return lax.all_to_all(x, AXES, 0, 0, tiled=True)


def partner(x, axis, step):
    n = lax.axis_size(axis)
    return lax.ppermute(x, axis, [(i, i ^ step) for i in range(n)])


def summed_over_devices(keep, send):
    n = lax.axis_size("seq")
    others = lax.axis_size("rows") * n // 2
    groups = [[2 * i + side for i in range(others)] for side in range(2)]

    def traded(x):
        return lax.all_to_all(x, AXES, 0, 0, tiled=True, axis_index_groups=groups)

    x = keep + partner(send, "seq", 1)
    chunk = (others, x.shape[0] * x.shape[1] // others, 1, LANES)
    part = jnp.sum(traded(x.reshape(chunk)), axis=0)
    x = traded(jnp.broadcast_to(part[None], chunk)).reshape(x.shape)
    return x, partner(x, "seq", 1), lax.axis_index("seq") % 2 == 1


def on_device(byte_ids, lengths, embed, conv_weight, conv_bias, score_weight, out_grad):
    rows, width = byte_ids.shape
    vocab, feat = embed.shape
    kernel = conv_weight.shape[0]
    run = width // RUNS
    half = width // 2
    vr = rows * RUNS
    sizes = (rows, width, run, feat, vocab, kernel)
    count = lax.axis_size("seq")
    devices = count * lax.axis_size("rows")
    span = -(-(run + LEFT + RIGHT) // 8) * 8
    tiles = feat // LANES
    struct = jax.ShapeDtypeStruct
    sem = pltpu.SemaphoreType.DMA

    params = pltpu.CompilerParams(vmem_limit_bytes=63 * 1024 * 1024)

    up = [(i, i + 1) for i in range(count - 1)]
    left = lax.ppermute(byte_ids, "seq", up)
    right = lax.ppermute(byte_ids, "seq", [(j, i) for i, j in up])

    pairs = feat // WIDE
    bf16 = jnp.bfloat16
    wide_emb = struct((span, vr, feat), f32)
    wide_conv = struct((run + 4, vr, feat), f32)
    wide_cot = struct((half // RUNS, vr, feat), f32)
    marks = struct((vocab, span * vr), bf16)
    pack = struct((SEEN + vocab // vr, vr, LANES), f32)
    sums = struct((devices, 1, LANES), f32)
    state = struct((20, vr, LANES), f32)

    def scratch(like):
        return pltpu.VMEM(like.shape, like.dtype)

    def per_pair(like):
        return [pltpu.VMEM((*like.shape[:-1], WIDE), like.dtype)] * pairs

    emb, conv, cot, mark, packed, first = pl.pallas_call(
        functools.partial(stats_kernel, sizes),
        out_shape=(wide_emb, wide_conv, wide_cot, marks, pack, sums),
        in_specs=[HBM] * 9, out_specs=(HBM,) * 4 + (VMEM,) * 2,
        scratch_shapes=[
            scratch(byte_ids), scratch(byte_ids), scratch(byte_ids), pltpu.SMEM((rows,), jnp.int32), scratch(embed),
            scratch(conv_weight), scratch(conv_bias), scratch(score_weight), pltpu.VMEM((rows * half, feat), f32),
            pltpu.VMEM((2, vocab, feat), bf16), pltpu.VMEM((16, vocab), f32), pltpu.VMEM((8, feat), f32),
            pltpu.VMEM((span * vr, vocab), bf16), scratch(marks), pltpu.VMEM((LANES // vr, vr, vocab), f32),
            pltpu.VMEM((-(-span * vr // LANES // 8) * 8, LANES), f32), pltpu.VMEM((vocab, LANES), f32),
            pltpu.VMEM((half, half), bf16), pltpu.VMEM((vr, LANES), jnp.int32),
            *per_pair(wide_emb), *per_pair(wide_conv), scratch(wide_cot), sem((4, 9)),
        ],
        compiler_params=params, name="stats",
    )(
        byte_ids, left, right, lengths, embed, conv_weight, conv_bias, score_weight,
        out_grad.reshape(rows * half, feat),
    )
    first = exchanged(first)

    states, second = pl.pallas_call(
        functools.partial(score_kernel, sizes),
        out_shape=(state, sums),
        in_specs=[VMEM] * 2, out_specs=(VMEM, VMEM), scratch_shapes=[pltpu.VMEM((8, feat), f32)],
        compiler_params=params, name="score",
    )(first, packed)
    second = exchanged(second)

    lines = vocab * tiles
    lines = -(-(lines + (kernel + 2) * tiles) // devices) * devices
    parts = struct((lines // 16, 8, LANES), f32)
    blocks, keep, send = pl.pallas_call(
        functools.partial(back_kernel, sizes),
        out_shape=(struct((rows * half, feat), f32), parts, parts),
        in_specs=[HBM] * 9, out_specs=(HBM, HBM, HBM),
        scratch_shapes=[
            scratch(sums), scratch(sums), scratch(pack), scratch(state), scratch(marks), scratch(embed),
            pltpu.VMEM((8, feat), f32), pltpu.VMEM((half // RUNS, RUNS, WIDE), f32),
            pltpu.VMEM((rows * half, feat), f32), pltpu.VMEM((half, half), bf16), pltpu.VMEM((10, vr, LANES), f32),
            pltpu.VMEM((kernel + 2, RUNS, feat), f32), pltpu.VMEM((lines // 8, 8, LANES), f32),
            scratch(wide_conv), scratch(wide_emb), scratch(wide_cot), scratch(wide_emb),
            sem((5, max(6, rows * pairs))),
        ],
        compiler_params=params, name="back",
    )(first, second, packed, states, mark, embed, conv, emb, cot)

    mine, other, swapped = summed_over_devices(keep, send)
    whole = jnp.where(swapped, jnp.concatenate([other, mine]), jnp.concatenate([mine, other]))
    table = whole[: vocab * tiles // 8].reshape(vocab // 8, tiles, 8, LANES).transpose(0, 2, 1, 3).reshape(vocab, feat)
    extra = whole[vocab * tiles // 8 :].reshape(-1, LANES)[: (kernel + 2) * tiles].reshape(kernel + 2, feat)
    return blocks.reshape(rows, half, feat), table, extra[:kernel], extra[kernel], extra[kernel + 1]


def solution(mesh):
    placed = (P("rows", "seq"), P("rows"), P(), P(), P(), P(), P("rows", "seq", None))
    return jax.shard_map(
        on_device,
        mesh=mesh,
        in_specs=placed,
        out_specs=(P("rows", "seq", None), P(), P(), P(), P()),
        check_vma=False,
    )
```

```python
import functools

import jax
import jax.numpy as jnp
from jax import lax
from jax.experimental import pallas as pl
from jax.experimental.pallas import tpu as pltpu
from jax.sharding import PartitionSpec as P

f32 = jnp.float32
EPS = 1e-06
LANES = 128
WIDE = 256
RUNS = 8
OFF = 8
LEFT, RIGHT = 5, 2
NT = (((1,), (1,)), ((), ()))
TN = (((0,), (0,)), ((), ()))
AXES = ("rows", "seq")
VMEM = pl.BlockSpec(memory_space=pltpu.VMEM)
HBM = pl.BlockSpec(memory_space=pltpu.HBM)


def iota(shape, dim):
    return lax.broadcasted_iota(jnp.int32, shape, dim)


def shifted(x, by):
    return x if by == 0 else pltpu.roll(x, (-by) % LANES, 1)


BIAS, SCORER = 4, 5
IDS, WEIGHTS, SEEN = 15, 16, 18


def stats_kernel(
    sizes, own_hbm, left_ref, right_ref, len_hbm, embed_hbm, taps_hbm, bias_hbm, scorer_hbm, grad_hbm,
    emb_hbm, conv_hbm, cot_hbm, mark_hbm, pack_ref, sums_ref,
    own_ref, len_ref, embed_ref, taps_ref, bias_ref, scorer_ref, grad_ref,
    split_ref, table_ref, rows_ref, turn_ref, line_ref, seen_ref, order_ref, run_ref, emb_ref, conv_ref, cot_ref, sems,
):
    rows, width, run, feat, vocab, kernel = sizes
    half = run // 2
    vr = rows * RUNS
    span = emb_ref.shape[0]
    sources = (own_hbm, len_hbm, embed_hbm, taps_hbm, bias_hbm, scorer_hbm, grad_hbm)
    targets = (own_ref, len_ref, embed_ref, taps_ref, bias_ref, scorer_ref, grad_ref)
    fetch = [pltpu.make_async_copy(a, b, sems.at[0, i]) for i, (a, b) in enumerate(zip(sources, targets))]
    for copy in fetch:
        copy.start()
    start = lax.axis_index("seq") * width
    lane = iota((RUNS, LANES), 1)
    sub = iota((RUNS, LANES), 0)
    base = start + run * sub
    back = (OFF - run) % LANES

    for copy in fetch[:2]:
        copy.wait()
    for r in range(rows):
        for s in range(RUNS):
            line = own_ref[r : r + 1, s * run // LANES * LANES : (s * run // LANES + 1) * LANES]
            shift = -(s * run % LANES) % LANES
            line = jnp.broadcast_to(line, (RUNS, LANES))
            line = pltpu.roll(line, shift, 1) if shift else line
            run_ref[r * RUNS + s : r * RUNS + s + 1, :] = line[0:1]
    for r in range(rows):
        own = run_ref[r * RUNS : (r + 1) * RUNS, :]
        before = pltpu.roll(pltpu.roll(own, 1, 0), back, 1)
        edge = pltpu.roll(jnp.broadcast_to(left_ref[r : r + 1, width - LANES : width], (RUNS, LANES)), OFF, 1)
        before = jnp.where(sub == 0, edge, before)
        after = pltpu.roll(pltpu.roll(own, RUNS - 1, 0), OFF + run, 1)
        edge = pltpu.roll(jnp.broadcast_to(right_ref[r : r + 1, 0:LANES], (RUNS, LANES)), OFF + run, 1)
        after = jnp.where(sub == RUNS - 1, edge, after)
        ids = jnp.where(lane < OFF, before, jnp.where(lane < OFF + run, pltpu.roll(own, OFF, 1), after))
        place = base + lane - OFF
        real = (place >= 0) & (place < len_ref[r])
        real = real & (lane >= OFF - LEFT) & (lane < OFF + run + RIGHT)
        pack_ref[IDS, r * RUNS : (r + 1) * RUNS, :] = jnp.where(real, ids, -1).astype(f32)

    group = LANES // (rows * RUNS)
    ids = pack_ref[IDS].astype(jnp.bfloat16)
    eye = (iota((LANES, LANES), 0) == iota((LANES, LANES), 1)).astype(f32).astype(jnp.bfloat16)
    turned = lax.dot_general(eye, ids, NT, preferred_element_type=f32).astype(jnp.bfloat16)
    lined = jnp.zeros((line_ref.shape[0], LANES), f32)
    for i in range(group):
        shape = (line_ref.shape[0], LANES)
        take = (iota(shape, 1) == iota(shape, 0) * group + (i + OFF - LEFT)).astype(f32).astype(jnp.bfloat16)
        put = (iota((vr, LANES), 1) == iota((vr, LANES), 0) + i * vr).astype(f32).astype(jnp.bfloat16)
        some = jnp.dot(take, turned, preferred_element_type=f32).astype(jnp.bfloat16)
        lined = lined + jnp.dot(some, put, preferred_element_type=f32)
    line_ref[...] = lined

    seen_ref[...] = jnp.zeros_like(seen_ref)
    for copy in fetch[2:6]:
        copy.wait()
    embed = embed_ref[...]
    high, low = in_two(embed)
    split_ref[0] = high
    split_ref[1] = low

    taps = taps_ref[...]
    bias = bias_ref[...].reshape(1, feat)
    scorer = scorer_ref[...].reshape(1, feat)
    rows_ref[0:kernel, :] = taps
    rows_ref[BIAS : BIAS + 1, :] = bias
    rows_ref[SCORER : SCORER + 1, :] = scorer
    rows_ref[SCORER + 1 : 8, :] = jnp.zeros((7 - SCORER, feat), f32)
    for tile in range(feat // LANES):
        at = slice(tile % 4 * 8, tile % 4 * 8 + 8)
        pack_ref[WEIGHTS + tile // 4, at, :] = rows_ref[:, tile * LANES : (tile + 1) * LANES]

    def inner(a, b):
        return lax.dot_general(a, b, NT, preferred_element_type=f32)

    scaled = in_two(jnp.concatenate([taps * scorer, taps * bias], axis=0))
    ones = jnp.ones((8, feat), jnp.bfloat16)
    squares = in_two(embed * embed)
    table_ref[0:8, :] = inner(scaled[0], high) + (inner(scaled[0], low) + inner(scaled[1], high))
    table_ref[8:16, :] = inner(ones, squares[0]) + inner(ones, squares[1])

    chunk = 2 * LANES
    lines = chunk // vr

    def embedding(step, carry):
        marks = []
        for i in range(chunk // LANES):
            column = step * (chunk // LANES) + i
            bytes_here = jnp.broadcast_to(line_ref[pl.ds(column, 1), :], (vocab, LANES))
            marks.append(jnp.where(bytes_here == iota((vocab, LANES), 0).astype(f32), 1.0, 0.0))
            line = column * group + iota((1, LANES), 1) // vr
            inside = ((line >= LEFT) & (line < LEFT + run)).astype(f32)
            seen_ref[...] = seen_ref[...] + marks[i] * inside
        marks = jnp.concatenate(marks, axis=1).astype(jnp.bfloat16)
        turn_ref[:, pl.ds(pl.multiple_of(step * chunk, chunk), chunk)] = marks
        total = lax.dot_general(marks, split_ref[0], TN, preferred_element_type=f32)
        total = total + lax.dot_general(marks, split_ref[1], TN, preferred_element_type=f32)
        emb_ref[pl.ds(step * lines, lines)] = total.reshape(lines, vr, feat)
        return carry

    lax.fori_loop(0, span // lines, embedding, 0)
    for i in range(vocab // vr):
        seen = jnp.sum(seen_ref[i * vr : (i + 1) * vr, :], axis=1, keepdims=True)
        pack_ref[SEEN + i] = jnp.broadcast_to(seen, (vr, LANES))
    keeps = [
        pltpu.make_async_copy(turn_ref, mark_hbm, sems.at[1, 0]), pltpu.make_async_copy(emb_ref, emb_hbm, sems.at[1, 1])
    ]
    for copy in keeps:
        copy.start()

    size = RUNS * half
    order = iota((size, size), 0)
    order = (iota((size, size), 1) == order % RUNS * half + order // RUNS).astype(f32)
    order_ref[...] = order.astype(jnp.bfloat16)

    def convolution(step, carry):
        r, pair = step % rows, step // rows
        sub = pl.ds(pl.multiple_of(r * RUNS, RUNS), RUNS)
        length = len_ref[r]
        for tile in range(WIDE // LANES):
            cols = pl.ds(pl.multiple_of(pair * WIDE + tile * LANES, LANES), LANES)
            taps = [jnp.broadcast_to(rows_ref[k : k + 1, cols], (RUNS, LANES)) for k in range(kernel)]
            window = [emb_ref[k, sub, cols] for k in range(kernel - 1)]
            for j in range(-2, run + 2):
                window.append(emb_ref[j + LEFT, sub, cols])
                total = taps[0] * window[0]
                for k in range(1, kernel):
                    total = total + taps[k] * window[k]
                window = window[1:]
                real = base < length - j
                if j < 0:
                    real = real & (base >= -j)
                conv_ref[j + 2, sub, cols] = jnp.where(real, total, 0.0)
        return carry

    lax.fori_loop(0, rows * (feat // WIDE), convolution, 0)
    keeps.append(pltpu.make_async_copy(conv_ref.at[0 : run + 4], conv_hbm, sems.at[2, 0]))
    keeps[-1].start()

    block = 4
    slices = run + 4
    zero = jnp.zeros((RUNS, LANES), f32)
    parts = 4
    portion = slices // parts

    def lagged(step, carry):
        at = pl.ds(pl.multiple_of(step // parts * RUNS, RUNS), RUNS)
        begin = step % parts * portion
        values = [jnp.where(begin == 0, 0.0, pack_ref[lag, at, :]) for lag in range(6)]
        for first in range(0, portion, block):
            some = min(block, portion - first)
            acc = {}
            for tile in range(feat // LANES):
                cols = slice(tile * LANES, (tile + 1) * LANES)
                u = [conv_ref[begin + (first + i), at, cols] for i in range(some + 5)]
                for i in range(some):
                    for lag in range(6):
                        term = u[i] * u[i + lag]
                        acc[i, lag] = term if tile == 0 else acc[i, lag] + term
            for i, lag in acc:
                here = lane == begin + (first + i + OFF - 2)
                values[lag] = jnp.where(here, jnp.sum(acc[i, lag], axis=1, keepdims=True), values[lag])
        for lag in range(6):
            pack_ref[lag, at, :] = values[lag]

        pair = jnp.minimum(step % parts, feat // WIDE - 1)
        wide = pl.ds(pl.multiple_of(pair * WIDE, LANES), WIDE)
        high, low = in_two(grad_ref[pl.ds(pl.multiple_of(step // parts * size, 8), size), wide])
        moved = jnp.dot(order_ref[...], high, preferred_element_type=f32)
        moved = moved + jnp.dot(order_ref[...], low, preferred_element_type=f32)
        cot_ref[:, at, wide] = moved.reshape(half, RUNS, WIDE)
        return carry

    conv_ref[slices:] = jnp.zeros((conv_ref.shape[0] - slices, vr, feat), f32)
    fetch[6].wait()
    lax.fori_loop(0, rows * parts, lagged, 0)
    keeps.append(pltpu.make_async_copy(cot_ref, cot_hbm, sems.at[3, 0]))
    keeps[-1].start()

    def crossed(r, carry):
        at = pl.ds(pl.multiple_of(r * RUNS, RUNS), RUNS)
        values = [zero] * 7
        for first in range(0, half, block):
            acc = {}
            for tile in range(feat // LANES):
                cols = slice(tile * LANES, (tile + 1) * LANES)
                u = [conv_ref[2 * first + i, at, cols] for i in range(2 * block + 4)]
                bias = jnp.broadcast_to(rows_ref[BIAS : BIAS + 1, tile * LANES : (tile + 1) * LANES], (RUNS, LANES))
                for i in range(block):
                    g = cot_ref[first + i, at, cols]
                    terms = [g * u[2 * i + d] for d in range(6)] + [g * bias]
                    for d in range(7):
                        acc[i, d] = terms[d] if tile == 0 else acc[i, d] + terms[d]
            for i, d in acc:
                here = lane == 2 * first + (2 * i + OFF)
                values[d] = jnp.where(here, jnp.sum(acc[i, d], axis=1, keepdims=True), values[d])
        for d in range(7):
            pack_ref[6 + d, at, :] = values[d]
        return carry

    lax.fori_loop(0, rows, crossed, 0)

    def total_of(x):
        return jnp.sum(jnp.sum(x, axis=1, keepdims=True), axis=0, keepdims=True)

    def lookups(r, sums):
        at = slice(r * RUNS, (r + 1) * RUNS)
        ids = pack_ref[IDS, at, :].astype(jnp.int32)
        real = ids >= 0
        low = jnp.where(real, ids, 0)

        def look(row):
            value = jnp.zeros((RUNS, LANES), f32)
            for part in range(vocab // LANES):
                entry = jnp.broadcast_to(
                    table_ref[row : row + 1, part * LANES : (part + 1) * LANES], (RUNS, LANES)
                )
                taken = jnp.take_along_axis(entry, low % LANES, axis=1)
                value = jnp.where(low // LANES == part, taken, value)
            return jnp.where(real, value, 0.0)

        scored = jnp.zeros((RUNS, LANES), f32)
        biased = jnp.zeros((RUNS, LANES), f32)
        for k in range(kernel):
            scored = scored + shifted(look(k), k - (kernel - 1))
            biased = biased + shifted(look(4 + k), k - (kernel - 1))
        inner_real = real & (lane >= OFF - 2)
        scored = jnp.where(inner_real, scored, 0.0)
        biased = jnp.where(inner_real, biased, 0.0)
        pack_ref[13, at, :] = scored
        pack_ref[14, at, :] = biased
        own = (real & (lane >= OFF) & (lane < OFF + run)).astype(f32)
        new = (own * look(8), own, own * biased, own * pack_ref[0, at, :], own * (1 - lane % 2).astype(f32))
        return tuple(a + b for a, b in zip(sums, new))

    sums = (zero,) * 5
    for r in range(rows):
        sums = lookups(r, sums)
    sums_ref[...] = spread([total_of(x) for x in sums], sums_ref.shape[0])
    for copy in keeps:
        copy.wait()


def in_two(x):
    high = x.astype(jnp.bfloat16)
    return high, (x - high.astype(f32)).astype(jnp.bfloat16)


def unpack_rows(pack_ref, rows_ref):
    for tile in range(rows_ref.shape[1] // LANES):
        at = slice(tile % 4 * 8, tile % 4 * 8 + 8)
        rows_ref[:, tile * LANES : (tile + 1) * LANES] = pack_ref[WEIGHTS + tile // 4, at, :]


def spread(sums, count):
    lane = iota((1, LANES), 1)
    row = jnp.zeros((1, LANES), f32)
    for i, x in enumerate(sums):
        row = jnp.where(lane == i, x, row)
    return jnp.broadcast_to(row[None], (count, 1, LANES))


def picked(ref, number):
    row = jnp.sum(ref[...], axis=0)
    return [row[:, i : i + 1] for i in range(number)]


def scales(first_ref, bias, feat):
    emb_sum, count, cross, square, count4 = picked(first_ref, 5)
    one = jnp.sqrt(emb_sum / (count * feat) + EPS)
    bias_sum = jnp.sum(bias * bias, axis=1, keepdims=True)
    conv_sum = jnp.maximum(count * bias_sum + 2.0 * cross / one + square / (one * one), 0.0)
    two = jnp.sqrt(conv_sum / (count * feat) + EPS)
    return one, two, count, count4, bias_sum, cross


class Places:
    def __init__(self, ids, start, run):
        shape = ids.shape
        self.j = iota(shape, 1) - OFF
        sub = iota(shape, 0) % RUNS
        self.inside = (self.j >= 0) & (self.j < run)
        self.real = ((ids >= 0) & (self.j >= -2)).astype(f32)
        self.own = jnp.where(self.inside, self.real, 0.0)
        shown = self.j + OFF
        self.two, self.four = shown % 2, shown % 4
        self.three = (start + run * sub + shown + (3 * OFF - OFF)) % 3

    def holds(self, size, by):
        if size == 1:
            return jnp.ones_like(self.real) if by == 0 else None
        if abs(by) >= size:
            return None
        phase = {2: self.two, 3: self.three, 4: self.four}[size]
        return ((phase + by >= 0) & (phase + by < size)).astype(f32)

    def pooled(self, size, x):
        if size == 1:
            return x
        pair = x + jnp.where(self.two == 0, shifted(x, 1), shifted(x, -1))
        if size == 2:
            return pair
        if size == 4:
            return pair + jnp.where(self.four < 2, shifted(pair, 2), shifted(pair, -2))
        left, right = shifted(x, -1), shifted(x, 1)
        side = jnp.where(self.three == 0, shifted(x, 2), left)
        far = jnp.where(self.three == 2, shifted(x, -2), right)
        return x + side + far

    def both(self, x):
        return x + shifted(x, -1)


SIZES = (1, 2, 3, 4)
REACH = range(-3, 4)


def score_kernel(sizes, first_ref, dots_ref, state_ref, sums_ref, rows_ref):
    rows, width, run, feat, vocab, kernel = sizes
    start = lax.axis_index("seq") * width
    unpack_rows(dots_ref, rows_ref)
    bias = rows_ref[BIAS : BIAS + 1, :]
    one, two, count, count4, bias_sum, cross = scales(first_ref, bias, feat)
    at = Places(dots_ref[IDS], start, run)
    real, own = at.real, at.own
    rate = 1.0 / (one * two)
    bias_score = jnp.sum(bias * rows_ref[SCORER : SCORER + 1, :], axis=1, keepdims=True) / two

    normed_score = real * bias_score + rate * dots_ref[13]
    counts = [jnp.maximum(at.pooled(b, real), 1.0) for b in SIZES]
    scores = [at.pooled(b, normed_score) / n for b, n in zip(SIZES, counts)]
    top = functools.reduce(jnp.maximum, scores)
    parts = [jnp.exp(s - top) for s in scores]
    whole = sum(parts)
    probs = [p / whole for p in parts]
    weights = [own * p / n for p, n in zip(probs, counts)]

    holds = {(b, d): at.holds(b, d) for b in SIZES for d in REACH}

    def blend(values):
        out = {}
        for d in REACH:
            terms = [v * holds[b, d] for b, v in zip(SIZES, values) if holds[b, d] is not None]
            out[d] = sum(terms)
        return out

    mixer = blend(weights)
    pair_count = jnp.maximum(at.pooled(2, real), 1.0)
    halver = {}
    even = at.two == 0
    for d in REACH:
        zero = jnp.zeros_like(real)
        ahead = shifted(mixer[d - 1], 1) if d - 1 >= -3 else zero
        behind = shifted(mixer[d + 1], -1) if d + 1 <= 3 else zero
        other = jnp.where(even, ahead, behind)
        halver[d] = jnp.where(at.inside, (mixer[d] + other) / pair_count, 0.0)

    bias_dot = dots_ref[14]
    normed_bias = real * (bias_sum / two) + rate * bias_dot
    lags = []
    for lag in range(6):
        later = shifted(real, lag)
        value = rate * rate * dots_ref[lag]
        value = value + (rate / two) * (bias_dot * later + real * shifted(bias_dot, lag))
        lags.append(value + (bias_sum / (two * two)) * (real * later))

    def gram(a, b):
        low, high = min(a, b), max(a, b)
        return shifted(lags[high - low], low) if high - low < 6 else None

    table = {(a, b): gram(a, b) for a in REACH for b in REACH if a <= b}

    def against(weighting):
        out = {}
        for a in REACH:
            out[a] = sum(
                weighting[b] * table[min(a, b), max(a, b)]
                for b in REACH if table[min(a, b), max(a, b)] is not None
            )
        return out

    with_mixed, with_half = against(mixer), against(halver)
    with_grad = {}
    grad_bias = dots_ref[12]
    cross_dots = {
        d: rate * dots_ref[6 + d + 2] + shifted(real, d) * (grad_bias / two) for d in range(-2, 4)
    }
    for d in REACH:
        here = cross_dots[d] if d >= -2 else jnp.zeros_like(real)
        before = shifted(cross_dots[d + 1], -1) if d + 1 <= 3 else jnp.zeros_like(real)
        with_grad[d] = jnp.where(even, here, before)

    def per_block(values, scale):
        out = []
        for b, n in zip(SIZES, counts):
            terms = [values[d] * holds[b, d] for d in REACH if holds[b, d] is not None]
            out.append(scale * sum(terms) / n)
        return out

    shared = own / pair_count
    bases = [per_block(with_grad, shared), per_block(with_half, shared), per_block(with_mixed, own)]

    def total_of(x):
        return jnp.sum(jnp.sum(x, axis=1, keepdims=True), axis=0, keepdims=True)

    first_of_pair = jnp.where(even & at.inside, 1.0, 0.0)
    mean_score = sum(p * s for p, s in zip(probs, scores))

    def bent(values):
        mean = sum(p * v for p, v in zip(probs, values))
        return total_of(own * (sum(p * s * v for p, s, v in zip(probs, scores, values)) - mean * mean_score))

    sums = [
        total_of(sum(own * mixer[d] * with_mixed[d] for d in REACH)),
        total_of(first_of_pair * sum(halver[d] * with_half[d] for d in REACH)),
        total_of(first_of_pair * sum(halver[d] * with_grad[d] for d in REACH)),
        bent(bases[0]), bent(bases[1]), bent(bases[2]),
        total_of(shared * at.both(grad_bias)),
        total_of(shared * sum(halver[d] * shifted(normed_bias, d) for d in REACH)),
        total_of(own * sum(mixer[d] * shifted(normed_bias, d) for d in REACH)),
    ]
    for i, b in enumerate(SIZES):
        state_ref[i] = weights[i]
        state_ref[4 + i] = probs[i]
        for f in range(3):
            state_ref[8 + 4 * f + i] = bases[f][i]
    sums_ref[...] = spread(sums, sums_ref.shape[0])


def back_kernel(
    sizes, first_hbm, second_hbm, pack_hbm, state_hbm, mark_hbm, embed_hbm, conv_hbm, emb_hbm, cot_hbm,
    out_hbm, keep_ref, send_ref,
    first_ref, second_ref, pack_ref, state_ref, mark_ref, embed_ref, rows_ref, turn_ref, out_ref, order_ref,
    narrow_ref, acc_ref, pay_ref, conv_ref, emb_ref, cot_ref, back_ref, sems,
):
    rows, width, run, feat, vocab, kernel = sizes
    tiles = feat // LANES
    per = WIDE // LANES
    units = rows * (feat // WIDE)
    half = run // 2
    vr = rows * RUNS

    def fetches(unit):
        sub = pl.ds(pl.multiple_of(unit % rows * RUNS, RUNS), RUNS)
        cols = pl.ds(pl.multiple_of(unit // rows * WIDE, LANES), WIDE)
        return [
            pltpu.make_async_copy(a.at[:, sub, cols], b.at[:, sub, cols], sems.at[i, unit])
            for i, (a, b) in enumerate(((conv_hbm, conv_ref), (cot_hbm, cot_ref), (emb_hbm, emb_ref)))
        ]

    size = RUNS * half

    def stored(unit):
        some = pl.ds(pl.multiple_of(unit % rows * size, 8), size)
        cols = pl.ds(pl.multiple_of(unit // rows * WIDE, LANES), WIDE)
        return pltpu.make_async_copy(out_ref.at[some, cols], out_hbm.at[some, cols], sems.at[3, unit])

    def restore(unit):
        some = pl.ds(pl.multiple_of(unit % rows * size, 8), size)
        cols = pl.ds(pl.multiple_of(unit // rows * WIDE, LANES), WIDE)
        high, low = in_two(turn_ref[...].reshape(size, WIDE))
        moved = jnp.dot(order_ref[...], high, preferred_element_type=f32)
        out_ref[some, cols] = moved + jnp.dot(order_ref[...], low, preferred_element_type=f32)

    sources = (first_hbm, second_hbm, pack_hbm, state_hbm, mark_hbm, embed_hbm)
    targets = (first_ref, second_ref, pack_ref, state_ref, mark_ref, embed_ref)
    small = [pltpu.make_async_copy(a, b, sems.at[4, i]) for i, (a, b) in enumerate(zip(sources, targets))]
    ahead = 3
    for copy in small[:4]:
        copy.start()
    for unit in range(ahead):
        for copy in fetches(unit):
            copy.start()
    for copy in small[4:]:
        copy.start()
    for copy in small[:4]:
        copy.wait()

    start = lax.axis_index("seq") * width
    unpack_rows(pack_ref, rows_ref)
    bias = rows_ref[BIAS : BIAS + 1, :]
    one, two, count, count4, bias_sum, cross = scales(first_ref, bias, feat)
    mixed_sum, half_sum, inner, bent_g, bent_h, bent_m, bias_g, bias_h, bias_m = picked(second_ref, 9)
    volume, volume4 = count * feat, count4 * feat
    three = jnp.sqrt(mixed_sum / volume + EPS)
    four = jnp.sqrt(half_sum / (three * three) / volume4 + EPS)
    fourth = (inner / three) / (four * four * four * volume4)
    alpha = 1.0 / (three * four)
    beta = -fourth / (three * three)
    gamma = -(inner / four - fourth / three * half_sum) / (three * three * three * volume)
    joint = alpha * (inner + bent_g) + beta * (half_sum + bent_h) + gamma * (mixed_sum + bent_m)
    rate = 1.0 / (one * two)
    normed_bias = count * bias_sum / two + rate * cross
    bias_back = (alpha * bias_g + beta * bias_h + gamma * bias_m - joint / volume * normed_bias) / two
    inner_one = one * (joint * EPS / (two * two) - bias_back)
    first_coef = inner_one / (one * one * one * volume)

    at = Places(pack_ref[IDS], start, run)
    probs = [state_ref[4 + i] for i in range(4)]
    weights = [state_ref[i] for i in range(4)]
    grads = [
        alpha * state_ref[8 + i] + beta * state_ref[12 + i] + gamma * state_ref[16 + i] for i in range(4)
    ]
    mean = sum(p * g for p, g in zip(probs, grads))
    spreading = jnp.zeros_like(probs[0])
    for i, b in enumerate(SIZES):
        bent = probs[i] * (grads[i] - mean)
        n = jnp.maximum(at.pooled(b, at.real), 1.0)
        spreading = spreading + at.pooled(b, jnp.where(at.inside, bent / n, 0.0))
    pair_real = at.pooled(2, at.real)
    pair_count = jnp.maximum(pair_real, 1.0)
    filled = (pair_real > 0).astype(f32)
    narrow = [rate * w for w in weights] + [rate * spreading, at.real]
    paired = [
        alpha / pair_count, alpha * filled, beta / (pair_count * pair_count), beta * filled / pair_count + gamma
    ]
    leak = jnp.sum(jnp.sum(spreading * at.real, axis=1, keepdims=True), axis=0, keepdims=True)

    for i, x in enumerate(narrow + paired):
        narrow_ref[i] = x
    order = iota((size, size), 0)
    order = (iota((size, size), 1) == order % half * RUNS + order // half).astype(f32)
    order_ref[...] = order.astype(jnp.bfloat16)
    turn_ref[...] = jnp.zeros_like(turn_ref)
    acc_ref[...] = jnp.zeros_like(acc_ref)
    phase = (start + run * iota((RUNS, LANES), 0)) % 3
    at_phase = [phase == p for p in range(3)]

    def chosen(j, a, b, c):
        return jnp.where(at_phase[(0 - j) % 3], a, jnp.where(at_phase[(1 - j) % 3], b, c))

    full = (RUNS, LANES)
    alpha_all = jnp.broadcast_to(alpha, full)
    gamma_all = jnp.broadcast_to(gamma, full)
    fall = jnp.broadcast_to(rate * rate * joint / volume, full)
    fall_bias = rate * joint / volume / two

    def column(r, tile, near, factor):
        sub = pl.ds(pl.multiple_of(r * RUNS, RUNS), RUNS)
        cols = pl.ds(pl.multiple_of(tile * LANES, LANES), LANES)
        taps = [jnp.broadcast_to(rows_ref[k : k + 1, cols], full) for k in range(kernel)]
        bias_row = rows_ref[BIAS : BIAS + 1, cols]
        normed_row = jnp.broadcast_to(bias_row / two, full)
        fall_row = jnp.broadcast_to(bias_row * fall_bias, full)
        scorer = jnp.broadcast_to(rows_ref[SCORER : SCORER + 1, cols], full)
        zero = jnp.zeros(full, f32)

        u, triple, y3, gc = {}, {}, {}, {}
        sums = [zero] * (kernel + 2)
        block = {}
        for j in range(-2, 2):
            u[j] = conv_ref[j + 2, sub, cols]
        triple[-2] = u[-2] + u[-1] + u[0]
        triple[-1] = u[-1] + u[0] + u[1]

        def window(j):
            near = [y3[i] for i in (j, j + 1, j + 2) if 0 <= i < run]
            return functools.reduce(lambda a, b: a + b, near) if near else zero

        def settle(s):
            nonlocal sums
            for j in (s, s - 1, s - 2):
                if j not in block:
                    block[j] = window(j)
            g = chosen(s, block[s], block[s - 1], block[s - 2])
            sigma = factor(4, s)
            g = g + sigma * scorer
            if 0 <= s < run:
                g = g + lone[s]
                g = g - fall * u[s] - fall_row
            g = g * factor(5, s)
            gc[s] = g
            for k in range(kernel):
                sums[k] = sums[k] + g * emb_ref[s - kernel + 1 + k + LEFT, sub, cols]
            sums[kernel] = sums[kernel] + g
            sums[kernel + 1] = sums[kernel + 1] + sigma * u[s]

        def finish(s):
            terms = [taps[k] * gc[s + kernel - 1 - k] for k in range(kernel) if s + kernel - 1 - k in gc]
            back_ref[s + LEFT, sub, cols] = functools.reduce(lambda a, b: a + b, terms)

        lone = {}
        settled = -2
        finished = -LEFT
        for quad in range(0, run, 4):
            for j in range(quad + 2, quad + 6):
                u[j] = conv_ref[j + 2, sub, cols]
            two_sums = [u[quad + 2 * p] + u[quad + 2 * p + 1] for p in range(2)]
            four_sum = two_sums[0] + two_sums[1]
            wide = zero
            for p in range(2):
                y = None
                xs = []
                for j in (quad + 2 * p, quad + 2 * p + 1):
                    triple[j] = u[j] + u[j + 1] + u[j + 2] if j % 2 else two_sums[p] + u[j + 2]
                    x = factor(0, j) * u[j] + factor(1, j) * two_sums[p]
                    x = x + factor(2, j) * chosen(j, triple[j], triple[j - 1], triple[j - 2])
                    x = x + factor(3, j) * four_sum
                    xs.append(x)
                y = xs[0] + xs[1]
                k = quad // 2 + p
                scale_y = factor(6, 2 * k)
                turn_ref[k, :, near] = scale_y * y + factor(7, 2 * k) * normed_row
                q = scale_y * cot_ref[k, sub, cols] + factor(8, 2 * k) * y + factor(9, 2 * k) * normed_row
                pair = zero
                for i, j in enumerate((quad + 2 * p, quad + 2 * p + 1)):
                    g = q + gamma_all * xs[i]
                    lone[j] = factor(0, j) * g
                    y3[j] = factor(2, j) * g
                    pair = factor(1, j) * g if i == 0 else pair + factor(1, j) * g
                    wide = factor(3, j) * g if i + p == 0 else wide + factor(3, j) * g
                for j in (quad + 2 * p, quad + 2 * p + 1):
                    lone[j] = lone[j] + pair
            for j in range(quad, quad + 4):
                lone[j] = lone[j] + wide
            last = quad + 3 - 2 if quad + 4 < run else run + 1
            while settled <= last:
                settle(settled)
                settled += 1
            done = settled - kernel if quad + 4 < run else run + RIGHT - 1
            while finished <= done:
                finish(finished)
                finished += 1
            yield
        for i in range(kernel + 2):
            acc_ref[i, :, cols] = acc_ref[i, :, cols] + sums[i]

    def some_columns(unit, carry):
        for copy in fetches(unit):
            copy.wait()

        @pl.when(unit + ahead < units)
        def _():
            for copy in fetches(unit + ahead):
                copy.start()

        r = unit % rows
        made = {}

        def factor(i, j):
            if (i, j) not in made:
                sub = pl.ds(pl.multiple_of(r * RUNS, RUNS), RUNS)
                made[i, j] = jnp.broadcast_to(narrow_ref[i, sub, j + OFF : j + OFF + 1], full)
            return made[i, j]

        last = jnp.maximum(unit - 1, 0)
        restore(last)
        parts = []
        for i in range(per):
            near = slice(i * LANES, (i + 1) * LANES)
            parts.append(column(r, unit // rows * per + i, near, factor))
        for _ in zip(*parts, strict=True):
            pass

        @pl.when(unit > 0)
        def _():
            stored(last).start()

        return carry

    lax.fori_loop(0, units, some_columns, 0)
    restore(units - 1)
    stored(units - 1).start()

    positions = mark_ref.shape[1]
    edge = run + LEFT + RIGHT
    back_ref[edge:] = jnp.zeros((back_ref.shape[0] - edge, vr, feat), f32)
    for copy in small[4:]:
        copy.wait()
    total_tiles = pay_ref.shape[0]

    def gather(pair, carry):
        cols = pl.ds(pl.multiple_of(pair * WIDE, LANES), WIDE)
        high, low = in_two(back_ref[:, :, cols].reshape(positions, WIDE))
        total = jnp.dot(mark_ref[...], high, preferred_element_type=f32)
        total = total + jnp.dot(mark_ref[...], low, preferred_element_type=f32)
        for v in range(vocab // 8):
            seen = first_coef * pack_ref[SEEN + v * 8 // vr, v * 8 % vr : v * 8 % vr + 8, :]
            for i in range(per):
                wide = pl.ds(pl.multiple_of(pair * WIDE + i * LANES, LANES), LANES)
                part = total[v * 8 : v * 8 + 8, i * LANES : (i + 1) * LANES]
                pay_ref[v * tiles + pair * per + i] = part - seen * embed_ref[v * 8 : v * 8 + 8, wide]
        return carry

    lax.fori_loop(0, feat // WIDE, gather, 0)

    end = vocab // 8 * tiles
    pay_ref[end:] = jnp.zeros((total_tiles - end, 8, LANES), f32)
    for i in range(kernel + 2):
        row = jnp.sum(acc_ref[i], axis=0, keepdims=True)
        if i == kernel:
            row = row * one
        if i == kernel + 1:
            row = row + bias * (leak / two)
        for tile in range(tiles):
            place = i * tiles + tile
            pay_ref[end + place // 8, place % 8 : place % 8 + 1, :] = row[:, tile * LANES : (tile + 1) * LANES]
    core = lax.axis_index("seq") % 2
    part = total_tiles // 2
    keep_ref[...] = pay_ref[pl.ds(core * part, part)]
    send_ref[...] = pay_ref[pl.ds((1 - core) * part, part)]
    for unit in range(units):
        stored(unit).wait()


def finish_kernel(feat, mine_ref, other_ref, table_hbm, taps_ref, bias_ref, scorer_ref, sems):
    core = lax.axis_index("seq") % 2
    tiles = feat // LANES
    part = mine_ref.shape[0]
    rest = table_hbm.shape[0] - part
    for side in range(2):

        @pl.when(core == side)
        def _():
            first, second = (mine_ref, other_ref) if side == 0 else (other_ref, mine_ref)
            copies = (
                pltpu.make_async_copy(first, table_hbm.at[0:part], sems.at[0]),
                pltpu.make_async_copy(second.at[0:rest], table_hbm.at[part : part + rest], sems.at[1]),
            )
            for copy in copies:
                copy.start()
            lines = []
            for i in range(taps_ref.shape[0] + 2):
                places = [i * tiles + tile for tile in range(tiles)]
                lines.append([second[rest + p // 8, p % 8 : p % 8 + 1, :] for p in places])
            for i in range(taps_ref.shape[0]):
                taps_ref[i : i + 1, :] = jnp.concatenate(lines[i], axis=1)
            bias_ref[...] = jnp.concatenate(lines[-2], axis=1).reshape(feat)
            scorer_ref[...] = jnp.concatenate(lines[-1], axis=1).reshape(feat)
            for copy in copies:
                copy.wait()


def exchanged(x):
    return lax.all_to_all(x, AXES, 0, 0, tiled=True)


def partner(x, axis, step):
    n = lax.axis_size(axis)
    return lax.ppermute(x, axis, [(i, i ^ step) for i in range(n)])


def summed_over_devices(keep, send):
    n = lax.axis_size("seq")
    others = lax.axis_size("rows") * n // 2
    groups = [[2 * i + side for i in range(others)] for side in range(2)]

    def traded(x):
        return lax.all_to_all(x, AXES, 0, 0, tiled=True, axis_index_groups=groups)

    x = keep + partner(send, "seq", 1)
    chunk = (others, x.shape[0] * x.shape[1] // others, 1, LANES)
    part = jnp.sum(traded(x.reshape(chunk)), axis=0)
    x = traded(jnp.broadcast_to(part[None], chunk)).reshape(x.shape)
    return x, partner(x, "seq", 1)


def on_device(byte_ids, lengths, embed, conv_weight, conv_bias, score_weight, out_grad):
    rows, width = byte_ids.shape
    vocab, feat = embed.shape
    kernel = conv_weight.shape[0]
    run = width // RUNS
    half = width // 2
    vr = rows * RUNS
    sizes = (rows, width, run, feat, vocab, kernel)
    count = lax.axis_size("seq")
    devices = count * lax.axis_size("rows")
    span = -(-(run + LEFT + RIGHT) // 8) * 8
    tiles = feat // LANES
    struct = jax.ShapeDtypeStruct
    sem = pltpu.SemaphoreType.DMA

    params = pltpu.CompilerParams(vmem_limit_bytes=60 * 1024 * 1024)

    up = [(i, i + 1) for i in range(count - 1)]
    left = pltpu.with_memory_space_constraint(lax.ppermute(byte_ids, "seq", up), pltpu.VMEM)
    right = pltpu.with_memory_space_constraint(lax.ppermute(byte_ids, "seq", [(j, i) for i, j in up]), pltpu.VMEM)

    pairs = feat // WIDE
    bf16 = jnp.bfloat16
    wide_emb = struct((span, vr, feat), f32)
    wide_conv = struct((run + 4, vr, feat), f32)
    wide_cot = struct((half // RUNS, vr, feat), f32)
    marks = struct((vocab, span * vr), bf16)
    pack = struct((SEEN + vocab // vr, vr, LANES), f32)
    sums = struct((devices, 1, LANES), f32)
    state = struct((20, vr, LANES), f32)

    def scratch(like):
        return pltpu.VMEM(like.shape, like.dtype)

    emb, conv, cot, mark, packed, first = pl.pallas_call(
        functools.partial(stats_kernel, sizes),
        out_shape=(*(pltpu.HBM(x.shape, x.dtype) for x in (wide_emb, wide_conv, wide_cot, marks, pack)), pltpu.VMEM(sums.shape, f32)),
        in_specs=[HBM, VMEM, VMEM] + [HBM] * 6, out_specs=(HBM,) * 4 + (VMEM,) * 2,
        scratch_shapes=[
            scratch(byte_ids), pltpu.SMEM((rows,), jnp.int32), scratch(embed),
            scratch(conv_weight), scratch(conv_bias), scratch(score_weight), pltpu.VMEM((rows * half, feat), f32),
            pltpu.VMEM((2, vocab, feat), bf16), pltpu.VMEM((16, vocab), f32), pltpu.VMEM((8, feat), f32),
            scratch(marks), pltpu.VMEM((-(-span * vr // LANES // 8) * 8, LANES), f32), pltpu.VMEM((vocab, LANES), f32),
            pltpu.VMEM((half, half), bf16), pltpu.VMEM((vr, LANES), jnp.int32), scratch(wide_emb),
            pltpu.VMEM((run + 12, vr, feat), f32), scratch(wide_cot), sem((4, 9)),
        ],
        compiler_params=params, name="stats",
    )(
        byte_ids, left, right, lengths, embed, conv_weight, conv_bias, score_weight,
        out_grad.reshape(rows * half, feat),
    )
    first = exchanged(first)

    states, second = pl.pallas_call(
        functools.partial(score_kernel, sizes),
        out_shape=(pltpu.HBM(state.shape, f32), pltpu.VMEM(sums.shape, f32)),
        in_specs=[VMEM] * 2, out_specs=(VMEM, VMEM), scratch_shapes=[pltpu.VMEM((8, feat), f32)],
        compiler_params=params, name="score",
    )(first, packed)
    second = exchanged(second)

    lines = vocab * tiles
    lines = -(-(lines + (kernel + 2) * tiles) // devices) * devices
    parts = struct((lines // 16, 8, LANES), f32)
    blocks, keep, send = pl.pallas_call(
        functools.partial(back_kernel, sizes),
        out_shape=(pltpu.HBM((rows * half, feat), f32), pltpu.VMEM(parts.shape, f32), pltpu.VMEM(parts.shape, f32)),
        in_specs=[HBM] * 9, out_specs=(HBM, VMEM, VMEM),
        scratch_shapes=[
            scratch(sums), scratch(sums), scratch(pack), scratch(state), scratch(marks), scratch(embed),
            pltpu.VMEM((8, feat), f32), pltpu.VMEM((half // RUNS, RUNS, WIDE), f32),
            pltpu.VMEM((rows * half, feat), f32), pltpu.VMEM((half, half), bf16), pltpu.VMEM((10, vr, LANES), f32),
            pltpu.VMEM((kernel + 2, RUNS, feat), f32), pltpu.VMEM((lines // 8, 8, LANES), f32),
            scratch(wide_conv), scratch(wide_emb), scratch(wide_cot), scratch(wide_emb),
            sem((5, max(6, rows * pairs))),
        ],
        compiler_params=params, name="back",
    )(first, second, packed, states, mark, embed, conv, emb, cot)

    mine, other = summed_over_devices(keep, send)
    table, taps_grad, bias_grad, scorer_grad = pl.pallas_call(
        functools.partial(finish_kernel, feat),
        out_shape=(
            pltpu.HBM((vocab * tiles // 8, 8, LANES), f32), struct((kernel, feat), f32), struct((feat,), f32),
            struct((feat,), f32),
        ),
        in_specs=[VMEM, VMEM], out_specs=(HBM, VMEM, VMEM, VMEM), scratch_shapes=[sem((2,))],
        compiler_params=pltpu.CompilerParams(vmem_limit_bytes=8 * 1024 * 1024), name="finish",
    )(mine, other)
    table = table.reshape(vocab // 8, tiles, 8, LANES).transpose(0, 2, 1, 3).reshape(vocab, feat)
    return blocks.reshape(rows, half, feat), table, taps_grad, bias_grad, scorer_grad


def solution(mesh):
    placed = (P("rows", "seq"), P("rows"), P(), P(), P(), P(), P("rows", "seq", None))
    return jax.shard_map(
        on_device,
        mesh=mesh,
        in_specs=placed,
        out_specs=(P("rows", "seq", None), P(), P(), P(), P()),
        check_vma=False,
    )
```

```python
import functools

import jax
import jax.numpy as jnp
from jax import lax
from jax.experimental import pallas as pl
from jax.experimental.pallas import tpu as pltpu
from jax.sharding import PartitionSpec as P

f32 = jnp.float32
EPS = 1e-06
LANES = 128
WIDE = 256
RUNS = 8
OFF = 8
LEFT, RIGHT = 5, 2
NT = (((1,), (1,)), ((), ()))
TN = (((0,), (0,)), ((), ()))
AXES = ("rows", "seq")
VMEM = pl.BlockSpec(memory_space=pltpu.VMEM)
HBM = pl.BlockSpec(memory_space=pltpu.HBM)


def iota(shape, dim):
    return lax.broadcasted_iota(jnp.int32, shape, dim)


def shifted(x, by):
    return x if by == 0 else pltpu.roll(x, (-by) % LANES, 1)


BIAS, SCORER = 4, 5
IDS, WEIGHTS, SEEN = 15, 16, 18


def stats_kernel(
    sizes, own_hbm, left_ref, right_ref, len_hbm, embed_hbm, taps_hbm, bias_hbm, scorer_hbm, grad_hbm,
    emb_hbm, conv_hbm, cot_hbm, mark_hbm, pack_ref, sums_ref,
    own_ref, len_ref, embed_ref, taps_ref, bias_ref, scorer_ref, grad_ref,
    split_ref, table_ref, rows_ref, turn_ref, line_ref, seen_ref, order_ref, run_ref, emb_ref, conv_ref, cot_ref, sems,
):
    rows, width, run, feat, vocab, kernel = sizes
    half = run // 2
    vr = rows * RUNS
    span = emb_ref.shape[0]
    sources = (own_hbm, len_hbm, embed_hbm, taps_hbm, bias_hbm, scorer_hbm, grad_hbm)
    targets = (own_ref, len_ref, embed_ref, taps_ref, bias_ref, scorer_ref, grad_ref)
    fetch = [pltpu.make_async_copy(a, b, sems.at[0, i]) for i, (a, b) in enumerate(zip(sources, targets))]
    for copy in fetch:
        copy.start()
    start = lax.axis_index("seq") * width
    lane = iota((RUNS, LANES), 1)
    sub = iota((RUNS, LANES), 0)
    base = start + run * sub
    back = (OFF - run) % LANES

    for copy in fetch[:2]:
        copy.wait()
    for r in range(rows):
        for s in range(RUNS):
            line = own_ref[r : r + 1, s * run // LANES * LANES : (s * run // LANES + 1) * LANES]
            shift = -(s * run % LANES) % LANES
            line = jnp.broadcast_to(line, (RUNS, LANES))
            line = pltpu.roll(line, shift, 1) if shift else line
            run_ref[r * RUNS + s : r * RUNS + s + 1, :] = line[0:1]
    for r in range(rows):
        own = run_ref[r * RUNS : (r + 1) * RUNS, :]
        before = pltpu.roll(pltpu.roll(own, 1, 0), back, 1)
        edge = pltpu.roll(jnp.broadcast_to(left_ref[r : r + 1, width - LANES : width], (RUNS, LANES)), OFF, 1)
        before = jnp.where(sub == 0, edge, before)
        after = pltpu.roll(pltpu.roll(own, RUNS - 1, 0), OFF + run, 1)
        edge = pltpu.roll(jnp.broadcast_to(right_ref[r : r + 1, 0:LANES], (RUNS, LANES)), OFF + run, 1)
        after = jnp.where(sub == RUNS - 1, edge, after)
        ids = jnp.where(lane < OFF, before, jnp.where(lane < OFF + run, pltpu.roll(own, OFF, 1), after))
        place = base + lane - OFF
        real = (place >= 0) & (place < len_ref[r])
        real = real & (lane >= OFF - LEFT) & (lane < OFF + run + RIGHT)
        pack_ref[IDS, r * RUNS : (r + 1) * RUNS, :] = jnp.where(real, ids, -1).astype(f32)

    group = LANES // (rows * RUNS)
    ids = pack_ref[IDS].astype(jnp.bfloat16)
    eye = (iota((LANES, LANES), 0) == iota((LANES, LANES), 1)).astype(f32).astype(jnp.bfloat16)
    turned = lax.dot_general(eye, ids, NT, preferred_element_type=f32).astype(jnp.bfloat16)
    lined = jnp.zeros((line_ref.shape[0], LANES), f32)
    for i in range(group):
        shape = (line_ref.shape[0], LANES)
        take = (iota(shape, 1) == iota(shape, 0) * group + (i + OFF - LEFT)).astype(f32).astype(jnp.bfloat16)
        put = (iota((vr, LANES), 1) == iota((vr, LANES), 0) + i * vr).astype(f32).astype(jnp.bfloat16)
        some = jnp.dot(take, turned, preferred_element_type=f32).astype(jnp.bfloat16)
        lined = lined + jnp.dot(some, put, preferred_element_type=f32)
    line_ref[...] = lined

    seen_ref[...] = jnp.zeros_like(seen_ref)
    for copy in fetch[2:6]:
        copy.wait()
    embed = embed_ref[...]
    high, low = in_two(embed)
    split_ref[0] = high
    split_ref[1] = low

    taps = taps_ref[...]
    bias = bias_ref[...].reshape(1, feat)
    scorer = scorer_ref[...].reshape(1, feat)
    rows_ref[0:kernel, :] = taps
    rows_ref[BIAS : BIAS + 1, :] = bias
    rows_ref[SCORER : SCORER + 1, :] = scorer
    rows_ref[SCORER + 1 : 8, :] = jnp.zeros((7 - SCORER, feat), f32)
    for tile in range(feat // LANES):
        at = slice(tile % 4 * 8, tile % 4 * 8 + 8)
        pack_ref[WEIGHTS + tile // 4, at, :] = rows_ref[:, tile * LANES : (tile + 1) * LANES]
    table_ref[...] = jnp.zeros_like(table_ref)

    def inner(a, b):
        return lax.dot_general(a, b, NT, preferred_element_type=f32)

    def products(tile):
        cols = pl.ds(pl.multiple_of(tile * LANES, LANES), LANES)
        taps = rows_ref[0:kernel, cols]
        scaled = jnp.concatenate(
            [taps * rows_ref[SCORER : SCORER + 1, cols], taps * rows_ref[BIAS : BIAS + 1, cols]], axis=0
        )
        scaled = in_two(scaled)
        high, low = split_ref[0, :, cols], split_ref[1, :, cols]
        ones = jnp.ones((8, LANES), jnp.bfloat16)
        some = embed_ref[:, cols]
        squares = in_two(some * some)
        table_ref[0:8, :] = table_ref[0:8, :] + (
            inner(scaled[0], high) + (inner(scaled[0], low) + inner(scaled[1], high))
        )
        table_ref[8:16, :] = table_ref[8:16, :] + (inner(ones, squares[0]) + inner(ones, squares[1]))

    chunk = 2 * LANES
    lines = chunk // vr

    def embedding(step):
        marks = []
        for i in range(chunk // LANES):
            column = step * (chunk // LANES) + i
            bytes_here = jnp.broadcast_to(line_ref[pl.ds(column, 1), :], (vocab, LANES))
            marks.append(jnp.where(bytes_here == iota((vocab, LANES), 0).astype(f32), 1.0, 0.0))
            line = column * group + iota((1, LANES), 1) // vr
            inside = ((line >= LEFT) & (line < LEFT + run)).astype(f32)
            seen_ref[...] = seen_ref[...] + marks[i] * inside
        marks = jnp.concatenate(marks, axis=1).astype(jnp.bfloat16)
        turn_ref[:, pl.ds(pl.multiple_of(step * chunk, chunk), chunk)] = marks
        total = lax.dot_general(marks, split_ref[0], TN, preferred_element_type=f32)
        total = total + lax.dot_general(marks, split_ref[1], TN, preferred_element_type=f32)
        emb_ref[pl.ds(step * lines, lines)] = total.reshape(lines, vr, feat)

    chunks, tiles = span // lines, feat // LANES
    trips = next(n for n in (3, 1) if chunks % n == 0 and tiles % n == 0)

    def some_chunks(trip, carry):
        for i in range(chunks // trips):
            embedding(trip * (chunks // trips) + i)
        for i in range(tiles // trips):
            products(trip * (tiles // trips) + i)
        return carry

    lax.fori_loop(0, trips, some_chunks, 0)
    for i in range(vocab // vr):
        seen = jnp.sum(seen_ref[i * vr : (i + 1) * vr, :], axis=1, keepdims=True)
        pack_ref[SEEN + i] = jnp.broadcast_to(seen, (vr, LANES))
    keeps = [
        pltpu.make_async_copy(turn_ref, mark_hbm, sems.at[1, 0]), pltpu.make_async_copy(emb_ref, emb_hbm, sems.at[1, 1])
    ]
    for copy in keeps:
        copy.start()

    size = RUNS * half
    order = iota((size, size), 0)
    order = (iota((size, size), 1) == order % RUNS * half + order // RUNS).astype(f32)
    order_ref[...] = order.astype(jnp.bfloat16)

    def convolution(step, carry):
        r, pair = step % rows, step // rows
        sub = pl.ds(pl.multiple_of(r * RUNS, RUNS), RUNS)
        length = len_ref[r]
        for tile in range(WIDE // LANES):
            cols = pl.ds(pl.multiple_of(pair * WIDE + tile * LANES, LANES), LANES)
            taps = [jnp.broadcast_to(rows_ref[k : k + 1, cols], (RUNS, LANES)) for k in range(kernel)]
            window = [emb_ref[k, sub, cols] for k in range(kernel - 1)]
            for j in range(-2, run + 2):
                window.append(emb_ref[j + LEFT, sub, cols])
                total = taps[0] * window[0]
                for k in range(1, kernel):
                    total = total + taps[k] * window[k]
                window = window[1:]
                real = base < length - j
                if j < 0:
                    real = real & (base >= -j)
                conv_ref[j + 2, sub, cols] = jnp.where(real, total, 0.0)
        return carry

    lax.fori_loop(0, rows * (feat // WIDE), convolution, 0)
    keeps.append(pltpu.make_async_copy(conv_ref, conv_hbm, sems.at[2, 0]))
    keeps[-1].start()

    block = 4
    slices = run + 4
    zero = jnp.zeros((RUNS, LANES), f32)
    def lagged(r, carry):
        at = pl.ds(pl.multiple_of(r * RUNS, RUNS), RUNS)
        some = grad_ref.at[pl.ds(pl.multiple_of(r * size, 8), size), :]
        for pair in range(feat // WIDE):
            wide = slice(pair * WIDE, (pair + 1) * WIDE)
            high, low = in_two(some[:, wide])
            moved = jnp.dot(order_ref[...], high, preferred_element_type=f32)
            moved = moved + jnp.dot(order_ref[...], low, preferred_element_type=f32)
            cot_ref[:, at, wide] = moved.reshape(half, RUNS, WIDE)
        values = [zero] * 6
        for first in range(0, slices, block):
            acc = {}
            for tile in range(feat // LANES):
                cols = slice(tile * LANES, (tile + 1) * LANES)
                u = [conv_ref[first + i, at, cols] for i in range(min(block + 5, slices - first))]
                for i in range(block):
                    for lag in range(min(6, slices - first - i)):
                        term = u[i] * u[i + lag]
                        acc[i, lag] = term if tile == 0 else acc[i, lag] + term
            for i, lag in acc:
                here = lane == first + (i + OFF - 2)
                values[lag] = jnp.where(here, jnp.sum(acc[i, lag], axis=1, keepdims=True), values[lag])
        for lag in range(6):
            pack_ref[lag, at, :] = values[lag]
        return carry

    fetch[6].wait()
    lax.fori_loop(0, rows, lagged, 0)
    keeps.append(pltpu.make_async_copy(cot_ref, cot_hbm, sems.at[3, 0]))
    keeps[-1].start()

    def total_of(x):
        return jnp.sum(jnp.sum(x, axis=1, keepdims=True), axis=0, keepdims=True)

    def lookups(r, sums):
        at = pl.ds(pl.multiple_of(r * RUNS, RUNS), RUNS)
        ids = pack_ref[IDS, at, :].astype(jnp.int32)
        real = ids >= 0
        low = jnp.where(real, ids, 0)

        def look(row):
            value = jnp.zeros((RUNS, LANES), f32)
            for part in range(vocab // LANES):
                entry = jnp.broadcast_to(
                    table_ref[row : row + 1, part * LANES : (part + 1) * LANES], (RUNS, LANES)
                )
                taken = jnp.take_along_axis(entry, low % LANES, axis=1)
                value = jnp.where(low // LANES == part, taken, value)
            return jnp.where(real, value, 0.0)

        scored = jnp.zeros((RUNS, LANES), f32)
        biased = jnp.zeros((RUNS, LANES), f32)
        for k in range(kernel):
            scored = scored + shifted(look(k), k - (kernel - 1))
            biased = biased + shifted(look(4 + k), k - (kernel - 1))
        inner_real = real & (lane >= OFF - 2)
        scored = jnp.where(inner_real, scored, 0.0)
        biased = jnp.where(inner_real, biased, 0.0)
        pack_ref[13, at, :] = scored
        pack_ref[14, at, :] = biased
        own = (real & (lane >= OFF) & (lane < OFF + run)).astype(f32)
        new = (own * look(8), own, own * biased, own * pack_ref[0, at, :], own * (1 - lane % 2).astype(f32))
        return tuple(a + b for a, b in zip(sums, new))

    def crossed(r, sums):
        at = pl.ds(pl.multiple_of(r * RUNS, RUNS), RUNS)
        sums = lookups(r, sums)
        values = [zero] * 7
        for first in range(0, half, block):
            acc = {}
            for tile in range(feat // LANES):
                cols = slice(tile * LANES, (tile + 1) * LANES)
                u = [conv_ref[2 * first + i, at, cols] for i in range(2 * block + 4)]
                bias = jnp.broadcast_to(rows_ref[BIAS : BIAS + 1, tile * LANES : (tile + 1) * LANES], (RUNS, LANES))
                for i in range(block):
                    g = cot_ref[first + i, at, cols]
                    terms = [g * u[2 * i + d] for d in range(6)] + [g * bias]
                    for d in range(7):
                        acc[i, d] = terms[d] if tile == 0 else acc[i, d] + terms[d]
            for i, d in acc:
                here = lane == 2 * first + (2 * i + OFF)
                values[d] = jnp.where(here, jnp.sum(acc[i, d], axis=1, keepdims=True), values[d])
        for d in range(7):
            pack_ref[6 + d, at, :] = values[d]
        return sums

    sums = lax.fori_loop(0, rows, crossed, (zero,) * 5)
    sums_ref[...] = spread([total_of(x) for x in sums], sums_ref.shape[0])
    for copy in keeps:
        copy.wait()


def in_two(x):
    high = x.astype(jnp.bfloat16)
    return high, (x - high.astype(f32)).astype(jnp.bfloat16)


def unpack_rows(pack_ref, rows_ref):
    for tile in range(rows_ref.shape[1] // LANES):
        at = slice(tile % 4 * 8, tile % 4 * 8 + 8)
        rows_ref[:, tile * LANES : (tile + 1) * LANES] = pack_ref[WEIGHTS + tile // 4, at, :]


def spread(sums, count):
    lane = iota((1, LANES), 1)
    row = jnp.zeros((1, LANES), f32)
    for i, x in enumerate(sums):
        row = jnp.where(lane == i, x, row)
    return jnp.broadcast_to(row[None], (count, 1, LANES))


def picked(ref, number):
    row = jnp.sum(ref[...], axis=0)
    return [row[:, i : i + 1] for i in range(number)]


def scales(first_ref, bias, feat):
    emb_sum, count, cross, square, count4 = picked(first_ref, 5)
    one = jnp.sqrt(emb_sum / (count * feat) + EPS)
    bias_sum = jnp.sum(bias * bias, axis=1, keepdims=True)
    conv_sum = jnp.maximum(count * bias_sum + 2.0 * cross / one + square / (one * one), 0.0)
    two = jnp.sqrt(conv_sum / (count * feat) + EPS)
    return one, two, count, count4, bias_sum, cross


class Places:
    def __init__(self, ids, start, run):
        shape = ids.shape
        self.j = iota(shape, 1) - OFF
        sub = iota(shape, 0) % RUNS
        self.inside = (self.j >= 0) & (self.j < run)
        self.real = ((ids >= 0) & (self.j >= -2)).astype(f32)
        self.own = jnp.where(self.inside, self.real, 0.0)
        shown = self.j + OFF
        self.two, self.four = shown % 2, shown % 4
        self.three = (start + run * sub + shown + (3 * OFF - OFF)) % 3

    def holds(self, size, by):
        if size == 1:
            return jnp.ones_like(self.real) if by == 0 else None
        if abs(by) >= size:
            return None
        phase = {2: self.two, 3: self.three, 4: self.four}[size]
        return ((phase + by >= 0) & (phase + by < size)).astype(f32)

    def pooled(self, size, x):
        if size == 1:
            return x
        pair = x + jnp.where(self.two == 0, shifted(x, 1), shifted(x, -1))
        if size == 2:
            return pair
        if size == 4:
            return pair + jnp.where(self.four < 2, shifted(pair, 2), shifted(pair, -2))
        left, right = shifted(x, -1), shifted(x, 1)
        side = jnp.where(self.three == 0, shifted(x, 2), left)
        far = jnp.where(self.three == 2, shifted(x, -2), right)
        return x + side + far

    def both(self, x):
        return x + shifted(x, -1)


SIZES = (1, 2, 3, 4)
REACH = range(-3, 4)


def score_kernel(sizes, first_ref, dots_ref, state_ref, sums_ref, rows_ref):
    rows, width, run, feat, vocab, kernel = sizes
    start = lax.axis_index("seq") * width
    unpack_rows(dots_ref, rows_ref)
    bias = rows_ref[BIAS : BIAS + 1, :]
    one, two, count, count4, bias_sum, cross = scales(first_ref, bias, feat)
    at = Places(dots_ref[IDS], start, run)
    real, own = at.real, at.own
    rate = 1.0 / (one * two)
    bias_score = jnp.sum(bias * rows_ref[SCORER : SCORER + 1, :], axis=1, keepdims=True) / two

    normed_score = real * bias_score + rate * dots_ref[13]
    counts = [jnp.maximum(at.pooled(b, real), 1.0) for b in SIZES]
    scores = [at.pooled(b, normed_score) / n for b, n in zip(SIZES, counts)]
    top = functools.reduce(jnp.maximum, scores)
    parts = [jnp.exp(s - top) for s in scores]
    whole = sum(parts)
    probs = [p / whole for p in parts]
    weights = [own * p / n for p, n in zip(probs, counts)]

    holds = {(b, d): at.holds(b, d) for b in SIZES for d in REACH}

    def blend(values):
        out = {}
        for d in REACH:
            terms = [v * holds[b, d] for b, v in zip(SIZES, values) if holds[b, d] is not None]
            out[d] = sum(terms)
        return out

    mixer = blend(weights)
    pair_count = jnp.maximum(at.pooled(2, real), 1.0)
    halver = {}
    even = at.two == 0
    for d in REACH:
        zero = jnp.zeros_like(real)
        ahead = shifted(mixer[d - 1], 1) if d - 1 >= -3 else zero
        behind = shifted(mixer[d + 1], -1) if d + 1 <= 3 else zero
        other = jnp.where(even, ahead, behind)
        halver[d] = jnp.where(at.inside, (mixer[d] + other) / pair_count, 0.0)

    bias_dot = dots_ref[14]
    normed_bias = real * (bias_sum / two) + rate * bias_dot
    lags = []
    for lag in range(6):
        later = shifted(real, lag)
        value = rate * rate * dots_ref[lag]
        value = value + (rate / two) * (bias_dot * later + real * shifted(bias_dot, lag))
        lags.append(value + (bias_sum / (two * two)) * (real * later))

    def gram(a, b):
        low, high = min(a, b), max(a, b)
        return shifted(lags[high - low], low) if high - low < 6 else None

    table = {(a, b): gram(a, b) for a in REACH for b in REACH if a <= b}

    def against(weighting):
        out = {}
        for a in REACH:
            out[a] = sum(
                weighting[b] * table[min(a, b), max(a, b)]
                for b in REACH if table[min(a, b), max(a, b)] is not None
            )
        return out

    with_mixed, with_half = against(mixer), against(halver)
    with_grad = {}
    grad_bias = dots_ref[12]
    cross_dots = {
        d: rate * dots_ref[6 + d + 2] + shifted(real, d) * (grad_bias / two) for d in range(-2, 4)
    }
    for d in REACH:
        here = cross_dots[d] if d >= -2 else jnp.zeros_like(real)
        before = shifted(cross_dots[d + 1], -1) if d + 1 <= 3 else jnp.zeros_like(real)
        with_grad[d] = jnp.where(even, here, before)

    def per_block(values, scale):
        out = []
        for b, n in zip(SIZES, counts):
            terms = [values[d] * holds[b, d] for d in REACH if holds[b, d] is not None]
            out.append(scale * sum(terms) / n)
        return out

    shared = own / pair_count
    bases = [per_block(with_grad, shared), per_block(with_half, shared), per_block(with_mixed, own)]

    def total_of(x):
        return jnp.sum(jnp.sum(x, axis=1, keepdims=True), axis=0, keepdims=True)

    first_of_pair = jnp.where(even & at.inside, 1.0, 0.0)
    mean_score = sum(p * s for p, s in zip(probs, scores))

    def bent(values):
        mean = sum(p * v for p, v in zip(probs, values))
        return total_of(own * (sum(p * s * v for p, s, v in zip(probs, scores, values)) - mean * mean_score))

    sums = [
        total_of(sum(own * mixer[d] * with_mixed[d] for d in REACH)),
        total_of(first_of_pair * sum(halver[d] * with_half[d] for d in REACH)),
        total_of(first_of_pair * sum(halver[d] * with_grad[d] for d in REACH)),
        bent(bases[0]), bent(bases[1]), bent(bases[2]),
        total_of(shared * at.both(grad_bias)),
        total_of(shared * sum(halver[d] * shifted(normed_bias, d) for d in REACH)),
        total_of(own * sum(mixer[d] * shifted(normed_bias, d) for d in REACH)),
    ]
    for i, b in enumerate(SIZES):
        state_ref[i] = weights[i]
        state_ref[4 + i] = probs[i]
        for f in range(3):
            state_ref[8 + 4 * f + i] = bases[f][i]
    sums_ref[...] = spread(sums, sums_ref.shape[0])


def back_kernel(
    sizes, first_hbm, second_hbm, pack_hbm, state_hbm, mark_hbm, embed_hbm, conv_hbm, emb_hbm, cot_hbm,
    out_hbm, keep_ref, send_ref,
    first_ref, second_ref, pack_ref, state_ref, mark_ref, embed_ref, rows_ref, turn_ref, out_ref, order_ref,
    narrow_ref, acc_ref, pay_ref, conv_ref, emb_ref, cot_ref, back_ref, sems,
):
    rows, width, run, feat, vocab, kernel = sizes
    tiles = feat // LANES
    per = WIDE // LANES
    units = rows * (feat // WIDE)
    half = run // 2
    vr = rows * RUNS

    def fetches(unit):
        sub = pl.ds(pl.multiple_of(unit % rows * RUNS, RUNS), RUNS)
        cols = pl.ds(pl.multiple_of(unit // rows * WIDE, LANES), WIDE)
        return [
            pltpu.make_async_copy(a.at[:, sub, cols], b.at[:, sub, cols], sems.at[i, unit])
            for i, (a, b) in enumerate(((conv_hbm, conv_ref), (cot_hbm, cot_ref), (emb_hbm, emb_ref)))
        ]

    size = RUNS * half

    def stored(unit):
        some = pl.ds(pl.multiple_of(unit % rows * size, 8), size)
        cols = pl.ds(pl.multiple_of(unit // rows * WIDE, LANES), WIDE)
        return pltpu.make_async_copy(out_ref.at[some, cols], out_hbm.at[some, cols], sems.at[3, unit])

    def restore(unit):
        some = pl.ds(pl.multiple_of(unit % rows * size, 8), size)
        cols = pl.ds(pl.multiple_of(unit // rows * WIDE, LANES), WIDE)
        high, low = in_two(turn_ref[...].reshape(size, WIDE))
        moved = jnp.dot(order_ref[...], high, preferred_element_type=f32)
        out_ref[some, cols] = moved + jnp.dot(order_ref[...], low, preferred_element_type=f32)

    sources = (first_hbm, second_hbm, pack_hbm, state_hbm, mark_hbm, embed_hbm)
    targets = (first_ref, second_ref, pack_ref, state_ref, mark_ref, embed_ref)
    small = [pltpu.make_async_copy(a, b, sems.at[4, i]) for i, (a, b) in enumerate(zip(sources, targets))]
    small[2] = pltpu.make_async_copy(pack_hbm.at[IDS:], pack_ref.at[IDS:], sems.at[4, 2])
    ahead = 3
    for copy in small[:4]:
        copy.start()
    for unit in range(ahead):
        for copy in fetches(unit):
            copy.start()
    for copy in small[4:]:
        copy.start()
    for copy in small[:4]:
        copy.wait()

    start = lax.axis_index("seq") * width
    unpack_rows(pack_ref, rows_ref)
    bias = rows_ref[BIAS : BIAS + 1, :]
    one, two, count, count4, bias_sum, cross = scales(first_ref, bias, feat)
    mixed_sum, half_sum, inner, bent_g, bent_h, bent_m, bias_g, bias_h, bias_m = picked(second_ref, 9)
    volume, volume4 = count * feat, count4 * feat
    three = jnp.sqrt(mixed_sum / volume + EPS)
    four = jnp.sqrt(half_sum / (three * three) / volume4 + EPS)
    fourth = (inner / three) / (four * four * four * volume4)
    alpha = 1.0 / (three * four)
    beta = -fourth / (three * three)
    gamma = -(inner / four - fourth / three * half_sum) / (three * three * three * volume)
    joint = alpha * (inner + bent_g) + beta * (half_sum + bent_h) + gamma * (mixed_sum + bent_m)
    rate = 1.0 / (one * two)
    normed_bias = count * bias_sum / two + rate * cross
    bias_back = (alpha * bias_g + beta * bias_h + gamma * bias_m - joint / volume * normed_bias) / two
    inner_one = one * (joint * EPS / (two * two) - bias_back)
    first_coef = inner_one / (one * one * one * volume)

    at = Places(pack_ref[IDS], start, run)
    probs = [state_ref[4 + i] for i in range(4)]
    weights = [state_ref[i] for i in range(4)]
    grads = [
        alpha * state_ref[8 + i] + beta * state_ref[12 + i] + gamma * state_ref[16 + i] for i in range(4)
    ]
    mean = sum(p * g for p, g in zip(probs, grads))
    spreading = jnp.zeros_like(probs[0])
    for i, b in enumerate(SIZES):
        bent = probs[i] * (grads[i] - mean)
        n = jnp.maximum(at.pooled(b, at.real), 1.0)
        spreading = spreading + at.pooled(b, jnp.where(at.inside, bent / n, 0.0))
    pair_real = at.pooled(2, at.real)
    pair_count = jnp.maximum(pair_real, 1.0)
    filled = (pair_real > 0).astype(f32)
    narrow = [rate * w for w in weights] + [rate * spreading, at.real]
    paired = [
        alpha / pair_count, alpha * filled, beta / (pair_count * pair_count), beta * filled / pair_count + gamma
    ]
    leak = jnp.sum(jnp.sum(spreading * at.real, axis=1, keepdims=True), axis=0, keepdims=True)

    for i, x in enumerate(narrow + paired):
        narrow_ref[i] = x
    order = iota((size, size), 0)
    order = (iota((size, size), 1) == order % half * RUNS + order // half).astype(f32)
    order_ref[...] = order.astype(jnp.bfloat16)
    turn_ref[...] = jnp.zeros_like(turn_ref)
    acc_ref[...] = jnp.zeros_like(acc_ref)
    phase = (start + run * iota((RUNS, LANES), 0)) % 3
    at_phase = [phase == p for p in range(3)]

    def chosen(j, a, b, c):
        return jnp.where(at_phase[(0 - j) % 3], a, jnp.where(at_phase[(1 - j) % 3], b, c))

    full = (RUNS, LANES)
    alpha_all = jnp.broadcast_to(alpha, full)
    gamma_all = jnp.broadcast_to(gamma, full)
    fall = jnp.broadcast_to(rate * rate * joint / volume, full)
    fall_bias = rate * joint / volume / two

    def column(r, tile, near, factor):
        sub = pl.ds(pl.multiple_of(r * RUNS, RUNS), RUNS)
        cols = pl.ds(pl.multiple_of(tile * LANES, LANES), LANES)
        taps = [jnp.broadcast_to(rows_ref[k : k + 1, cols], full) for k in range(kernel)]
        bias_row = rows_ref[BIAS : BIAS + 1, cols]
        normed_row = jnp.broadcast_to(bias_row / two, full)
        fall_row = jnp.broadcast_to(bias_row * fall_bias, full)
        scorer = jnp.broadcast_to(rows_ref[SCORER : SCORER + 1, cols], full)
        zero = jnp.zeros(full, f32)

        u, triple, y3, gc = {}, {}, {}, {}
        sums = [zero] * (kernel + 2)
        block = {}
        twos, y_twos = {}, {}
        for j in range(-2, 2):
            u[j] = conv_ref[j + 2, sub, cols]

        def pair_of(j):
            if j not in twos:
                twos[j] = u[j] + u[j + 1]
            return twos[j]

        triple[-2] = pair_of(-2) + u[0]
        triple[-1] = u[-1] + pair_of(0)

        def window(j):
            if 0 <= j <= run - 3:
                first = j if j % 2 == 0 else j + 1
                if first not in y_twos:
                    y_twos[first] = y3[first] + y3[first + 1]
                return y_twos[first] + y3[j + 2 if j % 2 == 0 else j]
            near = [y3[i] for i in (j, j + 1, j + 2) if 0 <= i < run]
            return functools.reduce(lambda a, b: a + b, near) if near else zero

        def settle(s):
            nonlocal sums
            for j in (s, s - 1, s - 2):
                if j not in block:
                    block[j] = window(j)
            g = chosen(s, block[s], block[s - 1], block[s - 2])
            sigma = factor(4, s)
            g = g + sigma * scorer
            if 0 <= s < run:
                g = g + lone[s]
                g = g - fall * u[s]
            g = g * factor(5, s)
            gc[s] = g
            for k in range(kernel):
                sums[k] = sums[k] + g * emb_ref[s - kernel + 1 + k + LEFT, sub, cols]
            sums[kernel] = sums[kernel] + g
            sums[kernel + 1] = sums[kernel + 1] + sigma * u[s]

        def finish(s):
            terms = [taps[k] * gc[s + kernel - 1 - k] for k in range(kernel) if s + kernel - 1 - k in gc]
            back_ref[s + LEFT, sub, cols] = functools.reduce(lambda a, b: a + b, terms)

        lone = {}
        settled = -2
        finished = -LEFT
        for quad in range(0, run, 4):
            for j in range(quad + 2, quad + 6):
                u[j] = conv_ref[j + 2, sub, cols]
            two_sums = [pair_of(quad), pair_of(quad + 2)]
            four_sum = two_sums[0] + two_sums[1]
            shares = []
            wide = zero
            for p in range(2):
                y = None
                xs = []
                for j in (quad + 2 * p, quad + 2 * p + 1):
                    triple[j] = u[j] + pair_of(j + 1) if j % 2 else two_sums[p] + u[j + 2]
                    x = factor(0, j) * u[j] + factor(1, j) * two_sums[p]
                    x = x + factor(2, j) * chosen(j, triple[j], triple[j - 1], triple[j - 2])
                    x = x + factor(3, j) * four_sum
                    xs.append(x)
                y = xs[0] + xs[1]
                k = quad // 2 + p
                scale_y = factor(6, 2 * k)
                turn_ref[k, :, near] = scale_y * y + factor(7, 2 * k) * normed_row
                q = scale_y * cot_ref[k, sub, cols] + factor(8, 2 * k) * y + factor(9, 2 * k) * normed_row
                pair = zero
                for i, j in enumerate((quad + 2 * p, quad + 2 * p + 1)):
                    g = q + gamma_all * xs[i]
                    lone[j] = factor(0, j) * g
                    y3[j] = factor(2, j) * g
                    pair = factor(1, j) * g if i == 0 else pair + factor(1, j) * g
                    wide = factor(3, j) * g if i + p == 0 else wide + factor(3, j) * g
                shares.append(pair)
            wide = wide - fall_row
            for p in range(2):
                share = shares[p] + wide
                for j in (quad + 2 * p, quad + 2 * p + 1):
                    lone[j] = lone[j] + share
            last = quad + 3 - 2 if quad + 4 < run else run + 1
            while settled <= last:
                settle(settled)
                settled += 1
            done = settled - kernel if quad + 4 < run else run + RIGHT - 1
            while finished <= done:
                finish(finished)
                finished += 1
            yield
        for i in range(kernel + 2):
            acc_ref[i, :, cols] = acc_ref[i, :, cols] + sums[i]

    def some_columns(unit, carry):
        for copy in fetches(unit):
            copy.wait()

        @pl.when(unit + ahead < units)
        def _():
            for copy in fetches(unit + ahead):
                copy.start()

        r = unit % rows
        made = {}

        def factor(i, j):
            if (i, j) not in made:
                sub = pl.ds(pl.multiple_of(r * RUNS, RUNS), RUNS)
                made[i, j] = jnp.broadcast_to(narrow_ref[i, sub, j + OFF : j + OFF + 1], full)
            return made[i, j]

        last = jnp.maximum(unit - 1, 0)
        restore(last)
        parts = []
        for i in range(per):
            near = slice(i * LANES, (i + 1) * LANES)
            parts.append(column(r, unit // rows * per + i, near, factor))
        for _ in zip(*parts, strict=True):
            pass

        @pl.when(unit > 0)
        def _():
            stored(last).start()

        return carry

    lax.fori_loop(0, units, some_columns, 0)
    restore(units - 1)
    stored(units - 1).start()

    positions = mark_ref.shape[1]
    edge = run + LEFT + RIGHT
    back_ref[edge:] = jnp.zeros((back_ref.shape[0] - edge, vr, feat), f32)
    for copy in small[4:]:
        copy.wait()
    total_tiles = pay_ref.shape[0]

    def gather(pair, carry):
        cols = pl.ds(pl.multiple_of(pair * WIDE, LANES), WIDE)
        high, low = in_two(back_ref[:, :, cols].reshape(positions, WIDE))
        total = jnp.dot(mark_ref[...], high, preferred_element_type=f32)
        total = total + jnp.dot(mark_ref[...], low, preferred_element_type=f32)
        for v in range(vocab // 8):
            seen = first_coef * pack_ref[SEEN + v * 8 // vr, v * 8 % vr : v * 8 % vr + 8, :]
            for i in range(per):
                wide = pl.ds(pl.multiple_of(pair * WIDE + i * LANES, LANES), LANES)
                part = total[v * 8 : v * 8 + 8, i * LANES : (i + 1) * LANES]
                pay_ref[v * tiles + pair * per + i] = part - seen * embed_ref[v * 8 : v * 8 + 8, wide]
        return carry

    lax.fori_loop(0, feat // WIDE, gather, 0)

    end = vocab // 8 * tiles
    pay_ref[end:] = jnp.zeros((total_tiles - end, 8, LANES), f32)
    for i in range(kernel + 2):
        row = jnp.sum(acc_ref[i], axis=0, keepdims=True)
        if i == kernel:
            row = row * one
        if i == kernel + 1:
            row = row + bias * (leak / two)
        for tile in range(tiles):
            place = i * tiles + tile
            pay_ref[end + place // 8, place % 8 : place % 8 + 1, :] = row[:, tile * LANES : (tile + 1) * LANES]
    core = lax.axis_index("seq") % 2
    part = total_tiles // 2
    keep_ref[...] = pay_ref[pl.ds(core * part, part)]
    send_ref[...] = pay_ref[pl.ds((1 - core) * part, part)]
    for unit in range(units):
        stored(unit).wait()


def finish_kernel(feat, mine_ref, other_ref, table_hbm, taps_ref, bias_ref, scorer_ref, sems):
    core = lax.axis_index("seq") % 2
    tiles = feat // LANES
    part = mine_ref.shape[0]
    rest = table_hbm.shape[0] - part
    for side in range(2):

        @pl.when(core == side)
        def _():
            first, second = (mine_ref, other_ref) if side == 0 else (other_ref, mine_ref)
            copies = (
                pltpu.make_async_copy(first, table_hbm.at[0:part], sems.at[0]),
                pltpu.make_async_copy(second.at[0:rest], table_hbm.at[part : part + rest], sems.at[1]),
            )
            for copy in copies:
                copy.start()
            lines = []
            for i in range(taps_ref.shape[0] + 2):
                places = [i * tiles + tile for tile in range(tiles)]
                lines.append([second[rest + p // 8, p % 8 : p % 8 + 1, :] for p in places])
            for i in range(taps_ref.shape[0]):
                taps_ref[i : i + 1, :] = jnp.concatenate(lines[i], axis=1)
            bias_ref[...] = jnp.concatenate(lines[-2], axis=1).reshape(feat)
            scorer_ref[...] = jnp.concatenate(lines[-1], axis=1).reshape(feat)
            for copy in copies:
                copy.wait()


def exchanged(x):
    return lax.all_to_all(x, AXES, 0, 0, tiled=True)


def partner(x, axis, step):
    n = lax.axis_size(axis)
    return lax.ppermute(x, axis, [(i, i ^ step) for i in range(n)])


def summed_over_devices(keep, send):
    n = lax.axis_size("seq")
    others = lax.axis_size("rows") * n // 2
    groups = [[2 * i + side for i in range(others)] for side in range(2)]

    def traded(x):
        return lax.all_to_all(x, AXES, 0, 0, tiled=True, axis_index_groups=groups)

    x = keep + partner(send, "seq", 1)
    chunk = (others, x.shape[0] * x.shape[1] // others, 1, LANES)
    part = jnp.sum(traded(x.reshape(chunk)), axis=0)
    x = traded(jnp.broadcast_to(part[None], chunk)).reshape(x.shape)
    return x, partner(x, "seq", 1)


def on_device(byte_ids, lengths, embed, conv_weight, conv_bias, score_weight, out_grad):
    rows, width = byte_ids.shape
    vocab, feat = embed.shape
    kernel = conv_weight.shape[0]
    run = width // RUNS
    half = width // 2
    vr = rows * RUNS
    sizes = (rows, width, run, feat, vocab, kernel)
    count = lax.axis_size("seq")
    devices = count * lax.axis_size("rows")
    span = -(-(run + LEFT + RIGHT) // 8) * 8
    tiles = feat // LANES
    struct = jax.ShapeDtypeStruct
    sem = pltpu.SemaphoreType.DMA

    params = pltpu.CompilerParams(vmem_limit_bytes=60 * 1024 * 1024)

    up = [(i, i + 1) for i in range(count - 1)]
    left = pltpu.with_memory_space_constraint(lax.ppermute(byte_ids, "seq", up), pltpu.VMEM)
    right = pltpu.with_memory_space_constraint(lax.ppermute(byte_ids, "seq", [(j, i) for i, j in up]), pltpu.VMEM)

    pairs = feat // WIDE
    bf16 = jnp.bfloat16
    wide_emb = struct((span, vr, feat), f32)
    wide_conv = struct((run + 4, vr, feat), f32)
    wide_cot = struct((half // RUNS, vr, feat), f32)
    marks = struct((vocab, span * vr), bf16)
    pack = struct((SEEN + vocab // vr, vr, LANES), f32)
    sums = struct((devices, 1, LANES), f32)
    state = struct((20, vr, LANES), f32)

    def scratch(like):
        return pltpu.VMEM(like.shape, like.dtype)

    emb, conv, cot, mark, packed, first = pl.pallas_call(
        functools.partial(stats_kernel, sizes),
        out_shape=(*(pltpu.HBM(x.shape, x.dtype) for x in (wide_emb, wide_conv, wide_cot, marks, pack)), pltpu.VMEM(sums.shape, f32)),
        in_specs=[HBM, VMEM, VMEM] + [HBM] * 6, out_specs=(HBM,) * 4 + (VMEM,) * 2,
        scratch_shapes=[
            scratch(byte_ids), pltpu.SMEM((rows,), jnp.int32), scratch(embed),
            scratch(conv_weight), scratch(conv_bias), scratch(score_weight), pltpu.VMEM((rows * half, feat), f32),
            pltpu.VMEM((2, vocab, feat), bf16), pltpu.VMEM((16, vocab), f32), pltpu.VMEM((8, feat), f32),
            scratch(marks), pltpu.VMEM((-(-span * vr // LANES // 8) * 8, LANES), f32), pltpu.VMEM((vocab, LANES), f32),
            pltpu.VMEM((half, half), bf16), pltpu.VMEM((vr, LANES), jnp.int32), scratch(wide_emb),
            scratch(wide_conv), scratch(wide_cot), sem((4, 9)),
        ],
        compiler_params=params, name="stats",
    )(
        byte_ids, left, right, lengths, embed, conv_weight, conv_bias, score_weight,
        out_grad.reshape(rows * half, feat),
    )
    first = exchanged(first)

    states, second = pl.pallas_call(
        functools.partial(score_kernel, sizes),
        out_shape=(pltpu.HBM(state.shape, f32), pltpu.VMEM(sums.shape, f32)),
        in_specs=[VMEM] * 2, out_specs=(VMEM, VMEM), scratch_shapes=[pltpu.VMEM((8, feat), f32)],
        compiler_params=params, name="score",
    )(first, packed)
    second = exchanged(second)

    lines = vocab * tiles
    lines = -(-(lines + (kernel + 2) * tiles) // devices) * devices
    parts = struct((lines // 16, 8, LANES), f32)
    blocks, keep, send = pl.pallas_call(
        functools.partial(back_kernel, sizes),
        out_shape=(pltpu.HBM((rows * half, feat), f32), pltpu.VMEM(parts.shape, f32), pltpu.VMEM(parts.shape, f32)),
        in_specs=[HBM] * 9, out_specs=(HBM, VMEM, VMEM),
        scratch_shapes=[
            scratch(sums), scratch(sums), scratch(pack), scratch(state), scratch(marks), scratch(embed),
            pltpu.VMEM((8, feat), f32), pltpu.VMEM((half // RUNS, RUNS, WIDE), f32),
            pltpu.VMEM((rows * half, feat), f32), pltpu.VMEM((half, half), bf16), pltpu.VMEM((10, vr, LANES), f32),
            pltpu.VMEM((kernel + 2, RUNS, feat), f32), pltpu.VMEM((lines // 8, 8, LANES), f32),
            scratch(wide_conv), scratch(wide_emb), scratch(wide_cot), scratch(wide_emb),
            sem((5, max(6, rows * pairs))),
        ],
        compiler_params=params, name="back",
    )(first, second, packed, states, mark, embed, conv, emb, cot)

    mine, other = summed_over_devices(keep, send)
    table, taps_grad, bias_grad, scorer_grad = pl.pallas_call(
        functools.partial(finish_kernel, feat),
        out_shape=(
            pltpu.HBM((vocab * tiles // 8, 8, LANES), f32), struct((kernel, feat), f32), struct((feat,), f32),
            struct((feat,), f32),
        ),
        in_specs=[VMEM, VMEM], out_specs=(HBM, VMEM, VMEM, VMEM), scratch_shapes=[sem((2,))],
        compiler_params=pltpu.CompilerParams(vmem_limit_bytes=8 * 1024 * 1024), name="finish",
    )(mine, other)
    table = table.reshape(vocab // 8, tiles, 8, LANES).transpose(0, 2, 1, 3).reshape(vocab, feat)
    return blocks.reshape(rows, half, feat), table, taps_grad, bias_grad, scorer_grad


def solution(mesh):
    placed = (P("rows", "seq"), P("rows"), P(), P(), P(), P(), P("rows", "seq", None))
    return jax.shard_map(
        on_device,
        mesh=mesh,
        in_specs=placed,
        out_specs=(P("rows", "seq", None), P(), P(), P(), P()),
        check_vma=False,
    )
```

```python
import functools

import jax
import jax.numpy as jnp
from jax import lax
from jax.experimental import pallas as pl
from jax.experimental.pallas import tpu as pltpu
from jax.sharding import PartitionSpec as P

f32 = jnp.float32
EPS = 1e-06
LANES = 128
WIDE = 256
RUNS = 8
OFF = 8
LEFT, RIGHT = 5, 2
NT = (((1,), (1,)), ((), ()))
TN = (((0,), (0,)), ((), ()))
AXES = ("rows", "seq")
VMEM = pl.BlockSpec(memory_space=pltpu.VMEM)
HBM = pl.BlockSpec(memory_space=pltpu.HBM)


def iota(shape, dim):
    return lax.broadcasted_iota(jnp.int32, shape, dim)


def shifted(x, by):
    return x if by == 0 else pltpu.roll(x, (-by) % LANES, 1)


BIAS, SCORER = 4, 5
IDS, WEIGHTS, SEEN = 15, 16, 18


def stats_kernel(
    sizes, own_hbm, even_ref, odd_ref, len_hbm, embed_hbm, taps_hbm, bias_hbm, scorer_hbm, grad_hbm,
    emb_hbm, conv_hbm, cot_hbm, mark_hbm, pack_ref, sums_ref,
    own_ref, len_ref, embed_ref, taps_ref, bias_ref, scorer_ref, grad_ref,
    split_ref, table_ref, rows_ref, turn_ref, line_ref, seen_ref, order_ref, run_ref, emb_ref, conv_ref, cot_ref, sems,
):
    rows, width, run, feat, vocab, kernel = sizes
    half = run // 2
    vr = rows * RUNS
    span = emb_ref.shape[0]
    sources = (own_hbm, len_hbm, embed_hbm, taps_hbm, bias_hbm, scorer_hbm, grad_hbm)
    targets = (own_ref, len_ref, embed_ref, taps_ref, bias_ref, scorer_ref, grad_ref)
    fetch = [pltpu.make_async_copy(a, b, sems.at[0, i]) for i, (a, b) in enumerate(zip(sources, targets))]
    for copy in fetch:
        copy.start()
    start = lax.axis_index("seq") * width
    lane = iota((RUNS, LANES), 1)
    sub = iota((RUNS, LANES), 0)
    base = start + run * sub
    back = (OFF - run) % LANES

    for copy in fetch[:2]:
        copy.wait()
    for r in range(rows):
        for s in range(RUNS):
            line = own_ref[r : r + 1, s * run // LANES * LANES : (s * run // LANES + 1) * LANES]
            shift = -(s * run % LANES) % LANES
            line = jnp.broadcast_to(line, (RUNS, LANES))
            line = pltpu.roll(line, shift, 1) if shift else line
            run_ref[r * RUNS + s : r * RUNS + s + 1, :] = line[0:1]
    odd = lax.axis_index("seq") % 2 == 1
    for r in range(rows):
        own = run_ref[r * RUNS : (r + 1) * RUNS, :]
        tail = slice(width - LANES, width)
        left = jnp.where(odd, even_ref[r : r + 1, tail], odd_ref[r : r + 1, tail])
        right = jnp.where(odd, odd_ref[r : r + 1, 0:LANES], even_ref[r : r + 1, 0:LANES])
        before = pltpu.roll(pltpu.roll(own, 1, 0), back, 1)
        edge = pltpu.roll(jnp.broadcast_to(left, (RUNS, LANES)), OFF, 1)
        before = jnp.where(sub == 0, edge, before)
        after = pltpu.roll(pltpu.roll(own, RUNS - 1, 0), OFF + run, 1)
        edge = pltpu.roll(jnp.broadcast_to(right, (RUNS, LANES)), OFF + run, 1)
        after = jnp.where(sub == RUNS - 1, edge, after)
        ids = jnp.where(lane < OFF, before, jnp.where(lane < OFF + run, pltpu.roll(own, OFF, 1), after))
        place = base + lane - OFF
        real = (place >= 0) & (place < len_ref[r])
        real = real & (lane >= OFF - LEFT) & (lane < OFF + run + RIGHT)
        pack_ref[IDS, r * RUNS : (r + 1) * RUNS, :] = jnp.where(real, ids, -1).astype(f32)

    group = LANES // (rows * RUNS)
    ids = pack_ref[IDS].astype(jnp.bfloat16)
    eye = (iota((LANES, LANES), 0) == iota((LANES, LANES), 1)).astype(f32).astype(jnp.bfloat16)
    turned = lax.dot_general(eye, ids, NT, preferred_element_type=f32).astype(jnp.bfloat16)
    lined = jnp.zeros((line_ref.shape[0], LANES), f32)
    for i in range(group):
        shape = (line_ref.shape[0], LANES)
        take = (iota(shape, 1) == iota(shape, 0) * group + (i + OFF - LEFT)).astype(f32).astype(jnp.bfloat16)
        put = (iota((vr, LANES), 1) == iota((vr, LANES), 0) + i * vr).astype(f32).astype(jnp.bfloat16)
        some = jnp.dot(take, turned, preferred_element_type=f32).astype(jnp.bfloat16)
        lined = lined + jnp.dot(some, put, preferred_element_type=f32)
    line_ref[...] = lined

    seen_ref[...] = jnp.zeros_like(seen_ref)
    for copy in fetch[2:6]:
        copy.wait()
    embed = embed_ref[...]
    high, low = in_two(embed)
    split_ref[0] = high
    split_ref[1] = low

    taps = taps_ref[...]
    bias = bias_ref[...].reshape(1, feat)
    scorer = scorer_ref[...].reshape(1, feat)
    rows_ref[0:kernel, :] = taps
    rows_ref[BIAS : BIAS + 1, :] = bias
    rows_ref[SCORER : SCORER + 1, :] = scorer
    rows_ref[SCORER + 1 : 8, :] = jnp.zeros((7 - SCORER, feat), f32)
    for tile in range(feat // LANES):
        at = slice(tile % 4 * 8, tile % 4 * 8 + 8)
        pack_ref[WEIGHTS + tile // 4, at, :] = rows_ref[:, tile * LANES : (tile + 1) * LANES]
    table_ref[...] = jnp.zeros_like(table_ref)

    def inner(a, b):
        return lax.dot_general(a, b, NT, preferred_element_type=f32)

    def products(tile):
        cols = pl.ds(pl.multiple_of(tile * LANES, LANES), LANES)
        taps = rows_ref[0:kernel, cols]
        scaled = jnp.concatenate(
            [taps * rows_ref[SCORER : SCORER + 1, cols], taps * rows_ref[BIAS : BIAS + 1, cols]], axis=0
        )
        scaled = in_two(scaled)
        high, low = split_ref[0, :, cols], split_ref[1, :, cols]
        ones = jnp.ones((8, LANES), jnp.bfloat16)
        some = embed_ref[:, cols]
        squares = in_two(some * some)
        table_ref[0:8, :] = table_ref[0:8, :] + (
            inner(scaled[0], high) + (inner(scaled[0], low) + inner(scaled[1], high))
        )
        table_ref[8:16, :] = table_ref[8:16, :] + (inner(ones, squares[0]) + inner(ones, squares[1]))

    chunk = 2 * LANES
    lines = chunk // vr

    def embedding(step):
        marks = []
        for i in range(chunk // LANES):
            column = step * (chunk // LANES) + i
            bytes_here = jnp.broadcast_to(line_ref[pl.ds(column, 1), :], (vocab, LANES))
            marks.append(jnp.where(bytes_here == iota((vocab, LANES), 0).astype(f32), 1.0, 0.0))
            line = column * group + iota((1, LANES), 1) // vr
            inside = ((line >= LEFT) & (line < LEFT + run)).astype(f32)
            seen_ref[...] = seen_ref[...] + marks[i] * inside
        marks = jnp.concatenate(marks, axis=1).astype(jnp.bfloat16)
        turn_ref[:, pl.ds(pl.multiple_of(step * chunk, chunk), chunk)] = marks
        total = lax.dot_general(marks, split_ref[0], TN, preferred_element_type=f32)
        total = total + lax.dot_general(marks, split_ref[1], TN, preferred_element_type=f32)
        emb_ref[pl.ds(step * lines, lines)] = total.reshape(lines, vr, feat)

    chunks, tiles = span // lines, feat // LANES
    trips = next(n for n in (1,) if chunks % n == 0 and tiles % n == 0)

    def some_chunks(trip, carry):
        for i in range(chunks // trips):
            embedding(trip * (chunks // trips) + i)
        for i in range(tiles // trips):
            products(trip * (tiles // trips) + i)
        return carry

    lax.fori_loop(0, trips, some_chunks, 0)
    for i in range(vocab // vr):
        seen = jnp.sum(seen_ref[i * vr : (i + 1) * vr, :], axis=1, keepdims=True)
        pack_ref[SEEN + i] = jnp.broadcast_to(seen, (vr, LANES))
    keeps = [
        pltpu.make_async_copy(turn_ref, mark_hbm, sems.at[1, 0]), pltpu.make_async_copy(emb_ref, emb_hbm, sems.at[1, 1])
    ]
    for copy in keeps:
        copy.start()

    size = RUNS * half
    order = iota((size, size), 0)
    order = (iota((size, size), 1) == order % RUNS * half + order // RUNS).astype(f32)
    order_ref[...] = order.astype(jnp.bfloat16)

    def convolution(step, carry):
        r, pair = step % rows, step // rows
        sub = pl.ds(pl.multiple_of(r * RUNS, RUNS), RUNS)
        length = len_ref[r]
        for tile in range(WIDE // LANES):
            cols = pl.ds(pl.multiple_of(pair * WIDE + tile * LANES, LANES), LANES)
            taps = [jnp.broadcast_to(rows_ref[k : k + 1, cols], (RUNS, LANES)) for k in range(kernel)]
            window = [emb_ref[k, sub, cols] for k in range(kernel - 1)]
            for j in range(-2, run + 2):
                window.append(emb_ref[j + LEFT, sub, cols])
                total = taps[0] * window[0]
                for k in range(1, kernel):
                    total = total + taps[k] * window[k]
                window = window[1:]
                real = base < length - j
                if j < 0:
                    real = real & (base >= -j)
                conv_ref[j + 2, sub, cols] = jnp.where(real, total, 0.0)
        return carry

    lax.fori_loop(0, rows * (feat // WIDE), convolution, 0)
    keeps.append(pltpu.make_async_copy(conv_ref, conv_hbm, sems.at[2, 0]))
    keeps[-1].start()

    block = 4
    slices = run + 4
    zero = jnp.zeros((RUNS, LANES), f32)
    def lagged(r, carry):
        at = pl.ds(pl.multiple_of(r * RUNS, RUNS), RUNS)
        some = grad_ref.at[pl.ds(pl.multiple_of(r * size, 8), size), :]
        for pair in range(feat // WIDE):
            wide = slice(pair * WIDE, (pair + 1) * WIDE)
            high, low = in_two(some[:, wide])
            moved = jnp.dot(order_ref[...], high, preferred_element_type=f32)
            moved = moved + jnp.dot(order_ref[...], low, preferred_element_type=f32)
            cot_ref[:, at, wide] = moved.reshape(half, RUNS, WIDE)
        values = [zero] * 6
        for first in range(0, slices, block):
            acc = {}
            for tile in range(feat // LANES):
                cols = slice(tile * LANES, (tile + 1) * LANES)
                u = [conv_ref[first + i, at, cols] for i in range(min(block + 5, slices - first))]
                for i in range(block):
                    for lag in range(min(6, slices - first - i)):
                        term = u[i] * u[i + lag]
                        acc[i, lag] = term if tile == 0 else acc[i, lag] + term
            for i, lag in acc:
                here = lane == first + (i + OFF - 2)
                values[lag] = jnp.where(here, jnp.sum(acc[i, lag], axis=1, keepdims=True), values[lag])
        for lag in range(6):
            pack_ref[lag, at, :] = values[lag]
        return carry

    fetch[6].wait()
    lax.fori_loop(0, rows, lagged, 0)
    keeps.append(pltpu.make_async_copy(cot_ref, cot_hbm, sems.at[3, 0]))
    keeps[-1].start()

    def total_of(x):
        return jnp.sum(jnp.sum(x, axis=1, keepdims=True), axis=0, keepdims=True)

    def lookups(r, sums):
        at = pl.ds(pl.multiple_of(r * RUNS, RUNS), RUNS)
        ids = pack_ref[IDS, at, :].astype(jnp.int32)
        real = ids >= 0
        low = jnp.where(real, ids, 0)

        def look(row):
            value = jnp.zeros((RUNS, LANES), f32)
            for part in range(vocab // LANES):
                entry = jnp.broadcast_to(
                    table_ref[row : row + 1, part * LANES : (part + 1) * LANES], (RUNS, LANES)
                )
                taken = jnp.take_along_axis(entry, low % LANES, axis=1)
                value = jnp.where(low // LANES == part, taken, value)
            return jnp.where(real, value, 0.0)

        scored = jnp.zeros((RUNS, LANES), f32)
        biased = jnp.zeros((RUNS, LANES), f32)
        for k in range(kernel):
            scored = scored + shifted(look(k), k - (kernel - 1))
            biased = biased + shifted(look(4 + k), k - (kernel - 1))
        inner_real = real & (lane >= OFF - 2)
        scored = jnp.where(inner_real, scored, 0.0)
        biased = jnp.where(inner_real, biased, 0.0)
        pack_ref[13, at, :] = scored
        pack_ref[14, at, :] = biased
        own = (real & (lane >= OFF) & (lane < OFF + run)).astype(f32)
        new = (own * look(8), own, own * biased, own * pack_ref[0, at, :], own * (1 - lane % 2).astype(f32))
        return tuple(a + b for a, b in zip(sums, new))

    def crossed(r, sums):
        at = pl.ds(pl.multiple_of(r * RUNS, RUNS), RUNS)
        sums = lookups(r, sums)
        values = [zero] * 7
        for first in range(0, half, block):
            acc = {}
            for tile in range(feat // LANES):
                cols = slice(tile * LANES, (tile + 1) * LANES)
                u = [conv_ref[2 * first + i, at, cols] for i in range(2 * block + 4)]
                bias = jnp.broadcast_to(rows_ref[BIAS : BIAS + 1, tile * LANES : (tile + 1) * LANES], (RUNS, LANES))
                for i in range(block):
                    g = cot_ref[first + i, at, cols]
                    terms = [g * u[2 * i + d] for d in range(6)] + [g * bias]
                    for d in range(7):
                        acc[i, d] = terms[d] if tile == 0 else acc[i, d] + terms[d]
            for i, d in acc:
                here = lane == 2 * first + (2 * i + OFF)
                values[d] = jnp.where(here, jnp.sum(acc[i, d], axis=1, keepdims=True), values[d])
        for d in range(7):
            pack_ref[6 + d, at, :] = values[d]
        return sums

    sums = lax.fori_loop(0, rows, crossed, (zero,) * 5)
    sums_ref[...] = spread([total_of(x) for x in sums], sums_ref.shape[0])
    for copy in keeps:
        copy.wait()


def in_two(x):
    high = x.astype(jnp.bfloat16)
    return high, (x - high.astype(f32)).astype(jnp.bfloat16)


def unpack_rows(pack_ref, rows_ref):
    for tile in range(rows_ref.shape[1] // LANES):
        at = slice(tile % 4 * 8, tile % 4 * 8 + 8)
        rows_ref[:, tile * LANES : (tile + 1) * LANES] = pack_ref[WEIGHTS + tile // 4, at, :]


def spread(sums, count):
    lane = iota((1, LANES), 1)
    row = jnp.zeros((1, LANES), f32)
    for i, x in enumerate(sums):
        row = jnp.where(lane == i, x, row)
    return jnp.broadcast_to(row[None], (count, 1, LANES))


def picked(ref, number):
    row = jnp.sum(ref[...], axis=0)
    return [row[:, i : i + 1] for i in range(number)]


def scales(first_ref, bias, feat):
    emb_sum, count, cross, square, count4 = picked(first_ref, 5)
    one = jnp.sqrt(emb_sum / (count * feat) + EPS)
    bias_sum = jnp.sum(bias * bias, axis=1, keepdims=True)
    conv_sum = jnp.maximum(count * bias_sum + 2.0 * cross / one + square / (one * one), 0.0)
    two = jnp.sqrt(conv_sum / (count * feat) + EPS)
    return one, two, count, count4, bias_sum, cross


class Places:
    def __init__(self, ids, start, run):
        shape = ids.shape
        self.j = iota(shape, 1) - OFF
        sub = iota(shape, 0) % RUNS
        self.inside = (self.j >= 0) & (self.j < run)
        self.real = ((ids >= 0) & (self.j >= -2)).astype(f32)
        self.own = jnp.where(self.inside, self.real, 0.0)
        shown = self.j + OFF
        self.two, self.four = shown % 2, shown % 4
        self.three = (start + run * sub + shown + (3 * OFF - OFF)) % 3

    def holds(self, size, by):
        if size == 1:
            return jnp.ones_like(self.real) if by == 0 else None
        if abs(by) >= size:
            return None
        phase = {2: self.two, 3: self.three, 4: self.four}[size]
        return ((phase + by >= 0) & (phase + by < size)).astype(f32)

    def pooled(self, size, x):
        if size == 1:
            return x
        pair = x + jnp.where(self.two == 0, shifted(x, 1), shifted(x, -1))
        if size == 2:
            return pair
        if size == 4:
            return pair + jnp.where(self.four < 2, shifted(pair, 2), shifted(pair, -2))
        left, right = shifted(x, -1), shifted(x, 1)
        side = jnp.where(self.three == 0, shifted(x, 2), left)
        far = jnp.where(self.three == 2, shifted(x, -2), right)
        return x + side + far

    def both(self, x):
        return x + shifted(x, -1)


SIZES = (1, 2, 3, 4)
REACH = range(-3, 4)


def score_kernel(sizes, first_ref, dots_ref, state_ref, sums_ref, rows_ref):
    rows, width, run, feat, vocab, kernel = sizes
    start = lax.axis_index("seq") * width
    unpack_rows(dots_ref, rows_ref)
    bias = rows_ref[BIAS : BIAS + 1, :]
    one, two, count, count4, bias_sum, cross = scales(first_ref, bias, feat)
    at = Places(dots_ref[IDS], start, run)
    real, own = at.real, at.own
    rate = 1.0 / (one * two)
    bias_score = jnp.sum(bias * rows_ref[SCORER : SCORER + 1, :], axis=1, keepdims=True) / two

    normed_score = real * bias_score + rate * dots_ref[13]
    counts = [jnp.maximum(at.pooled(b, real), 1.0) for b in SIZES]
    scores = [at.pooled(b, normed_score) / n for b, n in zip(SIZES, counts)]
    top = functools.reduce(jnp.maximum, scores)
    parts = [jnp.exp(s - top) for s in scores]
    whole = sum(parts)
    probs = [p / whole for p in parts]
    weights = [own * p / n for p, n in zip(probs, counts)]

    holds = {(b, d): at.holds(b, d) for b in SIZES for d in REACH}

    def blend(values):
        out = {}
        for d in REACH:
            terms = [v * holds[b, d] for b, v in zip(SIZES, values) if holds[b, d] is not None]
            out[d] = sum(terms)
        return out

    mixer = blend(weights)
    pair_count = jnp.maximum(at.pooled(2, real), 1.0)
    halver = {}
    even = at.two == 0
    for d in REACH:
        zero = jnp.zeros_like(real)
        ahead = shifted(mixer[d - 1], 1) if d - 1 >= -3 else zero
        behind = shifted(mixer[d + 1], -1) if d + 1 <= 3 else zero
        other = jnp.where(even, ahead, behind)
        halver[d] = jnp.where(at.inside, (mixer[d] + other) / pair_count, 0.0)

    bias_dot = dots_ref[14]
    normed_bias = real * (bias_sum / two) + rate * bias_dot
    lags = []
    for lag in range(6):
        later = shifted(real, lag)
        value = rate * rate * dots_ref[lag]
        value = value + (rate / two) * (bias_dot * later + real * shifted(bias_dot, lag))
        lags.append(value + (bias_sum / (two * two)) * (real * later))

    def gram(a, b):
        low, high = min(a, b), max(a, b)
        return shifted(lags[high - low], low) if high - low < 6 else None

    table = {(a, b): gram(a, b) for a in REACH for b in REACH if a <= b}

    def against(weighting):
        out = {}
        for a in REACH:
            out[a] = sum(
                weighting[b] * table[min(a, b), max(a, b)]
                for b in REACH if table[min(a, b), max(a, b)] is not None
            )
        return out

    with_mixed, with_half = against(mixer), against(halver)
    with_grad = {}
    grad_bias = dots_ref[12]
    cross_dots = {
        d: rate * dots_ref[6 + d + 2] + shifted(real, d) * (grad_bias / two) for d in range(-2, 4)
    }
    for d in REACH:
        here = cross_dots[d] if d >= -2 else jnp.zeros_like(real)
        before = shifted(cross_dots[d + 1], -1) if d + 1 <= 3 else jnp.zeros_like(real)
        with_grad[d] = jnp.where(even, here, before)

    def per_block(values, scale):
        out = []
        for b, n in zip(SIZES, counts):
            terms = [values[d] * holds[b, d] for d in REACH if holds[b, d] is not None]
            out.append(scale * sum(terms) / n)
        return out

    shared = own / pair_count
    bases = [per_block(with_grad, shared), per_block(with_half, shared), per_block(with_mixed, own)]

    def total_of(x):
        return jnp.sum(jnp.sum(x, axis=1, keepdims=True), axis=0, keepdims=True)

    first_of_pair = jnp.where(even & at.inside, 1.0, 0.0)
    mean_score = sum(p * s for p, s in zip(probs, scores))

    def bent(values):
        mean = sum(p * v for p, v in zip(probs, values))
        return total_of(own * (sum(p * s * v for p, s, v in zip(probs, scores, values)) - mean * mean_score))

    sums = [
        total_of(sum(own * mixer[d] * with_mixed[d] for d in REACH)),
        total_of(first_of_pair * sum(halver[d] * with_half[d] for d in REACH)),
        total_of(first_of_pair * sum(halver[d] * with_grad[d] for d in REACH)),
        bent(bases[0]), bent(bases[1]), bent(bases[2]),
        total_of(shared * at.both(grad_bias)),
        total_of(shared * sum(halver[d] * shifted(normed_bias, d) for d in REACH)),
        total_of(own * sum(mixer[d] * shifted(normed_bias, d) for d in REACH)),
    ]
    for i, b in enumerate(SIZES):
        state_ref[i] = weights[i]
        state_ref[4 + i] = probs[i]
        for f in range(3):
            state_ref[8 + 4 * f + i] = bases[f][i]
    sums_ref[...] = spread(sums, sums_ref.shape[0])


def back_kernel(
    sizes, first_hbm, second_hbm, pack_hbm, state_hbm, mark_hbm, embed_hbm, conv_hbm, emb_hbm, cot_hbm,
    out_hbm, keep_ref, send_ref,
    first_ref, second_ref, pack_ref, state_ref, mark_ref, embed_ref, rows_ref, turn_ref, out_ref, order_ref,
    narrow_ref, acc_ref, pay_ref, conv_ref, emb_ref, cot_ref, back_ref, sems,
):
    rows, width, run, feat, vocab, kernel = sizes
    tiles = feat // LANES
    per = WIDE // LANES
    units = rows * (feat // WIDE)
    half = run // 2
    vr = rows * RUNS

    def fetches(unit):
        sub = pl.ds(pl.multiple_of(unit % rows * RUNS, RUNS), RUNS)
        cols = pl.ds(pl.multiple_of(unit // rows * WIDE, LANES), WIDE)
        return [
            pltpu.make_async_copy(a.at[:, sub, cols], b.at[:, sub, cols], sems.at[i, unit])
            for i, (a, b) in enumerate(((conv_hbm, conv_ref), (cot_hbm, cot_ref), (emb_hbm, emb_ref)))
        ]

    size = RUNS * half

    def stored(unit):
        some = pl.ds(pl.multiple_of(unit % rows * size, 8), size)
        cols = pl.ds(pl.multiple_of(unit // rows * WIDE, LANES), WIDE)
        return pltpu.make_async_copy(out_ref.at[some, cols], out_hbm.at[some, cols], sems.at[3, unit])

    def restore(unit):
        some = pl.ds(pl.multiple_of(unit % rows * size, 8), size)
        cols = pl.ds(pl.multiple_of(unit // rows * WIDE, LANES), WIDE)
        high, low = in_two(turn_ref[...].reshape(size, WIDE))
        moved = jnp.dot(order_ref[...], high, preferred_element_type=f32)
        out_ref[some, cols] = moved + jnp.dot(order_ref[...], low, preferred_element_type=f32)

    sources = (first_hbm, second_hbm, pack_hbm, state_hbm, mark_hbm, embed_hbm)
    targets = (first_ref, second_ref, pack_ref, state_ref, mark_ref, embed_ref)
    small = [pltpu.make_async_copy(a, b, sems.at[4, i]) for i, (a, b) in enumerate(zip(sources, targets))]
    small[2] = pltpu.make_async_copy(pack_hbm.at[IDS:], pack_ref.at[IDS:], sems.at[4, 2])
    ahead = 3
    for copy in small[:4]:
        copy.start()
    for unit in range(ahead):
        for copy in fetches(unit):
            copy.start()
    for copy in small[4:]:
        copy.start()
    for copy in small[:4]:
        copy.wait()

    start = lax.axis_index("seq") * width
    unpack_rows(pack_ref, rows_ref)
    bias = rows_ref[BIAS : BIAS + 1, :]
    one, two, count, count4, bias_sum, cross = scales(first_ref, bias, feat)
    mixed_sum, half_sum, inner, bent_g, bent_h, bent_m, bias_g, bias_h, bias_m = picked(second_ref, 9)
    volume, volume4 = count * feat, count4 * feat
    three = jnp.sqrt(mixed_sum / volume + EPS)
    four = jnp.sqrt(half_sum / (three * three) / volume4 + EPS)
    fourth = (inner / three) / (four * four * four * volume4)
    alpha = 1.0 / (three * four)
    beta = -fourth / (three * three)
    gamma = -(inner / four - fourth / three * half_sum) / (three * three * three * volume)
    joint = alpha * (inner + bent_g) + beta * (half_sum + bent_h) + gamma * (mixed_sum + bent_m)
    rate = 1.0 / (one * two)
    normed_bias = count * bias_sum / two + rate * cross
    bias_back = (alpha * bias_g + beta * bias_h + gamma * bias_m - joint / volume * normed_bias) / two
    inner_one = one * (joint * EPS / (two * two) - bias_back)
    first_coef = inner_one / (one * one * one * volume)

    at = Places(pack_ref[IDS], start, run)
    probs = [state_ref[4 + i] for i in range(4)]
    weights = [state_ref[i] for i in range(4)]
    grads = [
        alpha * state_ref[8 + i] + beta * state_ref[12 + i] + gamma * state_ref[16 + i] for i in range(4)
    ]
    mean = sum(p * g for p, g in zip(probs, grads))
    spreading = jnp.zeros_like(probs[0])
    for i, b in enumerate(SIZES):
        bent = probs[i] * (grads[i] - mean)
        n = jnp.maximum(at.pooled(b, at.real), 1.0)
        spreading = spreading + at.pooled(b, jnp.where(at.inside, bent / n, 0.0))
    pair_real = at.pooled(2, at.real)
    pair_count = jnp.maximum(pair_real, 1.0)
    filled = (pair_real > 0).astype(f32)
    narrow = [rate * w for w in weights] + [rate * spreading, at.real]
    paired = [
        alpha / pair_count, alpha * filled, beta / (pair_count * pair_count), beta * filled / pair_count + gamma
    ]
    leak = jnp.sum(jnp.sum(spreading * at.real, axis=1, keepdims=True), axis=0, keepdims=True)

    for i, x in enumerate(narrow + paired):
        narrow_ref[i] = x
    order = iota((size, size), 0)
    order = (iota((size, size), 1) == order % half * RUNS + order // half).astype(f32)
    order_ref[...] = order.astype(jnp.bfloat16)
    turn_ref[...] = jnp.zeros_like(turn_ref)
    acc_ref[...] = jnp.zeros_like(acc_ref)
    phase = (start + run * iota((RUNS, LANES), 0)) % 3
    at_phase = [phase == p for p in range(3)]

    def chosen(j, a, b, c):
        return jnp.where(at_phase[(0 - j) % 3], a, jnp.where(at_phase[(1 - j) % 3], b, c))

    full = (RUNS, LANES)
    alpha_all = jnp.broadcast_to(alpha, full)
    gamma_all = jnp.broadcast_to(gamma, full)
    fall = jnp.broadcast_to(rate * rate * joint / volume, full)
    fall_bias = rate * joint / volume / two

    def column(r, tile, near, factor):
        sub = pl.ds(pl.multiple_of(r * RUNS, RUNS), RUNS)
        cols = pl.ds(pl.multiple_of(tile * LANES, LANES), LANES)
        taps = [jnp.broadcast_to(rows_ref[k : k + 1, cols], full) for k in range(kernel)]
        bias_row = rows_ref[BIAS : BIAS + 1, cols]
        normed_row = jnp.broadcast_to(bias_row / two, full)
        fall_row = jnp.broadcast_to(bias_row * fall_bias, full)
        scorer = jnp.broadcast_to(rows_ref[SCORER : SCORER + 1, cols], full)
        zero = jnp.zeros(full, f32)

        u, triple, y3, gc = {}, {}, {}, {}
        sums = [zero] * (kernel + 2)
        block = {}
        twos, y_twos = {}, {}
        for j in range(-2, 2):
            u[j] = conv_ref[j + 2, sub, cols]

        def pair_of(j):
            if j not in twos:
                twos[j] = u[j] + u[j + 1]
            return twos[j]

        triple[-2] = pair_of(-2) + u[0]
        triple[-1] = u[-1] + pair_of(0)

        def window(j):
            if 0 <= j <= run - 3:
                first = j if j % 2 == 0 else j + 1
                if first not in y_twos:
                    y_twos[first] = y3[first] + y3[first + 1]
                return y_twos[first] + y3[j + 2 if j % 2 == 0 else j]
            near = [y3[i] for i in (j, j + 1, j + 2) if 0 <= i < run]
            return functools.reduce(lambda a, b: a + b, near) if near else zero

        def settle(s):
            nonlocal sums
            for j in (s, s - 1, s - 2):
                if j not in block:
                    block[j] = window(j)
            g = chosen(s, block[s], block[s - 1], block[s - 2])
            sigma = factor(4, s)
            g = g + sigma * scorer
            if 0 <= s < run:
                g = g + lone[s]
                g = g - fall * u[s]
            g = g * factor(5, s)
            gc[s] = g
            for k in range(kernel):
                sums[k] = sums[k] + g * emb_ref[s - kernel + 1 + k + LEFT, sub, cols]
            sums[kernel] = sums[kernel] + g
            sums[kernel + 1] = sums[kernel + 1] + sigma * u[s]

        def finish(s):
            terms = [taps[k] * gc[s + kernel - 1 - k] for k in range(kernel) if s + kernel - 1 - k in gc]
            back_ref[s + LEFT, sub, cols] = functools.reduce(lambda a, b: a + b, terms)

        lone = {}
        settled = -2
        finished = -LEFT
        for quad in range(0, run, 4):
            for j in range(quad + 2, quad + 6):
                u[j] = conv_ref[j + 2, sub, cols]
            two_sums = [pair_of(quad), pair_of(quad + 2)]
            four_sum = two_sums[0] + two_sums[1]
            shares = []
            wide = zero
            for p in range(2):
                y = None
                xs = []
                for j in (quad + 2 * p, quad + 2 * p + 1):
                    triple[j] = u[j] + pair_of(j + 1) if j % 2 else two_sums[p] + u[j + 2]
                    x = factor(0, j) * u[j] + factor(1, j) * two_sums[p]
                    x = x + factor(2, j) * chosen(j, triple[j], triple[j - 1], triple[j - 2])
                    x = x + factor(3, j) * four_sum
                    xs.append(x)
                y = xs[0] + xs[1]
                k = quad // 2 + p
                scale_y = factor(6, 2 * k)
                turn_ref[k, :, near] = scale_y * y + factor(7, 2 * k) * normed_row
                q = scale_y * cot_ref[k, sub, cols] + factor(8, 2 * k) * y + factor(9, 2 * k) * normed_row
                pair = zero
                for i, j in enumerate((quad + 2 * p, quad + 2 * p + 1)):
                    g = q + gamma_all * xs[i]
                    lone[j] = factor(0, j) * g
                    y3[j] = factor(2, j) * g
                    pair = factor(1, j) * g if i == 0 else pair + factor(1, j) * g
                    wide = factor(3, j) * g if i + p == 0 else wide + factor(3, j) * g
                shares.append(pair)
            wide = wide - fall_row
            for p in range(2):
                share = shares[p] + wide
                for j in (quad + 2 * p, quad + 2 * p + 1):
                    lone[j] = lone[j] + share
            last = quad + 3 - 2 if quad + 4 < run else run + 1
            while settled <= last:
                settle(settled)
                settled += 1
            done = settled - kernel if quad + 4 < run else run + RIGHT - 1
            while finished <= done:
                finish(finished)
                finished += 1
            yield
        for i in range(kernel + 2):
            acc_ref[i, :, cols] = acc_ref[i, :, cols] + sums[i]

    def some_columns(unit, carry):
        for copy in fetches(unit):
            copy.wait()

        @pl.when(unit + ahead < units)
        def _():
            for copy in fetches(unit + ahead):
                copy.start()

        r = unit % rows
        made = {}

        def factor(i, j):
            if (i, j) not in made:
                sub = pl.ds(pl.multiple_of(r * RUNS, RUNS), RUNS)
                made[i, j] = jnp.broadcast_to(narrow_ref[i, sub, j + OFF : j + OFF + 1], full)
            return made[i, j]

        last = jnp.maximum(unit - 1, 0)
        restore(last)
        parts = []
        for i in range(per):
            near = slice(i * LANES, (i + 1) * LANES)
            parts.append(column(r, unit // rows * per + i, near, factor))
        for _ in zip(*parts, strict=True):
            pass

        @pl.when(unit > 0)
        def _():
            stored(last).start()

        return carry

    lax.fori_loop(0, units, some_columns, 0)
    restore(units - 1)
    stored(units - 1).start()

    positions = mark_ref.shape[1]
    edge = run + LEFT + RIGHT
    back_ref[edge:] = jnp.zeros((back_ref.shape[0] - edge, vr, feat), f32)
    for copy in small[4:]:
        copy.wait()
    total_tiles = pay_ref.shape[0]

    def gather(pair, carry):
        cols = pl.ds(pl.multiple_of(pair * WIDE, LANES), WIDE)
        high, low = in_two(back_ref[:, :, cols].reshape(positions, WIDE))
        total = jnp.dot(mark_ref[...], high, preferred_element_type=f32)
        total = total + jnp.dot(mark_ref[...], low, preferred_element_type=f32)
        for v in range(vocab // 8):
            seen = first_coef * pack_ref[SEEN + v * 8 // vr, v * 8 % vr : v * 8 % vr + 8, :]
            for i in range(per):
                wide = pl.ds(pl.multiple_of(pair * WIDE + i * LANES, LANES), LANES)
                part = total[v * 8 : v * 8 + 8, i * LANES : (i + 1) * LANES]
                pay_ref[v * tiles + pair * per + i] = part - seen * embed_ref[v * 8 : v * 8 + 8, wide]
        return carry

    for pair in range(feat // WIDE):
        gather(pair, 0)

    end = vocab // 8 * tiles
    pay_ref[end:] = jnp.zeros((total_tiles - end, 8, LANES), f32)
    for i in range(kernel + 2):
        row = jnp.sum(acc_ref[i], axis=0, keepdims=True)
        if i == kernel:
            row = row * one
        if i == kernel + 1:
            row = row + bias * (leak / two)
        for tile in range(tiles):
            place = i * tiles + tile
            pay_ref[end + place // 8, place % 8 : place % 8 + 1, :] = row[:, tile * LANES : (tile + 1) * LANES]
    core = lax.axis_index("seq") % 2
    part = total_tiles // 2
    keep_ref[...] = pay_ref[pl.ds(core * part, part)]
    send_ref[...] = pay_ref[pl.ds((1 - core) * part, part)]
    for unit in range(units):
        stored(unit).wait()


def finish_kernel(feat, mine_ref, other_ref, table_hbm, taps_ref, bias_ref, scorer_ref, sems):
    core = lax.axis_index("seq") % 2
    tiles = feat // LANES
    part = mine_ref.shape[0]
    rest = table_hbm.shape[0] - part
    for side in range(2):

        @pl.when(core == side)
        def _():
            first, second = (mine_ref, other_ref) if side == 0 else (other_ref, mine_ref)
            copies = (
                pltpu.make_async_copy(first, table_hbm.at[0:part], sems.at[0]),
                pltpu.make_async_copy(second.at[0:rest], table_hbm.at[part : part + rest], sems.at[1]),
            )
            for copy in copies:
                copy.start()
            lines = []
            for i in range(taps_ref.shape[0] + 2):
                places = [i * tiles + tile for tile in range(tiles)]
                lines.append([second[rest + p // 8, p % 8 : p % 8 + 1, :] for p in places])
            for i in range(taps_ref.shape[0]):
                taps_ref[i : i + 1, :] = jnp.concatenate(lines[i], axis=1)
            bias_ref[...] = jnp.concatenate(lines[-2], axis=1).reshape(feat)
            scorer_ref[...] = jnp.concatenate(lines[-1], axis=1).reshape(feat)
            for copy in copies:
                copy.wait()


def exchanged(x):
    return lax.all_to_all(x, AXES, 0, 0, tiled=True)


def partner(x, axis, step):
    n = lax.axis_size(axis)
    return lax.ppermute(x, axis, [(i, i ^ step) for i in range(n)])


def summed_over_devices(keep, send):
    n = lax.axis_size("seq")
    others = lax.axis_size("rows") * n // 2
    groups = [[2 * i + side for i in range(others)] for side in range(2)]

    def traded(x):
        return lax.all_to_all(x, AXES, 0, 0, tiled=True, axis_index_groups=groups)

    x = keep + partner(send, "seq", 1)
    chunk = (others, x.shape[0] * x.shape[1] // others, 1, LANES)
    part = jnp.sum(traded(x.reshape(chunk)), axis=0)
    x = traded(jnp.broadcast_to(part[None], chunk)).reshape(x.shape)
    return x, partner(x, "seq", 1)


def on_device(byte_ids, lengths, embed, conv_weight, conv_bias, score_weight, out_grad):
    rows, width = byte_ids.shape
    vocab, feat = embed.shape
    kernel = conv_weight.shape[0]
    run = width // RUNS
    half = width // 2
    vr = rows * RUNS
    sizes = (rows, width, run, feat, vocab, kernel)
    count = lax.axis_size("seq")
    devices = count * lax.axis_size("rows")
    span = -(-(run + LEFT + RIGHT) // 8) * 8
    tiles = feat // LANES
    struct = jax.ShapeDtypeStruct
    sem = pltpu.SemaphoreType.DMA

    params = pltpu.CompilerParams(vmem_limit_bytes=60 * 1024 * 1024)

    pairs_of = [[(i, i + 1) for i in range(first, count - 1, 2)] for first in range(2)]
    near = [lax.ppermute(byte_ids, "seq", some + [(j, i) for i, j in some]) for some in pairs_of]
    near = [pltpu.with_memory_space_constraint(x, pltpu.VMEM) for x in near]

    pairs = feat // WIDE
    bf16 = jnp.bfloat16
    wide_emb = struct((span, vr, feat), f32)
    wide_conv = struct((run + 4, vr, feat), f32)
    wide_cot = struct((half // RUNS, vr, feat), f32)
    marks = struct((vocab, span * vr), bf16)
    pack = struct((SEEN + vocab // vr, vr, LANES), f32)
    sums = struct((devices, 1, LANES), f32)
    state = struct((20, vr, LANES), f32)

    def scratch(like):
        return pltpu.VMEM(like.shape, like.dtype)

    emb, conv, cot, mark, packed, first = pl.pallas_call(
        functools.partial(stats_kernel, sizes),
        out_shape=(*(pltpu.HBM(x.shape, x.dtype) for x in (wide_emb, wide_conv, wide_cot, marks, pack)), pltpu.VMEM(sums.shape, f32)),
        in_specs=[HBM, VMEM, VMEM] + [HBM] * 6, out_specs=(HBM,) * 4 + (VMEM,) * 2,
        scratch_shapes=[
            scratch(byte_ids), pltpu.SMEM((rows,), jnp.int32), scratch(embed),
            scratch(conv_weight), scratch(conv_bias), scratch(score_weight), pltpu.VMEM((rows * half, feat), f32),
            pltpu.VMEM((2, vocab, feat), bf16), pltpu.VMEM((16, vocab), f32), pltpu.VMEM((8, feat), f32),
            scratch(marks), pltpu.VMEM((-(-span * vr // LANES // 8) * 8, LANES), f32), pltpu.VMEM((vocab, LANES), f32),
            pltpu.VMEM((half, half), bf16), pltpu.VMEM((vr, LANES), jnp.int32), scratch(wide_emb),
            scratch(wide_conv), scratch(wide_cot), sem((4, 9)),
        ],
        compiler_params=params, name="stats",
    )(
        byte_ids, *near, lengths, embed, conv_weight, conv_bias, score_weight,
        out_grad.reshape(rows * half, feat),
    )
    first = exchanged(first)

    states, second = pl.pallas_call(
        functools.partial(score_kernel, sizes),
        out_shape=(pltpu.HBM(state.shape, f32), pltpu.VMEM(sums.shape, f32)),
        in_specs=[VMEM] * 2, out_specs=(VMEM, VMEM), scratch_shapes=[pltpu.VMEM((8, feat), f32)],
        compiler_params=params, name="score",
    )(first, packed)
    second = exchanged(second)

    lines = vocab * tiles
    lines = -(-(lines + (kernel + 2) * tiles) // devices) * devices
    parts = struct((lines // 16, 8, LANES), f32)
    blocks, keep, send = pl.pallas_call(
        functools.partial(back_kernel, sizes),
        out_shape=(pltpu.HBM((rows * half, feat), f32), pltpu.VMEM(parts.shape, f32), pltpu.VMEM(parts.shape, f32)),
        in_specs=[HBM] * 9, out_specs=(HBM, VMEM, VMEM),
        scratch_shapes=[
            scratch(sums), scratch(sums), scratch(pack), scratch(state), scratch(marks), scratch(embed),
            pltpu.VMEM((8, feat), f32), pltpu.VMEM((half // RUNS, RUNS, WIDE), f32),
            pltpu.VMEM((rows * half, feat), f32), pltpu.VMEM((half, half), bf16), pltpu.VMEM((10, vr, LANES), f32),
            pltpu.VMEM((kernel + 2, RUNS, feat), f32), pltpu.VMEM((lines // 8, 8, LANES), f32),
            scratch(wide_conv), scratch(wide_emb), scratch(wide_cot), scratch(wide_emb),
            sem((5, max(6, rows * pairs))),
        ],
        compiler_params=params, name="back",
    )(first, second, packed, states, mark, embed, conv, emb, cot)

    mine, other = summed_over_devices(keep, send)
    table, taps_grad, bias_grad, scorer_grad = pl.pallas_call(
        functools.partial(finish_kernel, feat),
        out_shape=(
            pltpu.HBM((vocab * tiles // 8, 8, LANES), f32), struct((kernel, feat), f32), struct((feat,), f32),
            struct((feat,), f32),
        ),
        in_specs=[VMEM, VMEM], out_specs=(HBM, VMEM, VMEM, VMEM), scratch_shapes=[sem((2,))],
        compiler_params=pltpu.CompilerParams(vmem_limit_bytes=8 * 1024 * 1024), name="finish",
    )(mine, other)
    table = table.reshape(vocab // 8, tiles, 8, LANES).transpose(0, 2, 1, 3).reshape(vocab, feat)
    return blocks.reshape(rows, half, feat), table, taps_grad, bias_grad, scorer_grad


def solution(mesh):
    placed = (P("rows", "seq"), P("rows"), P(), P(), P(), P(), P("rows", "seq", None))
    return jax.shard_map(
        on_device,
        mesh=mesh,
        in_specs=placed,
        out_specs=(P("rows", "seq", None), P(), P(), P(), P()),
        check_vma=False,
    )
```

```python
import functools

import jax
import jax.numpy as jnp
from jax import lax
from jax.experimental import pallas as pl
from jax.experimental.pallas import tpu as pltpu
from jax.sharding import PartitionSpec as P

f32 = jnp.float32
EPS = 1e-06
LANES = 128
WIDE = 256
RUNS = 8
OFF = 8
LEFT, RIGHT = 5, 2
NT = (((1,), (1,)), ((), ()))
TN = (((0,), (0,)), ((), ()))
AXES = ("rows", "seq")
VMEM = pl.BlockSpec(memory_space=pltpu.VMEM)
HBM = pl.BlockSpec(memory_space=pltpu.HBM)


def iota(shape, dim):
    return lax.broadcasted_iota(jnp.int32, shape, dim)


def shifted(x, by):
    return x if by == 0 else pltpu.roll(x, (-by) % LANES, 1)


BIAS, SCORER = 4, 5
IDS, WEIGHTS, SEEN = 15, 16, 18


def stats_kernel(
    sizes, own_hbm, even_ref, odd_ref, len_hbm, embed_hbm, taps_hbm, bias_hbm, scorer_hbm, grad_hbm,
    emb_hbm, conv_hbm, cot_hbm, mark_hbm, pack_ref, sums_ref,
    own_ref, len_ref, embed_ref, taps_ref, bias_ref, scorer_ref, grad_ref,
    split_ref, table_ref, rows_ref, turn_ref, line_ref, seen_ref, order_ref, run_ref, emb_ref, conv_ref, cot_ref, sems,
):
    rows, width, run, feat, vocab, kernel = sizes
    half = run // 2
    vr = rows * RUNS
    span = emb_ref.shape[0]
    sources = (own_hbm, len_hbm, embed_hbm, taps_hbm, bias_hbm, scorer_hbm, grad_hbm)
    targets = (own_ref, len_ref, embed_ref, taps_ref, bias_ref, scorer_ref, grad_ref)
    fetch = [pltpu.make_async_copy(a, b, sems.at[0, i]) for i, (a, b) in enumerate(zip(sources, targets))]
    for copy in fetch:
        copy.start()
    start = lax.axis_index("seq") * width
    lane = iota((RUNS, LANES), 1)
    sub = iota((RUNS, LANES), 0)
    base = start + run * sub
    back = (OFF - run) % LANES

    for copy in fetch[:2]:
        copy.wait()
    for r in range(rows):
        for s in range(RUNS):
            line = own_ref[r : r + 1, s * run // LANES * LANES : (s * run // LANES + 1) * LANES]
            shift = -(s * run % LANES) % LANES
            line = jnp.broadcast_to(line, (RUNS, LANES))
            line = pltpu.roll(line, shift, 1) if shift else line
            run_ref[r * RUNS + s : r * RUNS + s + 1, :] = line[0:1]
    odd = lax.axis_index("seq") % 2 == 1
    for r in range(rows):
        own = run_ref[r * RUNS : (r + 1) * RUNS, :]
        tail = slice(width - LANES, width)
        left = jnp.where(odd, even_ref[r : r + 1, tail], odd_ref[r : r + 1, tail])
        right = jnp.where(odd, odd_ref[r : r + 1, 0:LANES], even_ref[r : r + 1, 0:LANES])
        before = pltpu.roll(pltpu.roll(own, 1, 0), back, 1)
        edge = pltpu.roll(jnp.broadcast_to(left, (RUNS, LANES)), OFF, 1)
        before = jnp.where(sub == 0, edge, before)
        after = pltpu.roll(pltpu.roll(own, RUNS - 1, 0), OFF + run, 1)
        edge = pltpu.roll(jnp.broadcast_to(right, (RUNS, LANES)), OFF + run, 1)
        after = jnp.where(sub == RUNS - 1, edge, after)
        ids = jnp.where(lane < OFF, before, jnp.where(lane < OFF + run, pltpu.roll(own, OFF, 1), after))
        place = base + lane - OFF
        real = (place >= 0) & (place < len_ref[r])
        real = real & (lane >= OFF - LEFT) & (lane < OFF + run + RIGHT)
        pack_ref[IDS, r * RUNS : (r + 1) * RUNS, :] = jnp.where(real, ids, -1).astype(f32)

    group = LANES // (rows * RUNS)
    ids = pack_ref[IDS].astype(jnp.bfloat16)
    eye = (iota((LANES, LANES), 0) == iota((LANES, LANES), 1)).astype(f32).astype(jnp.bfloat16)
    turned = lax.dot_general(eye, ids, NT, preferred_element_type=f32).astype(jnp.bfloat16)
    lined = jnp.zeros((line_ref.shape[0], LANES), f32)
    for i in range(group):
        shape = (line_ref.shape[0], LANES)
        take = (iota(shape, 1) == iota(shape, 0) * group + (i + OFF - LEFT)).astype(f32).astype(jnp.bfloat16)
        put = (iota((vr, LANES), 1) == iota((vr, LANES), 0) + i * vr).astype(f32).astype(jnp.bfloat16)
        some = jnp.dot(take, turned, preferred_element_type=f32).astype(jnp.bfloat16)
        lined = lined + jnp.dot(some, put, preferred_element_type=f32)
    line_ref[...] = lined

    seen_ref[...] = jnp.zeros_like(seen_ref)
    for copy in fetch[2:6]:
        copy.wait()
    embed = embed_ref[...]
    high, low = in_two(embed)
    split_ref[0] = high
    split_ref[1] = low

    taps = taps_ref[...]
    bias = bias_ref[...].reshape(1, feat)
    scorer = scorer_ref[...].reshape(1, feat)
    rows_ref[0:kernel, :] = taps
    rows_ref[BIAS : BIAS + 1, :] = bias
    rows_ref[SCORER : SCORER + 1, :] = scorer
    rows_ref[SCORER + 1 : 8, :] = jnp.zeros((7 - SCORER, feat), f32)
    for tile in range(feat // LANES):
        at = slice(tile % 4 * 8, tile % 4 * 8 + 8)
        pack_ref[WEIGHTS + tile // 4, at, :] = rows_ref[:, tile * LANES : (tile + 1) * LANES]
    table_ref[...] = jnp.zeros_like(table_ref)

    def inner(a, b):
        return lax.dot_general(a, b, NT, preferred_element_type=f32)

    def products(tile):
        cols = pl.ds(pl.multiple_of(tile * LANES, LANES), LANES)
        taps = rows_ref[0:kernel, cols]
        scaled = jnp.concatenate(
            [taps * rows_ref[SCORER : SCORER + 1, cols], taps * rows_ref[BIAS : BIAS + 1, cols]], axis=0
        )
        scaled = in_two(scaled)
        high, low = split_ref[0, :, cols], split_ref[1, :, cols]
        ones = jnp.ones((8, LANES), jnp.bfloat16)
        some = embed_ref[:, cols]
        squares = in_two(some * some)
        table_ref[0:8, :] = table_ref[0:8, :] + (
            inner(scaled[0], high) + (inner(scaled[0], low) + inner(scaled[1], high))
        )
        table_ref[8:16, :] = table_ref[8:16, :] + (inner(ones, squares[0]) + inner(ones, squares[1]))

    chunk = 2 * LANES
    lines = chunk // vr

    def embedding(step):
        marks = []
        for i in range(chunk // LANES):
            column = step * (chunk // LANES) + i
            bytes_here = jnp.broadcast_to(line_ref[pl.ds(column, 1), :], (vocab, LANES))
            marks.append(jnp.where(bytes_here == iota((vocab, LANES), 0).astype(f32), 1.0, 0.0))
            line = column * group + iota((1, LANES), 1) // vr
            inside = ((line >= LEFT) & (line < LEFT + run)).astype(f32)
            seen_ref[...] = seen_ref[...] + marks[i] * inside
        marks = jnp.concatenate(marks, axis=1).astype(jnp.bfloat16)
        turn_ref[:, pl.ds(pl.multiple_of(step * chunk, chunk), chunk)] = marks
        total = lax.dot_general(marks, split_ref[0], TN, preferred_element_type=f32)
        total = total + lax.dot_general(marks, split_ref[1], TN, preferred_element_type=f32)
        emb_ref[pl.ds(step * lines, lines)] = total.reshape(lines, vr, feat)

    def convolution(begin, end):
        for r in range(rows):
            sub = slice(r * RUNS, (r + 1) * RUNS)
            length = len_ref[r]
            for tile in range(feat // LANES):
                cols = slice(tile * LANES, (tile + 1) * LANES)
                taps = [jnp.broadcast_to(rows_ref[k : k + 1, cols], (RUNS, LANES)) for k in range(kernel)]
                window = [emb_ref[begin + k, sub, cols] for k in range(kernel - 1)]
                for i in range(begin, end):
                    window.append(emb_ref[i + kernel - 1, sub, cols])
                    total = taps[0] * window[0]
                    for k in range(1, kernel):
                        total = total + taps[k] * window[k]
                    window = window[1:]
                    real = base < length - (i - 2)
                    if i < 2:
                        real = real & (base >= 2 - i)
                    conv_ref[i, sub, cols] = jnp.where(real, total, 0.0)

    chunks, tiles = span // lines, feat // LANES
    done = 0
    for step in range(chunks):
        embedding(step)
        if step < tiles:
            products(step)
        ready = min(step * lines - (kernel - 1), run + 4)
        if ready > done:
            convolution(done, ready)
            done = ready
    for tile in range(chunks, tiles):
        products(tile)
    convolution(done, run + 4)
    for i in range(vocab // vr):
        seen = jnp.sum(seen_ref[i * vr : (i + 1) * vr, :], axis=1, keepdims=True)
        pack_ref[SEEN + i] = jnp.broadcast_to(seen, (vr, LANES))
    keeps = [
        pltpu.make_async_copy(turn_ref, mark_hbm, sems.at[1, 0]), pltpu.make_async_copy(emb_ref, emb_hbm, sems.at[1, 1])
    ]
    for copy in keeps:
        copy.start()

    size = RUNS * half
    order = iota((size, size), 0)
    order = (iota((size, size), 1) == order % RUNS * half + order // RUNS).astype(f32)
    order_ref[...] = order.astype(jnp.bfloat16)

    keeps.append(pltpu.make_async_copy(conv_ref, conv_hbm, sems.at[2, 0]))
    keeps[-1].start()

    block = 4
    slices = run + 4
    zero = jnp.zeros((RUNS, LANES), f32)
    def lagged(r, carry):
        at = pl.ds(pl.multiple_of(r * RUNS, RUNS), RUNS)
        some = grad_ref.at[pl.ds(pl.multiple_of(r * size, 8), size), :]
        for pair in range(feat // WIDE):
            wide = slice(pair * WIDE, (pair + 1) * WIDE)
            high, low = in_two(some[:, wide])
            moved = jnp.dot(order_ref[...], high, preferred_element_type=f32)
            moved = moved + jnp.dot(order_ref[...], low, preferred_element_type=f32)
            cot_ref[:, at, wide] = moved.reshape(half, RUNS, WIDE)
        values = [zero] * 6
        for first in range(0, slices, block):
            acc = {}
            for tile in range(feat // LANES):
                cols = slice(tile * LANES, (tile + 1) * LANES)
                u = [conv_ref[first + i, at, cols] for i in range(min(block + 5, slices - first))]
                for i in range(block):
                    for lag in range(min(6, slices - first - i)):
                        term = u[i] * u[i + lag]
                        acc[i, lag] = term if tile == 0 else acc[i, lag] + term
            for i, lag in acc:
                here = lane == first + (i + OFF - 2)
                values[lag] = jnp.where(here, jnp.sum(acc[i, lag], axis=1, keepdims=True), values[lag])
        for lag in range(6):
            pack_ref[lag, at, :] = values[lag]
        return carry

    fetch[6].wait()
    lax.fori_loop(0, rows, lagged, 0)
    keeps.append(pltpu.make_async_copy(cot_ref, cot_hbm, sems.at[3, 0]))
    keeps[-1].start()

    def total_of(x):
        return jnp.sum(jnp.sum(x, axis=1, keepdims=True), axis=0, keepdims=True)

    def lookups(r, sums):
        at = pl.ds(pl.multiple_of(r * RUNS, RUNS), RUNS)
        ids = pack_ref[IDS, at, :].astype(jnp.int32)
        real = ids >= 0
        low = jnp.where(real, ids, 0)

        def look(row):
            value = jnp.zeros((RUNS, LANES), f32)
            for part in range(vocab // LANES):
                entry = jnp.broadcast_to(
                    table_ref[row : row + 1, part * LANES : (part + 1) * LANES], (RUNS, LANES)
                )
                taken = jnp.take_along_axis(entry, low % LANES, axis=1)
                value = jnp.where(low // LANES == part, taken, value)
            return jnp.where(real, value, 0.0)

        scored = jnp.zeros((RUNS, LANES), f32)
        biased = jnp.zeros((RUNS, LANES), f32)
        for k in range(kernel):
            scored = scored + shifted(look(k), k - (kernel - 1))
            biased = biased + shifted(look(4 + k), k - (kernel - 1))
        inner_real = real & (lane >= OFF - 2)
        scored = jnp.where(inner_real, scored, 0.0)
        biased = jnp.where(inner_real, biased, 0.0)
        pack_ref[13, at, :] = scored
        pack_ref[14, at, :] = biased
        own = (real & (lane >= OFF) & (lane < OFF + run)).astype(f32)
        new = (own * look(8), own, own * biased, own * pack_ref[0, at, :], own * (1 - lane % 2).astype(f32))
        return tuple(a + b for a, b in zip(sums, new))

    def crossed(r, sums):
        at = pl.ds(pl.multiple_of(r * RUNS, RUNS), RUNS)
        sums = lookups(r, sums)
        values = [zero] * 7
        for first in range(0, half, block):
            acc = {}
            for tile in range(feat // LANES):
                cols = slice(tile * LANES, (tile + 1) * LANES)
                u = [conv_ref[2 * first + i, at, cols] for i in range(2 * block + 4)]
                bias = jnp.broadcast_to(rows_ref[BIAS : BIAS + 1, tile * LANES : (tile + 1) * LANES], (RUNS, LANES))
                for i in range(block):
                    g = cot_ref[first + i, at, cols]
                    terms = [g * u[2 * i + d] for d in range(6)] + [g * bias]
                    for d in range(7):
                        acc[i, d] = terms[d] if tile == 0 else acc[i, d] + terms[d]
            for i, d in acc:
                here = lane == 2 * first + (2 * i + OFF)
                values[d] = jnp.where(here, jnp.sum(acc[i, d], axis=1, keepdims=True), values[d])
        for d in range(7):
            pack_ref[6 + d, at, :] = values[d]
        return sums

    sums = lax.fori_loop(0, rows, crossed, (zero,) * 5)
    sums_ref[...] = spread([total_of(x) for x in sums], sums_ref.shape[0])
    for copy in keeps:
        copy.wait()


def in_two(x):
    high = x.astype(jnp.bfloat16)
    return high, (x - high.astype(f32)).astype(jnp.bfloat16)


def unpack_rows(pack_ref, rows_ref):
    for tile in range(rows_ref.shape[1] // LANES):
        at = slice(tile % 4 * 8, tile % 4 * 8 + 8)
        rows_ref[:, tile * LANES : (tile + 1) * LANES] = pack_ref[WEIGHTS + tile // 4, at, :]


def spread(sums, count):
    lane = iota((1, LANES), 1)
    row = jnp.zeros((1, LANES), f32)
    for i, x in enumerate(sums):
        row = jnp.where(lane == i, x, row)
    return jnp.broadcast_to(row[None], (count, 1, LANES))


def picked(ref, number):
    row = jnp.sum(ref[...], axis=0)
    return [row[:, i : i + 1] for i in range(number)]


def scales(first_ref, bias, feat):
    emb_sum, count, cross, square, count4 = picked(first_ref, 5)
    one = jnp.sqrt(emb_sum / (count * feat) + EPS)
    bias_sum = jnp.sum(bias * bias, axis=1, keepdims=True)
    conv_sum = jnp.maximum(count * bias_sum + 2.0 * cross / one + square / (one * one), 0.0)
    two = jnp.sqrt(conv_sum / (count * feat) + EPS)
    return one, two, count, count4, bias_sum, cross


class Places:
    def __init__(self, ids, start, run):
        shape = ids.shape
        self.j = iota(shape, 1) - OFF
        sub = iota(shape, 0) % RUNS
        self.inside = (self.j >= 0) & (self.j < run)
        self.real = ((ids >= 0) & (self.j >= -2)).astype(f32)
        self.own = jnp.where(self.inside, self.real, 0.0)
        shown = self.j + OFF
        self.two, self.four = shown % 2, shown % 4
        self.three = (start + run * sub + shown + (3 * OFF - OFF)) % 3

    def holds(self, size, by):
        if size == 1:
            return jnp.ones_like(self.real) if by == 0 else None
        if abs(by) >= size:
            return None
        phase = {2: self.two, 3: self.three, 4: self.four}[size]
        return ((phase + by >= 0) & (phase + by < size)).astype(f32)

    def pooled(self, size, x):
        if size == 1:
            return x
        pair = x + jnp.where(self.two == 0, shifted(x, 1), shifted(x, -1))
        if size == 2:
            return pair
        if size == 4:
            return pair + jnp.where(self.four < 2, shifted(pair, 2), shifted(pair, -2))
        left, right = shifted(x, -1), shifted(x, 1)
        side = jnp.where(self.three == 0, shifted(x, 2), left)
        far = jnp.where(self.three == 2, shifted(x, -2), right)
        return x + side + far

    def both(self, x):
        return x + shifted(x, -1)


SIZES = (1, 2, 3, 4)
REACH = range(-3, 4)


def score_kernel(sizes, first_ref, dots_ref, state_ref, sums_ref, rows_ref):
    rows, width, run, feat, vocab, kernel = sizes
    start = lax.axis_index("seq") * width
    unpack_rows(dots_ref, rows_ref)
    bias = rows_ref[BIAS : BIAS + 1, :]
    one, two, count, count4, bias_sum, cross = scales(first_ref, bias, feat)
    at = Places(dots_ref[IDS], start, run)
    real, own = at.real, at.own
    rate = 1.0 / (one * two)
    bias_score = jnp.sum(bias * rows_ref[SCORER : SCORER + 1, :], axis=1, keepdims=True) / two

    normed_score = real * bias_score + rate * dots_ref[13]
    counts = [jnp.maximum(at.pooled(b, real), 1.0) for b in SIZES]
    scores = [at.pooled(b, normed_score) / n for b, n in zip(SIZES, counts)]
    top = functools.reduce(jnp.maximum, scores)
    parts = [jnp.exp(s - top) for s in scores]
    whole = sum(parts)
    probs = [p / whole for p in parts]
    weights = [own * p / n for p, n in zip(probs, counts)]

    holds = {(b, d): at.holds(b, d) for b in SIZES for d in REACH}

    def blend(values):
        out = {}
        for d in REACH:
            terms = [v * holds[b, d] for b, v in zip(SIZES, values) if holds[b, d] is not None]
            out[d] = sum(terms)
        return out

    mixer = blend(weights)
    pair_count = jnp.maximum(at.pooled(2, real), 1.0)
    halver = {}
    even = at.two == 0
    for d in REACH:
        zero = jnp.zeros_like(real)
        ahead = shifted(mixer[d - 1], 1) if d - 1 >= -3 else zero
        behind = shifted(mixer[d + 1], -1) if d + 1 <= 3 else zero
        other = jnp.where(even, ahead, behind)
        halver[d] = jnp.where(at.inside, (mixer[d] + other) / pair_count, 0.0)

    bias_dot = dots_ref[14]
    normed_bias = real * (bias_sum / two) + rate * bias_dot
    lags = []
    for lag in range(6):
        later = shifted(real, lag)
        value = rate * rate * dots_ref[lag]
        value = value + (rate / two) * (bias_dot * later + real * shifted(bias_dot, lag))
        lags.append(value + (bias_sum / (two * two)) * (real * later))

    def gram(a, b):
        low, high = min(a, b), max(a, b)
        return shifted(lags[high - low], low) if high - low < 6 else None

    table = {(a, b): gram(a, b) for a in REACH for b in REACH if a <= b}

    def against(weighting):
        out = {}
        for a in REACH:
            out[a] = sum(
                weighting[b] * table[min(a, b), max(a, b)]
                for b in REACH if table[min(a, b), max(a, b)] is not None
            )
        return out

    with_mixed, with_half = against(mixer), against(halver)
    with_grad = {}
    grad_bias = dots_ref[12]
    cross_dots = {
        d: rate * dots_ref[6 + d + 2] + shifted(real, d) * (grad_bias / two) for d in range(-2, 4)
    }
    for d in REACH:
        here = cross_dots[d] if d >= -2 else jnp.zeros_like(real)
        before = shifted(cross_dots[d + 1], -1) if d + 1 <= 3 else jnp.zeros_like(real)
        with_grad[d] = jnp.where(even, here, before)

    def per_block(values, scale):
        out = []
        for b, n in zip(SIZES, counts):
            terms = [values[d] * holds[b, d] for d in REACH if holds[b, d] is not None]
            out.append(scale * sum(terms) / n)
        return out

    shared = own / pair_count
    bases = [per_block(with_grad, shared), per_block(with_half, shared), per_block(with_mixed, own)]

    def total_of(x):
        return jnp.sum(jnp.sum(x, axis=1, keepdims=True), axis=0, keepdims=True)

    first_of_pair = jnp.where(even & at.inside, 1.0, 0.0)
    mean_score = sum(p * s for p, s in zip(probs, scores))

    def bent(values):
        mean = sum(p * v for p, v in zip(probs, values))
        return total_of(own * (sum(p * s * v for p, s, v in zip(probs, scores, values)) - mean * mean_score))

    sums = [
        total_of(sum(own * mixer[d] * with_mixed[d] for d in REACH)),
        total_of(first_of_pair * sum(halver[d] * with_half[d] for d in REACH)),
        total_of(first_of_pair * sum(halver[d] * with_grad[d] for d in REACH)),
        bent(bases[0]), bent(bases[1]), bent(bases[2]),
        total_of(shared * at.both(grad_bias)),
        total_of(shared * sum(halver[d] * shifted(normed_bias, d) for d in REACH)),
        total_of(own * sum(mixer[d] * shifted(normed_bias, d) for d in REACH)),
    ]
    for i, b in enumerate(SIZES):
        state_ref[i] = weights[i]
        state_ref[4 + i] = probs[i]
        for f in range(3):
            state_ref[8 + 4 * f + i] = bases[f][i]
    sums_ref[...] = spread(sums, sums_ref.shape[0])


def back_kernel(
    sizes, first_hbm, second_hbm, pack_hbm, state_hbm, mark_hbm, embed_hbm, conv_hbm, emb_hbm, cot_hbm,
    out_hbm, keep_ref, send_ref,
    first_ref, second_ref, pack_ref, state_ref, mark_ref, embed_ref, rows_ref, turn_ref, out_ref, order_ref,
    narrow_ref, acc_ref, pay_ref, conv_ref, emb_ref, cot_ref, back_ref, sems,
):
    rows, width, run, feat, vocab, kernel = sizes
    tiles = feat // LANES
    per = WIDE // LANES
    units = rows * (feat // WIDE)
    half = run // 2
    vr = rows * RUNS

    def fetches(unit):
        sub = pl.ds(pl.multiple_of(unit % rows * RUNS, RUNS), RUNS)
        cols = pl.ds(pl.multiple_of(unit // rows * WIDE, LANES), WIDE)
        return [
            pltpu.make_async_copy(a.at[:, sub, cols], b.at[:, sub, cols], sems.at[i, unit])
            for i, (a, b) in enumerate(((conv_hbm, conv_ref), (cot_hbm, cot_ref), (emb_hbm, emb_ref)))
        ]

    size = RUNS * half

    def stored(unit):
        some = pl.ds(pl.multiple_of(unit % rows * size, 8), size)
        cols = pl.ds(pl.multiple_of(unit // rows * WIDE, LANES), WIDE)
        return pltpu.make_async_copy(out_ref.at[some, cols], out_hbm.at[some, cols], sems.at[3, unit])

    def restore(unit):
        some = pl.ds(pl.multiple_of(unit % rows * size, 8), size)
        cols = pl.ds(pl.multiple_of(unit // rows * WIDE, LANES), WIDE)
        high, low = in_two(turn_ref[...].reshape(size, WIDE))
        moved = jnp.dot(order_ref[...], high, preferred_element_type=f32)
        out_ref[some, cols] = moved + jnp.dot(order_ref[...], low, preferred_element_type=f32)

    sources = (first_hbm, second_hbm, pack_hbm, state_hbm, mark_hbm, embed_hbm)
    targets = (first_ref, second_ref, pack_ref, state_ref, mark_ref, embed_ref)
    small = [pltpu.make_async_copy(a, b, sems.at[4, i]) for i, (a, b) in enumerate(zip(sources, targets))]
    small[2] = pltpu.make_async_copy(pack_hbm.at[IDS:], pack_ref.at[IDS:], sems.at[4, 2])
    ahead = 3
    for copy in small[:4]:
        copy.start()
    for unit in range(ahead):
        for copy in fetches(unit):
            copy.start()
    for copy in small[4:]:
        copy.start()
    for copy in small[:4]:
        copy.wait()

    start = lax.axis_index("seq") * width
    unpack_rows(pack_ref, rows_ref)
    bias = rows_ref[BIAS : BIAS + 1, :]
    one, two, count, count4, bias_sum, cross = scales(first_ref, bias, feat)
    mixed_sum, half_sum, inner, bent_g, bent_h, bent_m, bias_g, bias_h, bias_m = picked(second_ref, 9)
    volume, volume4 = count * feat, count4 * feat
    three = jnp.sqrt(mixed_sum / volume + EPS)
    four = jnp.sqrt(half_sum / (three * three) / volume4 + EPS)
    fourth = (inner / three) / (four * four * four * volume4)
    alpha = 1.0 / (three * four)
    beta = -fourth / (three * three)
    gamma = -(inner / four - fourth / three * half_sum) / (three * three * three * volume)
    joint = alpha * (inner + bent_g) + beta * (half_sum + bent_h) + gamma * (mixed_sum + bent_m)
    rate = 1.0 / (one * two)
    normed_bias = count * bias_sum / two + rate * cross
    bias_back = (alpha * bias_g + beta * bias_h + gamma * bias_m - joint / volume * normed_bias) / two
    inner_one = one * (joint * EPS / (two * two) - bias_back)
    first_coef = inner_one / (one * one * one * volume)

    at = Places(pack_ref[IDS], start, run)
    probs = [state_ref[4 + i] for i in range(4)]
    weights = [state_ref[i] for i in range(4)]
    grads = [
        alpha * state_ref[8 + i] + beta * state_ref[12 + i] + gamma * state_ref[16 + i] for i in range(4)
    ]
    mean = sum(p * g for p, g in zip(probs, grads))
    spreading = jnp.zeros_like(probs[0])
    for i, b in enumerate(SIZES):
        bent = probs[i] * (grads[i] - mean)
        n = jnp.maximum(at.pooled(b, at.real), 1.0)
        spreading = spreading + at.pooled(b, jnp.where(at.inside, bent / n, 0.0))
    pair_real = at.pooled(2, at.real)
    pair_count = jnp.maximum(pair_real, 1.0)
    filled = (pair_real > 0).astype(f32)
    narrow = [rate * w for w in weights] + [rate * spreading, at.real]
    paired = [
        alpha / pair_count, alpha * filled, beta / (pair_count * pair_count), beta * filled / pair_count + gamma
    ]
    leak = jnp.sum(jnp.sum(spreading * at.real, axis=1, keepdims=True), axis=0, keepdims=True)

    for i, x in enumerate(narrow + paired):
        narrow_ref[i] = x
    order = iota((size, size), 0)
    order = (iota((size, size), 1) == order % half * RUNS + order // half).astype(f32)
    order_ref[...] = order.astype(jnp.bfloat16)
    turn_ref[...] = jnp.zeros_like(turn_ref)
    acc_ref[...] = jnp.zeros_like(acc_ref)
    phase = (start + run * iota((RUNS, LANES), 0)) % 3
    at_phase = [phase == p for p in range(3)]

    def chosen(j, a, b, c):
        return jnp.where(at_phase[(0 - j) % 3], a, jnp.where(at_phase[(1 - j) % 3], b, c))

    full = (RUNS, LANES)
    alpha_all = jnp.broadcast_to(alpha, full)
    gamma_all = jnp.broadcast_to(gamma, full)
    fall = jnp.broadcast_to(rate * rate * joint / volume, full)
    fall_bias = rate * joint / volume / two

    def column(r, tile, near, factor):
        sub = pl.ds(pl.multiple_of(r * RUNS, RUNS), RUNS)
        cols = pl.ds(pl.multiple_of(tile * LANES, LANES), LANES)
        taps = [jnp.broadcast_to(rows_ref[k : k + 1, cols], full) for k in range(kernel)]
        bias_row = rows_ref[BIAS : BIAS + 1, cols]
        normed_row = jnp.broadcast_to(bias_row / two, full)
        fall_row = jnp.broadcast_to(bias_row * fall_bias, full)
        scorer = jnp.broadcast_to(rows_ref[SCORER : SCORER + 1, cols], full)
        zero = jnp.zeros(full, f32)

        u, triple, y3, gc = {}, {}, {}, {}
        sums = [zero] * (kernel + 2)
        block = {}
        twos, y_twos = {}, {}
        for j in range(-2, 2):
            u[j] = conv_ref[j + 2, sub, cols]

        def pair_of(j):
            if j not in twos:
                twos[j] = u[j] + u[j + 1]
            return twos[j]

        triple[-2] = pair_of(-2) + u[0]
        triple[-1] = u[-1] + pair_of(0)

        def window(j):
            if 0 <= j <= run - 3:
                first = j if j % 2 == 0 else j + 1
                if first not in y_twos:
                    y_twos[first] = y3[first] + y3[first + 1]
                return y_twos[first] + y3[j + 2 if j % 2 == 0 else j]
            near = [y3[i] for i in (j, j + 1, j + 2) if 0 <= i < run]
            return functools.reduce(lambda a, b: a + b, near) if near else zero

        def settle(s):
            nonlocal sums
            for j in (s, s - 1, s - 2):
                if j not in block:
                    block[j] = window(j)
            g = chosen(s, block[s], block[s - 1], block[s - 2])
            sigma = factor(4, s)
            g = g + sigma * scorer
            if 0 <= s < run:
                g = g + lone[s]
                g = g - fall * u[s]
            g = g * factor(5, s)
            gc[s] = g
            for k in range(kernel):
                sums[k] = sums[k] + g * emb_ref[s - kernel + 1 + k + LEFT, sub, cols]
            sums[kernel] = sums[kernel] + g
            sums[kernel + 1] = sums[kernel + 1] + sigma * u[s]

        def finish(s):
            terms = [taps[k] * gc[s + kernel - 1 - k] for k in range(kernel) if s + kernel - 1 - k in gc]
            back_ref[s + LEFT, sub, cols] = functools.reduce(lambda a, b: a + b, terms)

        lone = {}
        settled = -2
        finished = -LEFT
        for quad in range(0, run, 4):
            for j in range(quad + 2, quad + 6):
                u[j] = conv_ref[j + 2, sub, cols]
            two_sums = [pair_of(quad), pair_of(quad + 2)]
            four_sum = two_sums[0] + two_sums[1]
            shares = []
            wide = zero
            for p in range(2):
                y = None
                xs = []
                for j in (quad + 2 * p, quad + 2 * p + 1):
                    triple[j] = u[j] + pair_of(j + 1) if j % 2 else two_sums[p] + u[j + 2]
                    x = factor(0, j) * u[j] + factor(1, j) * two_sums[p]
                    x = x + factor(2, j) * chosen(j, triple[j], triple[j - 1], triple[j - 2])
                    x = x + factor(3, j) * four_sum
                    xs.append(x)
                y = xs[0] + xs[1]
                k = quad // 2 + p
                scale_y = factor(6, 2 * k)
                turn_ref[k, :, near] = scale_y * y + factor(7, 2 * k) * normed_row
                q = scale_y * cot_ref[k, sub, cols] + factor(8, 2 * k) * y + factor(9, 2 * k) * normed_row
                pair = zero
                for i, j in enumerate((quad + 2 * p, quad + 2 * p + 1)):
                    g = q + gamma_all * xs[i]
                    lone[j] = factor(0, j) * g
                    y3[j] = factor(2, j) * g
                    pair = factor(1, j) * g if i == 0 else pair + factor(1, j) * g
                    wide = factor(3, j) * g if i + p == 0 else wide + factor(3, j) * g
                shares.append(pair)
            wide = wide - fall_row
            for p in range(2):
                share = shares[p] + wide
                for j in (quad + 2 * p, quad + 2 * p + 1):
                    lone[j] = lone[j] + share
            last = quad + 3 - 2 if quad + 4 < run else run + 1
            while settled <= last:
                settle(settled)
                settled += 1
            done = settled - kernel if quad + 4 < run else run + RIGHT - 1
            while finished <= done:
                finish(finished)
                finished += 1
            yield
        for i in range(kernel + 2):
            acc_ref[i, :, cols] = acc_ref[i, :, cols] + sums[i]

    def some_columns(unit, carry):
        for copy in fetches(unit):
            copy.wait()

        @pl.when(unit + ahead < units)
        def _():
            for copy in fetches(unit + ahead):
                copy.start()

        r = unit % rows
        made = {}

        def factor(i, j):
            if (i, j) not in made:
                sub = pl.ds(pl.multiple_of(r * RUNS, RUNS), RUNS)
                made[i, j] = jnp.broadcast_to(narrow_ref[i, sub, j + OFF : j + OFF + 1], full)
            return made[i, j]

        last = jnp.maximum(unit - 1, 0)
        restore(last)
        parts = []
        for i in range(per):
            near = slice(i * LANES, (i + 1) * LANES)
            parts.append(column(r, unit // rows * per + i, near, factor))
        for _ in zip(*parts, strict=True):
            pass

        @pl.when(unit > 0)
        def _():
            stored(last).start()

        return carry

    lax.fori_loop(0, units, some_columns, 0)
    restore(units - 1)
    stored(units - 1).start()

    positions = mark_ref.shape[1]
    edge = run + LEFT + RIGHT
    back_ref[edge:] = jnp.zeros((back_ref.shape[0] - edge, vr, feat), f32)
    for copy in small[4:]:
        copy.wait()
    total_tiles = pay_ref.shape[0]

    def gather(pair, carry):
        cols = pl.ds(pl.multiple_of(pair * WIDE, LANES), WIDE)
        high, low = in_two(back_ref[:, :, cols].reshape(positions, WIDE))
        total = jnp.dot(mark_ref[...], high, preferred_element_type=f32)
        total = total + jnp.dot(mark_ref[...], low, preferred_element_type=f32)
        for v in range(vocab // 8):
            seen = first_coef * pack_ref[SEEN + v * 8 // vr, v * 8 % vr : v * 8 % vr + 8, :]
            for i in range(per):
                wide = pl.ds(pl.multiple_of(pair * WIDE + i * LANES, LANES), LANES)
                part = total[v * 8 : v * 8 + 8, i * LANES : (i + 1) * LANES]
                pay_ref[v * tiles + pair * per + i] = part - seen * embed_ref[v * 8 : v * 8 + 8, wide]
        return carry

    for pair in range(feat // WIDE):
        gather(pair, 0)

    end = vocab // 8 * tiles
    pay_ref[end:] = jnp.zeros((total_tiles - end, 8, LANES), f32)
    for i in range(kernel + 2):
        row = jnp.sum(acc_ref[i], axis=0, keepdims=True)
        if i == kernel:
            row = row * one
        if i == kernel + 1:
            row = row + bias * (leak / two)
        for tile in range(tiles):
            place = i * tiles + tile
            pay_ref[end + place // 8, place % 8 : place % 8 + 1, :] = row[:, tile * LANES : (tile + 1) * LANES]
    core = lax.axis_index("seq") % 2
    part = total_tiles // 2
    keep_ref[...] = pay_ref[pl.ds(core * part, part)]
    send_ref[...] = pay_ref[pl.ds((1 - core) * part, part)]
    for unit in range(units):
        stored(unit).wait()


def finish_kernel(feat, mine_ref, other_ref, table_hbm, taps_ref, bias_ref, scorer_ref, sems):
    core = lax.axis_index("seq") % 2
    tiles = feat // LANES
    part = mine_ref.shape[0]
    rest = table_hbm.shape[0] - part
    for side in range(2):

        @pl.when(core == side)
        def _():
            first, second = (mine_ref, other_ref) if side == 0 else (other_ref, mine_ref)
            copies = (
                pltpu.make_async_copy(first, table_hbm.at[0:part], sems.at[0]),
                pltpu.make_async_copy(second.at[0:rest], table_hbm.at[part : part + rest], sems.at[1]),
            )
            for copy in copies:
                copy.start()
            lines = []
            for i in range(taps_ref.shape[0] + 2):
                places = [i * tiles + tile for tile in range(tiles)]
                lines.append([second[rest + p // 8, p % 8 : p % 8 + 1, :] for p in places])
            for i in range(taps_ref.shape[0]):
                taps_ref[i : i + 1, :] = jnp.concatenate(lines[i], axis=1)
            bias_ref[...] = jnp.concatenate(lines[-2], axis=1).reshape(feat)
            scorer_ref[...] = jnp.concatenate(lines[-1], axis=1).reshape(feat)
            for copy in copies:
                copy.wait()


def exchanged(x):
    return lax.all_to_all(x, AXES, 0, 0, tiled=True)


def partner(x, axis, step):
    n = lax.axis_size(axis)
    return lax.ppermute(x, axis, [(i, i ^ step) for i in range(n)])


def summed_over_devices(keep, send):
    n = lax.axis_size("seq")
    others = lax.axis_size("rows") * n // 2
    groups = [[2 * i + side for i in range(others)] for side in range(2)]

    def traded(x):
        return lax.all_to_all(x, AXES, 0, 0, tiled=True, axis_index_groups=groups)

    x = keep + partner(send, "seq", 1)
    chunk = (others, x.shape[0] * x.shape[1] // others, 1, LANES)
    part = jnp.sum(traded(x.reshape(chunk)), axis=0)
    x = traded(jnp.broadcast_to(part[None], chunk)).reshape(x.shape)
    return x, partner(x, "seq", 1)


def on_device(byte_ids, lengths, embed, conv_weight, conv_bias, score_weight, out_grad):
    rows, width = byte_ids.shape
    vocab, feat = embed.shape
    kernel = conv_weight.shape[0]
    run = width // RUNS
    half = width // 2
    vr = rows * RUNS
    sizes = (rows, width, run, feat, vocab, kernel)
    count = lax.axis_size("seq")
    devices = count * lax.axis_size("rows")
    span = -(-(run + LEFT + RIGHT) // 8) * 8
    tiles = feat // LANES
    struct = jax.ShapeDtypeStruct
    sem = pltpu.SemaphoreType.DMA

    params = pltpu.CompilerParams(vmem_limit_bytes=60 * 1024 * 1024)

    pairs_of = [[(i, i + 1) for i in range(first, count - 1, 2)] for first in range(2)]
    near = [lax.ppermute(byte_ids, "seq", some + [(j, i) for i, j in some]) for some in pairs_of]
    near = [pltpu.with_memory_space_constraint(x, pltpu.VMEM) for x in near]

    pairs = feat // WIDE
    bf16 = jnp.bfloat16
    wide_emb = struct((span, vr, feat), f32)
    wide_conv = struct((run + 4, vr, feat), f32)
    wide_cot = struct((half // RUNS, vr, feat), f32)
    marks = struct((vocab, span * vr), bf16)
    pack = struct((SEEN + vocab // vr, vr, LANES), f32)
    sums = struct((devices, 1, LANES), f32)
    state = struct((20, vr, LANES), f32)

    def scratch(like):
        return pltpu.VMEM(like.shape, like.dtype)

    emb, conv, cot, mark, packed, first = pl.pallas_call(
        functools.partial(stats_kernel, sizes),
        out_shape=(*(pltpu.HBM(x.shape, x.dtype) for x in (wide_emb, wide_conv, wide_cot, marks, pack)), pltpu.VMEM(sums.shape, f32)),
        in_specs=[HBM, VMEM, VMEM] + [HBM] * 6, out_specs=(HBM,) * 4 + (VMEM,) * 2,
        scratch_shapes=[
            scratch(byte_ids), pltpu.SMEM((rows,), jnp.int32), scratch(embed),
            scratch(conv_weight), scratch(conv_bias), scratch(score_weight), pltpu.VMEM((rows * half, feat), f32),
            pltpu.VMEM((2, vocab, feat), bf16), pltpu.VMEM((16, vocab), f32), pltpu.VMEM((8, feat), f32),
            scratch(marks), pltpu.VMEM((-(-span * vr // LANES // 8) * 8, LANES), f32), pltpu.VMEM((vocab, LANES), f32),
            pltpu.VMEM((half, half), bf16), pltpu.VMEM((vr, LANES), jnp.int32), scratch(wide_emb),
            scratch(wide_conv), scratch(wide_cot), sem((4, 9)),
        ],
        compiler_params=params, name="stats",
    )(
        byte_ids, *near, lengths, embed, conv_weight, conv_bias, score_weight,
        out_grad.reshape(rows * half, feat),
    )
    first = exchanged(first)

    states, second = pl.pallas_call(
        functools.partial(score_kernel, sizes),
        out_shape=(pltpu.HBM(state.shape, f32), pltpu.VMEM(sums.shape, f32)),
        in_specs=[VMEM] * 2, out_specs=(VMEM, VMEM), scratch_shapes=[pltpu.VMEM((8, feat), f32)],
        compiler_params=params, name="score",
    )(first, packed)
    second = exchanged(second)

    lines = vocab * tiles
    lines = -(-(lines + (kernel + 2) * tiles) // devices) * devices
    parts = struct((lines // 16, 8, LANES), f32)
    blocks, keep, send = pl.pallas_call(
        functools.partial(back_kernel, sizes),
        out_shape=(pltpu.HBM((rows * half, feat), f32), pltpu.VMEM(parts.shape, f32), pltpu.VMEM(parts.shape, f32)),
        in_specs=[HBM] * 9, out_specs=(HBM, VMEM, VMEM),
        scratch_shapes=[
            scratch(sums), scratch(sums), scratch(pack), scratch(state), scratch(marks), scratch(embed),
            pltpu.VMEM((8, feat), f32), pltpu.VMEM((half // RUNS, RUNS, WIDE), f32),
            pltpu.VMEM((rows * half, feat), f32), pltpu.VMEM((half, half), bf16), pltpu.VMEM((10, vr, LANES), f32),
            pltpu.VMEM((kernel + 2, RUNS, feat), f32), pltpu.VMEM((lines // 8, 8, LANES), f32),
            scratch(wide_conv), scratch(wide_emb), scratch(wide_cot), scratch(wide_emb),
            sem((5, max(6, rows * pairs))),
        ],
        compiler_params=params, name="back",
    )(first, second, packed, states, mark, embed, conv, emb, cot)

    mine, other = summed_over_devices(keep, send)
    table, taps_grad, bias_grad, scorer_grad = pl.pallas_call(
        functools.partial(finish_kernel, feat),
        out_shape=(
            pltpu.HBM((vocab * tiles // 8, 8, LANES), f32), struct((kernel, feat), f32), struct((feat,), f32),
            struct((feat,), f32),
        ),
        in_specs=[VMEM, VMEM], out_specs=(HBM, VMEM, VMEM, VMEM), scratch_shapes=[sem((2,))],
        compiler_params=pltpu.CompilerParams(vmem_limit_bytes=8 * 1024 * 1024), name="finish",
    )(mine, other)
    table = table.reshape(vocab // 8, tiles, 8, LANES).transpose(0, 2, 1, 3).reshape(vocab, feat)
    return blocks.reshape(rows, half, feat), table, taps_grad, bias_grad, scorer_grad


def solution(mesh):
    placed = (P("rows", "seq"), P("rows"), P(), P(), P(), P(), P("rows", "seq", None))
    return jax.shard_map(
        on_device,
        mesh=mesh,
        in_specs=placed,
        out_specs=(P("rows", "seq", None), P(), P(), P(), P()),
        check_vma=False,
    )
```

```python
import functools

import jax
import jax.numpy as jnp
from jax import lax
from jax.experimental import pallas as pl
from jax.experimental.pallas import tpu as pltpu
from jax.sharding import PartitionSpec as P

f32 = jnp.float32
EPS = 1e-06
LANES = 128
WIDE = 256
RUNS = 8
OFF = 8
LEFT, RIGHT = 5, 2
NT = (((1,), (1,)), ((), ()))
TN = (((0,), (0,)), ((), ()))
AXES = ("rows", "seq")
VMEM = pl.BlockSpec(memory_space=pltpu.VMEM)
HBM = pl.BlockSpec(memory_space=pltpu.HBM)


def iota(shape, dim):
    return lax.broadcasted_iota(jnp.int32, shape, dim)


def shifted(x, by):
    return x if by == 0 else pltpu.roll(x, (-by) % LANES, 1)


BIAS, SCORER = 4, 5
IDS, WEIGHTS, SEEN = 15, 16, 18


def stats_kernel(
    sizes, own_hbm, even_ref, odd_ref, len_hbm, embed_hbm, taps_hbm, bias_hbm, scorer_hbm, grad_hbm,
    emb_hbm, conv_hbm, cot_hbm, mark_hbm, pack_ref, sums_ref,
    own_ref, len_ref, embed_ref, taps_ref, bias_ref, scorer_ref, grad_ref,
    split_ref, table_ref, rows_ref, turn_ref, line_ref, seen_ref, order_ref, run_ref, emb_ref, conv_ref, cot_ref, sems,
):
    rows, width, run, feat, vocab, kernel = sizes
    half = run // 2
    vr = rows * RUNS
    span = emb_ref.shape[0]
    sources = (own_hbm, len_hbm, embed_hbm, taps_hbm, bias_hbm, scorer_hbm, grad_hbm)
    targets = (own_ref, len_ref, embed_ref, taps_ref, bias_ref, scorer_ref, grad_ref)
    fetch = [pltpu.make_async_copy(a, b, sems.at[0, i]) for i, (a, b) in enumerate(zip(sources, targets))]
    for copy in fetch:
        copy.start()
    start = lax.axis_index("seq") * width
    lane = iota((RUNS, LANES), 1)
    sub = iota((RUNS, LANES), 0)
    base = start + run * sub
    back = (OFF - run) % LANES

    for copy in fetch[:2]:
        copy.wait()
    for r in range(rows):
        for s in range(RUNS):
            line = own_ref[r : r + 1, s * run // LANES * LANES : (s * run // LANES + 1) * LANES]
            shift = -(s * run % LANES) % LANES
            line = jnp.broadcast_to(line, (RUNS, LANES))
            line = pltpu.roll(line, shift, 1) if shift else line
            run_ref[r * RUNS + s : r * RUNS + s + 1, :] = line[0:1]
    odd = lax.axis_index("seq") % 2 == 1
    for r in range(rows):
        own = run_ref[r * RUNS : (r + 1) * RUNS, :]
        tail = slice(width - LANES, width)
        left = jnp.where(odd, even_ref[r : r + 1, tail], odd_ref[r : r + 1, tail])
        right = jnp.where(odd, odd_ref[r : r + 1, 0:LANES], even_ref[r : r + 1, 0:LANES])
        before = pltpu.roll(pltpu.roll(own, 1, 0), back, 1)
        edge = pltpu.roll(jnp.broadcast_to(left, (RUNS, LANES)), OFF, 1)
        before = jnp.where(sub == 0, edge, before)
        after = pltpu.roll(pltpu.roll(own, RUNS - 1, 0), OFF + run, 1)
        edge = pltpu.roll(jnp.broadcast_to(right, (RUNS, LANES)), OFF + run, 1)
        after = jnp.where(sub == RUNS - 1, edge, after)
        ids = jnp.where(lane < OFF, before, jnp.where(lane < OFF + run, pltpu.roll(own, OFF, 1), after))
        place = base + lane - OFF
        real = (place >= 0) & (place < len_ref[r])
        real = real & (lane >= OFF - LEFT) & (lane < OFF + run + RIGHT)
        pack_ref[IDS, r * RUNS : (r + 1) * RUNS, :] = jnp.where(real, ids, -1).astype(f32)

    group = LANES // (rows * RUNS)
    ids = pack_ref[IDS].astype(jnp.bfloat16)
    eye = (iota((LANES, LANES), 0) == iota((LANES, LANES), 1)).astype(f32).astype(jnp.bfloat16)
    turned = lax.dot_general(eye, ids, NT, preferred_element_type=f32).astype(jnp.bfloat16)
    lined = jnp.zeros((line_ref.shape[0], LANES), f32)
    for i in range(group):
        shape = (line_ref.shape[0], LANES)
        take = (iota(shape, 1) == iota(shape, 0) * group + (i + OFF - LEFT)).astype(f32).astype(jnp.bfloat16)
        put = (iota((vr, LANES), 1) == iota((vr, LANES), 0) + i * vr).astype(f32).astype(jnp.bfloat16)
        some = jnp.dot(take, turned, preferred_element_type=f32).astype(jnp.bfloat16)
        lined = lined + jnp.dot(some, put, preferred_element_type=f32)
    line_ref[...] = lined

    seen_ref[...] = jnp.zeros_like(seen_ref)
    for copy in fetch[2:6]:
        copy.wait()
    embed = embed_ref[...]
    high, low = in_two(embed)
    split_ref[0] = high
    split_ref[1] = low

    taps = taps_ref[...]
    bias = bias_ref[...].reshape(1, feat)
    scorer = scorer_ref[...].reshape(1, feat)
    rows_ref[0:kernel, :] = taps
    rows_ref[BIAS : BIAS + 1, :] = bias
    rows_ref[SCORER : SCORER + 1, :] = scorer
    rows_ref[SCORER + 1 : 8, :] = jnp.zeros((7 - SCORER, feat), f32)
    for tile in range(feat // LANES):
        at = slice(tile % 4 * 8, tile % 4 * 8 + 8)
        pack_ref[WEIGHTS + tile // 4, at, :] = rows_ref[:, tile * LANES : (tile + 1) * LANES]
    table_ref[...] = jnp.zeros_like(table_ref)

    def inner(a, b):
        return lax.dot_general(a, b, NT, preferred_element_type=f32)

    def products(tile):
        cols = pl.ds(pl.multiple_of(tile * LANES, LANES), LANES)
        taps = rows_ref[0:kernel, cols]
        scaled = jnp.concatenate(
            [taps * rows_ref[SCORER : SCORER + 1, cols], taps * rows_ref[BIAS : BIAS + 1, cols]], axis=0
        )
        scaled = in_two(scaled)
        high, low = split_ref[0, :, cols], split_ref[1, :, cols]
        ones = jnp.ones((8, LANES), jnp.bfloat16)
        some = embed_ref[:, cols]
        squares = in_two(some * some)
        table_ref[0:8, :] = table_ref[0:8, :] + (
            inner(scaled[0], high) + (inner(scaled[0], low) + inner(scaled[1], high))
        )
        table_ref[8:16, :] = table_ref[8:16, :] + (inner(ones, squares[0]) + inner(ones, squares[1]))

    chunk = 2 * LANES
    lines = chunk // vr

    def embedding(step):
        marks = []
        for i in range(chunk // LANES):
            column = step * (chunk // LANES) + i
            bytes_here = jnp.broadcast_to(line_ref[pl.ds(column, 1), :], (vocab, LANES))
            marks.append(jnp.where(bytes_here == iota((vocab, LANES), 0).astype(f32), 1.0, 0.0))
            line = column * group + iota((1, LANES), 1) // vr
            inside = ((line >= LEFT) & (line < LEFT + run)).astype(f32)
            seen_ref[...] = seen_ref[...] + marks[i] * inside
        marks = jnp.concatenate(marks, axis=1).astype(jnp.bfloat16)
        turn_ref[:, pl.ds(pl.multiple_of(step * chunk, chunk), chunk)] = marks
        total = lax.dot_general(marks, split_ref[0], TN, preferred_element_type=f32)
        total = total + lax.dot_general(marks, split_ref[1], TN, preferred_element_type=f32)
        emb_ref[pl.ds(step * lines, lines)] = total.reshape(lines, vr, feat)

    def convolution(begin, end):
        for r in range(rows):
            sub = slice(r * RUNS, (r + 1) * RUNS)
            length = len_ref[r]
            for tile in range(feat // LANES):
                cols = slice(tile * LANES, (tile + 1) * LANES)
                taps = [jnp.broadcast_to(rows_ref[k : k + 1, cols], (RUNS, LANES)) for k in range(kernel)]
                window = [emb_ref[begin + k, sub, cols] for k in range(kernel - 1)]
                for i in range(begin, end):
                    window.append(emb_ref[i + kernel - 1, sub, cols])
                    total = taps[0] * window[0]
                    for k in range(1, kernel):
                        total = total + taps[k] * window[k]
                    window = window[1:]
                    real = base < length - (i - 2)
                    if i < 2:
                        real = real & (base >= 2 - i)
                    conv_ref[i, sub, cols] = jnp.where(real, total, 0.0)

    chunks, tiles = span // lines, feat // LANES
    done = 0
    for step in range(chunks):
        embedding(step)
        if step < tiles:
            products(step)
        ready = min(step * lines - (kernel - 1), run + 4)
        if ready > done:
            convolution(done, ready)
            done = ready
    for tile in range(chunks, tiles):
        products(tile)
    convolution(done, run + 4)
    for i in range(vocab // vr):
        seen = jnp.sum(seen_ref[i * vr : (i + 1) * vr, :], axis=1, keepdims=True)
        pack_ref[SEEN + i] = jnp.broadcast_to(seen, (vr, LANES))
    keeps = [
        pltpu.make_async_copy(turn_ref, mark_hbm, sems.at[1, 0]), pltpu.make_async_copy(emb_ref, emb_hbm, sems.at[1, 1])
    ]
    for copy in keeps:
        copy.start()

    size = RUNS * half
    order = iota((size, size), 0)
    order = (iota((size, size), 1) == order % RUNS * half + order // RUNS).astype(f32)
    order_ref[...] = order.astype(jnp.bfloat16)

    keeps.append(pltpu.make_async_copy(conv_ref, conv_hbm, sems.at[2, 0]))
    keeps[-1].start()

    block = 4
    slices = run + 4
    zero = jnp.zeros((RUNS, LANES), f32)
    def lagged(r, carry):
        at = pl.ds(pl.multiple_of(r * RUNS, RUNS), RUNS)
        some = grad_ref.at[pl.ds(pl.multiple_of(r * size, 8), size), :]
        for pair in range(feat // WIDE):
            wide = slice(pair * WIDE, (pair + 1) * WIDE)
            high, low = in_two(some[:, wide])
            moved = jnp.dot(order_ref[...], high, preferred_element_type=f32)
            moved = moved + jnp.dot(order_ref[...], low, preferred_element_type=f32)
            cot_ref[:, at, wide] = moved.reshape(half, RUNS, WIDE)
        values = [zero] * 6
        for first in range(0, slices, block):
            acc = {}
            for tile in range(feat // LANES):
                cols = slice(tile * LANES, (tile + 1) * LANES)
                u = [conv_ref[first + i, at, cols] for i in range(min(block + 5, slices - first))]
                for i in range(block):
                    for lag in range(min(6, slices - first - i)):
                        term = u[i] * u[i + lag]
                        acc[i, lag] = term if tile == 0 else acc[i, lag] + term
            for i, lag in acc:
                here = lane == first + (i + OFF - 2)
                values[lag] = jnp.where(here, jnp.sum(acc[i, lag], axis=1, keepdims=True), values[lag])
        for lag in range(6):
            pack_ref[lag, at, :] = values[lag]
        return carry

    fetch[6].wait()
    lax.fori_loop(0, rows, lagged, 0)
    keeps.append(pltpu.make_async_copy(cot_ref, cot_hbm, sems.at[3, 0]))
    keeps[-1].start()

    def total_of(x):
        return jnp.sum(jnp.sum(x, axis=1, keepdims=True), axis=0, keepdims=True)

    def lookups(r, sums):
        at = pl.ds(pl.multiple_of(r * RUNS, RUNS), RUNS)
        ids = pack_ref[IDS, at, :].astype(jnp.int32)
        real = ids >= 0
        low = jnp.where(real, ids, 0)

        def look(row):
            value = jnp.zeros((RUNS, LANES), f32)
            for part in range(vocab // LANES):
                entry = jnp.broadcast_to(
                    table_ref[row : row + 1, part * LANES : (part + 1) * LANES], (RUNS, LANES)
                )
                taken = jnp.take_along_axis(entry, low % LANES, axis=1)
                value = jnp.where(low // LANES == part, taken, value)
            return jnp.where(real, value, 0.0)

        scored = jnp.zeros((RUNS, LANES), f32)
        biased = jnp.zeros((RUNS, LANES), f32)
        for k in range(kernel):
            scored = scored + shifted(look(k), k - (kernel - 1))
            biased = biased + shifted(look(4 + k), k - (kernel - 1))
        inner_real = real & (lane >= OFF - 2)
        scored = jnp.where(inner_real, scored, 0.0)
        biased = jnp.where(inner_real, biased, 0.0)
        pack_ref[13, at, :] = scored
        pack_ref[14, at, :] = biased
        own = (real & (lane >= OFF) & (lane < OFF + run)).astype(f32)
        new = (own * look(8), own, own * biased, own * pack_ref[0, at, :], own * (1 - lane % 2).astype(f32))
        return tuple(a + b for a, b in zip(sums, new))

    def crossed(r, sums):
        at = pl.ds(pl.multiple_of(r * RUNS, RUNS), RUNS)
        sums = lookups(r, sums)
        values = [zero] * 7
        for first in range(0, half, block):
            acc = {}
            for tile in range(feat // LANES):
                cols = slice(tile * LANES, (tile + 1) * LANES)
                u = [conv_ref[2 * first + i, at, cols] for i in range(2 * block + 4)]
                bias = jnp.broadcast_to(rows_ref[BIAS : BIAS + 1, tile * LANES : (tile + 1) * LANES], (RUNS, LANES))
                for i in range(block):
                    g = cot_ref[first + i, at, cols]
                    terms = [g * u[2 * i + d] for d in range(6)] + [g * bias]
                    for d in range(7):
                        acc[i, d] = terms[d] if tile == 0 else acc[i, d] + terms[d]
            for i, d in acc:
                here = lane == 2 * first + (2 * i + OFF)
                values[d] = jnp.where(here, jnp.sum(acc[i, d], axis=1, keepdims=True), values[d])
        for d in range(7):
            pack_ref[6 + d, at, :] = values[d]
        return sums

    sums = lax.fori_loop(0, rows, crossed, (zero,) * 5)
    sums_ref[...] = spread([total_of(x) for x in sums], sums_ref.shape[0])
    for copy in keeps:
        copy.wait()


def in_two(x):
    high = x.astype(jnp.bfloat16)
    return high, (x - high.astype(f32)).astype(jnp.bfloat16)


def unpack_rows(pack_ref, rows_ref):
    for tile in range(rows_ref.shape[1] // LANES):
        at = slice(tile % 4 * 8, tile % 4 * 8 + 8)
        rows_ref[:, tile * LANES : (tile + 1) * LANES] = pack_ref[WEIGHTS + tile // 4, at, :]


def spread(sums, count):
    lane = iota((1, LANES), 1)
    row = jnp.zeros((1, LANES), f32)
    for i, x in enumerate(sums):
        row = jnp.where(lane == i, x, row)
    return jnp.broadcast_to(row[None], (count, 1, LANES))


def picked(ref, number):
    row = jnp.sum(ref[...], axis=0)
    return [row[:, i : i + 1] for i in range(number)]


def scales(first_ref, bias, feat):
    emb_sum, count, cross, square, count4 = picked(first_ref, 5)
    one = jnp.sqrt(emb_sum / (count * feat) + EPS)
    bias_sum = jnp.sum(bias * bias, axis=1, keepdims=True)
    conv_sum = jnp.maximum(count * bias_sum + 2.0 * cross / one + square / (one * one), 0.0)
    two = jnp.sqrt(conv_sum / (count * feat) + EPS)
    return one, two, count, count4, bias_sum, cross


class Places:
    def __init__(self, ids, start, run):
        shape = ids.shape
        self.j = iota(shape, 1) - OFF
        sub = iota(shape, 0) % RUNS
        self.inside = (self.j >= 0) & (self.j < run)
        self.real = ((ids >= 0) & (self.j >= -2)).astype(f32)
        self.own = jnp.where(self.inside, self.real, 0.0)
        shown = self.j + OFF
        self.two, self.four = shown % 2, shown % 4
        self.three = (start + run * sub + shown + (3 * OFF - OFF)) % 3

    def holds(self, size, by):
        if size == 1:
            return jnp.ones_like(self.real) if by == 0 else None
        if abs(by) >= size:
            return None
        phase = {2: self.two, 3: self.three, 4: self.four}[size]
        return ((phase + by >= 0) & (phase + by < size)).astype(f32)

    def pooled(self, size, x):
        if size == 1:
            return x
        pair = x + jnp.where(self.two == 0, shifted(x, 1), shifted(x, -1))
        if size == 2:
            return pair
        if size == 4:
            return pair + jnp.where(self.four < 2, shifted(pair, 2), shifted(pair, -2))
        left, right = shifted(x, -1), shifted(x, 1)
        side = jnp.where(self.three == 0, shifted(x, 2), left)
        far = jnp.where(self.three == 2, shifted(x, -2), right)
        return x + side + far

    def both(self, x):
        return x + shifted(x, -1)


SIZES = (1, 2, 3, 4)
REACH = range(-3, 4)


def score_kernel(sizes, first_hbm, dots_hbm, state_hbm, sums_ref, first_ref, dots_ref, state_ref, rows_ref, sems):
    rows, width, run, feat, vocab, kernel = sizes
    fetch = (
        pltpu.make_async_copy(dots_hbm.at[0:SEEN], dots_ref, sems.at[0]),
        pltpu.make_async_copy(first_hbm, first_ref, sems.at[1]),
    )
    for copy in fetch:
        copy.start()
    for copy in fetch:
        copy.wait()
    start = lax.axis_index("seq") * width
    unpack_rows(dots_ref, rows_ref)
    bias = rows_ref[BIAS : BIAS + 1, :]
    one, two, count, count4, bias_sum, cross = scales(first_ref, bias, feat)
    at = Places(dots_ref[IDS], start, run)
    real, own = at.real, at.own
    rate = 1.0 / (one * two)
    bias_score = jnp.sum(bias * rows_ref[SCORER : SCORER + 1, :], axis=1, keepdims=True) / two

    normed_score = real * bias_score + rate * dots_ref[13]
    counts = [jnp.maximum(at.pooled(b, real), 1.0) for b in SIZES]
    scores = [at.pooled(b, normed_score) / n for b, n in zip(SIZES, counts)]
    top = functools.reduce(jnp.maximum, scores)
    parts = [jnp.exp(s - top) for s in scores]
    whole = sum(parts)
    probs = [p / whole for p in parts]
    weights = [own * p / n for p, n in zip(probs, counts)]

    for i in range(4):
        state_ref[i] = weights[i]
        state_ref[4 + i] = probs[i]
    early = pltpu.make_async_copy(state_ref.at[0:8], state_hbm.at[0:8], sems.at[2])
    early.start()
    holds = {(b, d): at.holds(b, d) for b in SIZES for d in REACH}

    def blend(values):
        out = {}
        for d in REACH:
            terms = [v * holds[b, d] for b, v in zip(SIZES, values) if holds[b, d] is not None]
            out[d] = sum(terms)
        return out

    mixer = blend(weights)
    pair_count = jnp.maximum(at.pooled(2, real), 1.0)
    halver = {}
    even = at.two == 0
    for d in REACH:
        zero = jnp.zeros_like(real)
        ahead = shifted(mixer[d - 1], 1) if d - 1 >= -3 else zero
        behind = shifted(mixer[d + 1], -1) if d + 1 <= 3 else zero
        other = jnp.where(even, ahead, behind)
        halver[d] = jnp.where(at.inside, (mixer[d] + other) / pair_count, 0.0)

    bias_dot = dots_ref[14]
    normed_bias = real * (bias_sum / two) + rate * bias_dot
    lags = []
    for lag in range(6):
        later = shifted(real, lag)
        value = rate * rate * dots_ref[lag]
        value = value + (rate / two) * (bias_dot * later + real * shifted(bias_dot, lag))
        lags.append(value + (bias_sum / (two * two)) * (real * later))

    def gram(a, b):
        low, high = min(a, b), max(a, b)
        return shifted(lags[high - low], low) if high - low < 6 else None

    table = {(a, b): gram(a, b) for a in REACH for b in REACH if a <= b}

    def against(weighting):
        out = {}
        for a in REACH:
            out[a] = sum(
                weighting[b] * table[min(a, b), max(a, b)]
                for b in REACH if table[min(a, b), max(a, b)] is not None
            )
        return out

    with_mixed, with_half = against(mixer), against(halver)
    with_grad = {}
    grad_bias = dots_ref[12]
    cross_dots = {
        d: rate * dots_ref[6 + d + 2] + shifted(real, d) * (grad_bias / two) for d in range(-2, 4)
    }
    for d in REACH:
        here = cross_dots[d] if d >= -2 else jnp.zeros_like(real)
        before = shifted(cross_dots[d + 1], -1) if d + 1 <= 3 else jnp.zeros_like(real)
        with_grad[d] = jnp.where(even, here, before)

    def per_block(values, scale):
        out = []
        for b, n in zip(SIZES, counts):
            terms = [values[d] * holds[b, d] for d in REACH if holds[b, d] is not None]
            out.append(scale * sum(terms) / n)
        return out

    shared = own / pair_count
    bases = [per_block(with_grad, shared), per_block(with_half, shared), per_block(with_mixed, own)]

    for i in range(4):
        for f in range(3):
            state_ref[8 + 4 * f + i] = bases[f][i]
    late = pltpu.make_async_copy(state_ref.at[8:], state_hbm.at[8:], sems.at[3])
    late.start()

    def total_of(x):
        return jnp.sum(jnp.sum(x, axis=1, keepdims=True), axis=0, keepdims=True)

    first_of_pair = jnp.where(even & at.inside, 1.0, 0.0)
    mean_score = sum(p * s for p, s in zip(probs, scores))

    def bent(values):
        mean = sum(p * v for p, v in zip(probs, values))
        return total_of(own * (sum(p * s * v for p, s, v in zip(probs, scores, values)) - mean * mean_score))

    sums = [
        total_of(sum(own * mixer[d] * with_mixed[d] for d in REACH)),
        total_of(first_of_pair * sum(halver[d] * with_half[d] for d in REACH)),
        total_of(first_of_pair * sum(halver[d] * with_grad[d] for d in REACH)),
        bent(bases[0]), bent(bases[1]), bent(bases[2]),
        total_of(shared * at.both(grad_bias)),
        total_of(shared * sum(halver[d] * shifted(normed_bias, d) for d in REACH)),
        total_of(own * sum(mixer[d] * shifted(normed_bias, d) for d in REACH)),
    ]
    sums_ref[...] = spread(sums, sums_ref.shape[0])
    early.wait()
    late.wait()


def back_kernel(
    sizes, first_hbm, second_hbm, pack_hbm, state_hbm, mark_hbm, embed_hbm, conv_hbm, emb_hbm, cot_hbm,
    out_hbm, keep_ref, send_ref,
    first_ref, second_ref, pack_ref, state_ref, mark_ref, embed_ref, rows_ref, turn_ref, out_ref, order_ref,
    narrow_ref, acc_ref, pay_ref, conv_ref, emb_ref, cot_ref, back_ref, sems,
):
    rows, width, run, feat, vocab, kernel = sizes
    tiles = feat // LANES
    per = WIDE // LANES
    units = rows * (feat // WIDE)
    half = run // 2
    vr = rows * RUNS

    def fetches(unit):
        sub = pl.ds(pl.multiple_of(unit % rows * RUNS, RUNS), RUNS)
        cols = pl.ds(pl.multiple_of(unit // rows * WIDE, LANES), WIDE)
        return [
            pltpu.make_async_copy(a.at[:, sub, cols], b.at[:, sub, cols], sems.at[i, unit])
            for i, (a, b) in enumerate(((conv_hbm, conv_ref), (cot_hbm, cot_ref), (emb_hbm, emb_ref)))
        ]

    size = RUNS * half

    def stored(unit):
        some = pl.ds(pl.multiple_of(unit % rows * size, 8), size)
        cols = pl.ds(pl.multiple_of(unit // rows * WIDE, LANES), WIDE)
        return pltpu.make_async_copy(out_ref.at[some, cols], out_hbm.at[some, cols], sems.at[3, unit])

    def restore(unit):
        some = pl.ds(pl.multiple_of(unit % rows * size, 8), size)
        cols = pl.ds(pl.multiple_of(unit // rows * WIDE, LANES), WIDE)
        high, low = in_two(turn_ref[...].reshape(size, WIDE))
        moved = jnp.dot(order_ref[...], high, preferred_element_type=f32)
        out_ref[some, cols] = moved + jnp.dot(order_ref[...], low, preferred_element_type=f32)

    sources = (first_hbm, second_hbm, pack_hbm, state_hbm, mark_hbm, embed_hbm)
    targets = (first_ref, second_ref, pack_ref, state_ref, mark_ref, embed_ref)
    small = [pltpu.make_async_copy(a, b, sems.at[4, i]) for i, (a, b) in enumerate(zip(sources, targets))]
    small[2] = pltpu.make_async_copy(pack_hbm.at[IDS:], pack_ref.at[IDS:], sems.at[4, 2])
    ahead = 3
    for copy in small[:4]:
        copy.start()
    for unit in range(ahead):
        for copy in fetches(unit):
            copy.start()
    for copy in small[4:]:
        copy.start()
    order = iota((size, size), 0)
    order = (iota((size, size), 1) == order % half * RUNS + order // half).astype(f32)
    order_ref[...] = order.astype(jnp.bfloat16)
    turn_ref[...] = jnp.zeros_like(turn_ref)
    acc_ref[...] = jnp.zeros_like(acc_ref)
    for copy in small[:4]:
        copy.wait()

    start = lax.axis_index("seq") * width
    unpack_rows(pack_ref, rows_ref)
    bias = rows_ref[BIAS : BIAS + 1, :]
    one, two, count, count4, bias_sum, cross = scales(first_ref, bias, feat)
    mixed_sum, half_sum, inner, bent_g, bent_h, bent_m, bias_g, bias_h, bias_m = picked(second_ref, 9)
    volume, volume4 = count * feat, count4 * feat
    three = jnp.sqrt(mixed_sum / volume + EPS)
    four = jnp.sqrt(half_sum / (three * three) / volume4 + EPS)
    fourth = (inner / three) / (four * four * four * volume4)
    alpha = 1.0 / (three * four)
    beta = -fourth / (three * three)
    gamma = -(inner / four - fourth / three * half_sum) / (three * three * three * volume)
    joint = alpha * (inner + bent_g) + beta * (half_sum + bent_h) + gamma * (mixed_sum + bent_m)
    rate = 1.0 / (one * two)
    normed_bias = count * bias_sum / two + rate * cross
    bias_back = (alpha * bias_g + beta * bias_h + gamma * bias_m - joint / volume * normed_bias) / two
    inner_one = one * (joint * EPS / (two * two) - bias_back)
    first_coef = inner_one / (one * one * one * volume)

    at = Places(pack_ref[IDS], start, run)
    probs = [state_ref[4 + i] for i in range(4)]
    weights = [state_ref[i] for i in range(4)]
    grads = [
        alpha * state_ref[8 + i] + beta * state_ref[12 + i] + gamma * state_ref[16 + i] for i in range(4)
    ]
    mean = sum(p * g for p, g in zip(probs, grads))
    spreading = jnp.zeros_like(probs[0])
    for i, b in enumerate(SIZES):
        bent = probs[i] * (grads[i] - mean)
        n = jnp.maximum(at.pooled(b, at.real), 1.0)
        spreading = spreading + at.pooled(b, jnp.where(at.inside, bent / n, 0.0))
    pair_real = at.pooled(2, at.real)
    pair_count = jnp.maximum(pair_real, 1.0)
    filled = (pair_real > 0).astype(f32)
    narrow = [rate * w for w in weights] + [rate * spreading, at.real]
    paired = [
        alpha / pair_count, alpha * filled, beta / (pair_count * pair_count), beta * filled / pair_count + gamma
    ]
    leak = jnp.sum(jnp.sum(spreading * at.real, axis=1, keepdims=True), axis=0, keepdims=True)

    for i, x in enumerate(narrow + paired):
        narrow_ref[i] = x
    phase = (start + run * iota((RUNS, LANES), 0)) % 3
    at_phase = [phase == p for p in range(3)]

    def chosen(j, a, b, c):
        return jnp.where(at_phase[(0 - j) % 3], a, jnp.where(at_phase[(1 - j) % 3], b, c))

    full = (RUNS, LANES)
    alpha_all = jnp.broadcast_to(alpha, full)
    gamma_all = jnp.broadcast_to(gamma, full)
    fall = jnp.broadcast_to(rate * rate * joint / volume, full)
    fall_bias = rate * joint / volume / two

    def column(r, tile, near, factor):
        sub = pl.ds(pl.multiple_of(r * RUNS, RUNS), RUNS)
        cols = pl.ds(pl.multiple_of(tile * LANES, LANES), LANES)
        taps = [jnp.broadcast_to(rows_ref[k : k + 1, cols], full) for k in range(kernel)]
        bias_row = rows_ref[BIAS : BIAS + 1, cols]
        normed_row = jnp.broadcast_to(bias_row / two, full)
        fall_row = jnp.broadcast_to(bias_row * fall_bias, full)
        scorer = jnp.broadcast_to(rows_ref[SCORER : SCORER + 1, cols], full)
        zero = jnp.zeros(full, f32)

        u, triple, y3, gc = {}, {}, {}, {}
        sums = [zero] * (kernel + 2)
        block = {}
        twos, y_twos = {}, {}
        for j in range(-2, 2):
            u[j] = conv_ref[j + 2, sub, cols]

        def pair_of(j):
            if j not in twos:
                twos[j] = u[j] + u[j + 1]
            return twos[j]

        triple[-2] = pair_of(-2) + u[0]
        triple[-1] = u[-1] + pair_of(0)

        def window(j):
            if 0 <= j <= run - 3:
                first = j if j % 2 == 0 else j + 1
                if first not in y_twos:
                    y_twos[first] = y3[first] + y3[first + 1]
                return y_twos[first] + y3[j + 2 if j % 2 == 0 else j]
            near = [y3[i] for i in (j, j + 1, j + 2) if 0 <= i < run]
            return functools.reduce(lambda a, b: a + b, near) if near else zero

        def settle(s):
            nonlocal sums
            for j in (s, s - 1, s - 2):
                if j not in block:
                    block[j] = window(j)
            g = chosen(s, block[s], block[s - 1], block[s - 2])
            sigma = factor(4, s)
            g = g + sigma * scorer
            if 0 <= s < run:
                g = g + lone[s]
                g = g - fall * u[s]
            g = g * factor(5, s)
            gc[s] = g
            for k in range(kernel):
                sums[k] = sums[k] + g * emb_ref[s - kernel + 1 + k + LEFT, sub, cols]
            sums[kernel] = sums[kernel] + g
            sums[kernel + 1] = sums[kernel + 1] + sigma * u[s]

        def finish(s):
            terms = [taps[k] * gc[s + kernel - 1 - k] for k in range(kernel) if s + kernel - 1 - k in gc]
            back_ref[s + LEFT, sub, cols] = functools.reduce(lambda a, b: a + b, terms)

        lone = {}
        settled = -2
        finished = -LEFT
        for quad in range(0, run, 4):
            for j in range(quad + 2, quad + 6):
                u[j] = conv_ref[j + 2, sub, cols]
            two_sums = [pair_of(quad), pair_of(quad + 2)]
            four_sum = two_sums[0] + two_sums[1]
            shares = []
            wide = zero
            for p in range(2):
                y = None
                xs = []
                for j in (quad + 2 * p, quad + 2 * p + 1):
                    triple[j] = u[j] + pair_of(j + 1) if j % 2 else two_sums[p] + u[j + 2]
                    x = factor(0, j) * u[j] + factor(1, j) * two_sums[p]
                    x = x + factor(2, j) * chosen(j, triple[j], triple[j - 1], triple[j - 2])
                    x = x + factor(3, j) * four_sum
                    xs.append(x)
                y = xs[0] + xs[1]
                k = quad // 2 + p
                scale_y = factor(6, 2 * k)
                turn_ref[k, :, near] = scale_y * y + factor(7, 2 * k) * normed_row
                q = scale_y * cot_ref[k, sub, cols] + factor(8, 2 * k) * y + factor(9, 2 * k) * normed_row
                pair = zero
                for i, j in enumerate((quad + 2 * p, quad + 2 * p + 1)):
                    g = q + gamma_all * xs[i]
                    lone[j] = factor(0, j) * g
                    y3[j] = factor(2, j) * g
                    pair = factor(1, j) * g if i == 0 else pair + factor(1, j) * g
                    wide = factor(3, j) * g if i + p == 0 else wide + factor(3, j) * g
                shares.append(pair)
            wide = wide - fall_row
            for p in range(2):
                share = shares[p] + wide
                for j in (quad + 2 * p, quad + 2 * p + 1):
                    lone[j] = lone[j] + share
            last = quad + 3 - 2 if quad + 4 < run else run + 1
            while settled <= last:
                settle(settled)
                settled += 1
            done = settled - kernel if quad + 4 < run else run + RIGHT - 1
            while finished <= done:
                finish(finished)
                finished += 1
            yield
        for i in range(kernel + 2):
            acc_ref[i, :, cols] = acc_ref[i, :, cols] + sums[i]

    def some_columns(unit, carry):
        for copy in fetches(unit):
            copy.wait()

        @pl.when(unit + ahead < units)
        def _():
            for copy in fetches(unit + ahead):
                copy.start()

        r = unit % rows
        made = {}

        def factor(i, j):
            if (i, j) not in made:
                sub = pl.ds(pl.multiple_of(r * RUNS, RUNS), RUNS)
                made[i, j] = jnp.broadcast_to(narrow_ref[i, sub, j + OFF : j + OFF + 1], full)
            return made[i, j]

        last = jnp.maximum(unit - 1, 0)
        restore(last)
        parts = []
        for i in range(per):
            near = slice(i * LANES, (i + 1) * LANES)
            parts.append(column(r, unit // rows * per + i, near, factor))
        for _ in zip(*parts, strict=True):
            pass

        @pl.when(unit > 0)
        def _():
            stored(last).start()

        return carry

    lax.fori_loop(0, units, some_columns, 0)
    restore(units - 1)
    stored(units - 1).start()

    positions = mark_ref.shape[1]
    edge = run + LEFT + RIGHT
    back_ref[edge:] = jnp.zeros((back_ref.shape[0] - edge, vr, feat), f32)
    for copy in small[4:]:
        copy.wait()
    total_tiles = pay_ref.shape[0]

    def gather(pair, carry):
        cols = pl.ds(pl.multiple_of(pair * WIDE, LANES), WIDE)
        high, low = in_two(back_ref[:, :, cols].reshape(positions, WIDE))
        total = jnp.dot(mark_ref[...], high, preferred_element_type=f32)
        total = total + jnp.dot(mark_ref[...], low, preferred_element_type=f32)
        for v in range(vocab // 8):
            seen = first_coef * pack_ref[SEEN + v * 8 // vr, v * 8 % vr : v * 8 % vr + 8, :]
            for i in range(per):
                wide = pl.ds(pl.multiple_of(pair * WIDE + i * LANES, LANES), LANES)
                part = total[v * 8 : v * 8 + 8, i * LANES : (i + 1) * LANES]
                pay_ref[v * tiles + pair * per + i] = part - seen * embed_ref[v * 8 : v * 8 + 8, wide]
        return carry

    for pair in range(feat // WIDE):
        gather(pair, 0)

    end = vocab // 8 * tiles
    pay_ref[end:] = jnp.zeros((total_tiles - end, 8, LANES), f32)
    for i in range(kernel + 2):
        row = jnp.sum(acc_ref[i], axis=0, keepdims=True)
        if i == kernel:
            row = row * one
        if i == kernel + 1:
            row = row + bias * (leak / two)
        for tile in range(tiles):
            place = i * tiles + tile
            pay_ref[end + place // 8, place % 8 : place % 8 + 1, :] = row[:, tile * LANES : (tile + 1) * LANES]
    core = lax.axis_index("seq") % 2
    part = total_tiles // 2
    keep_ref[...] = pay_ref[pl.ds(core * part, part)]
    send_ref[...] = pay_ref[pl.ds((1 - core) * part, part)]
    for unit in range(units):
        stored(unit).wait()


def finish_kernel(feat, mine_ref, other_ref, table_hbm, taps_ref, bias_ref, scorer_ref, sems):
    core = lax.axis_index("seq") % 2
    tiles = feat // LANES
    part = mine_ref.shape[0]
    rest = table_hbm.shape[0] - part
    for side in range(2):

        @pl.when(core == side)
        def _():
            first, second = (mine_ref, other_ref) if side == 0 else (other_ref, mine_ref)
            copies = (
                pltpu.make_async_copy(first, table_hbm.at[0:part], sems.at[0]),
                pltpu.make_async_copy(second.at[0:rest], table_hbm.at[part : part + rest], sems.at[1]),
            )
            for copy in copies:
                copy.start()
            lines = []
            for i in range(taps_ref.shape[0] + 2):
                places = [i * tiles + tile for tile in range(tiles)]
                lines.append([second[rest + p // 8, p % 8 : p % 8 + 1, :] for p in places])
            for i in range(taps_ref.shape[0]):
                taps_ref[i : i + 1, :] = jnp.concatenate(lines[i], axis=1)
            bias_ref[...] = jnp.concatenate(lines[-2], axis=1).reshape(feat)
            scorer_ref[...] = jnp.concatenate(lines[-1], axis=1).reshape(feat)
            for copy in copies:
                copy.wait()


def exchanged(x):
    return lax.all_to_all(x, AXES, 0, 0, tiled=True)


def partner(x, axis, step):
    n = lax.axis_size(axis)
    return lax.ppermute(x, axis, [(i, i ^ step) for i in range(n)])


def summed_over_devices(keep, send):
    n = lax.axis_size("seq")
    others = lax.axis_size("rows") * n // 2
    groups = [[2 * i + side for i in range(others)] for side in range(2)]

    def traded(x):
        return lax.all_to_all(x, AXES, 0, 0, tiled=True, axis_index_groups=groups)

    x = keep + partner(send, "seq", 1)
    chunk = (others, x.shape[0] * x.shape[1] // others, 1, LANES)
    part = jnp.sum(traded(x.reshape(chunk)), axis=0)
    x = traded(jnp.broadcast_to(part[None], chunk)).reshape(x.shape)
    return x, partner(x, "seq", 1)


def on_device(byte_ids, lengths, embed, conv_weight, conv_bias, score_weight, out_grad):
    rows, width = byte_ids.shape
    vocab, feat = embed.shape
    kernel = conv_weight.shape[0]
    run = width // RUNS
    half = width // 2
    vr = rows * RUNS
    sizes = (rows, width, run, feat, vocab, kernel)
    count = lax.axis_size("seq")
    devices = count * lax.axis_size("rows")
    span = -(-(run + LEFT + RIGHT) // 8) * 8
    tiles = feat // LANES
    struct = jax.ShapeDtypeStruct
    sem = pltpu.SemaphoreType.DMA

    params = pltpu.CompilerParams(vmem_limit_bytes=60 * 1024 * 1024)

    pairs_of = [[(i, i + 1) for i in range(first, count - 1, 2)] for first in range(2)]
    near = [lax.ppermute(byte_ids, "seq", some + [(j, i) for i, j in some]) for some in pairs_of]
    near = [pltpu.with_memory_space_constraint(x, pltpu.VMEM) for x in near]

    pairs = feat // WIDE
    bf16 = jnp.bfloat16
    wide_emb = struct((span, vr, feat), f32)
    wide_conv = struct((run + 4, vr, feat), f32)
    wide_cot = struct((half // RUNS, vr, feat), f32)
    marks = struct((vocab, span * vr), bf16)
    pack = struct((SEEN + vocab // vr, vr, LANES), f32)
    sums = struct((devices, 1, LANES), f32)
    state = struct((20, vr, LANES), f32)

    def scratch(like):
        return pltpu.VMEM(like.shape, like.dtype)

    emb, conv, cot, mark, packed, first = pl.pallas_call(
        functools.partial(stats_kernel, sizes),
        out_shape=(*(pltpu.HBM(x.shape, x.dtype) for x in (wide_emb, wide_conv, wide_cot, marks, pack)), pltpu.VMEM(sums.shape, f32)),
        in_specs=[HBM, VMEM, VMEM] + [HBM] * 6, out_specs=(HBM,) * 4 + (VMEM,) * 2,
        scratch_shapes=[
            scratch(byte_ids), pltpu.SMEM((rows,), jnp.int32), scratch(embed),
            scratch(conv_weight), scratch(conv_bias), scratch(score_weight), pltpu.VMEM((rows * half, feat), f32),
            pltpu.VMEM((2, vocab, feat), bf16), pltpu.VMEM((16, vocab), f32), pltpu.VMEM((8, feat), f32),
            scratch(marks), pltpu.VMEM((-(-span * vr // LANES // 8) * 8, LANES), f32), pltpu.VMEM((vocab, LANES), f32),
            pltpu.VMEM((half, half), bf16), pltpu.VMEM((vr, LANES), jnp.int32), scratch(wide_emb),
            scratch(wide_conv), scratch(wide_cot), sem((4, 9)),
        ],
        compiler_params=params, name="stats",
    )(
        byte_ids, *near, lengths, embed, conv_weight, conv_bias, score_weight,
        out_grad.reshape(rows * half, feat),
    )
    first = exchanged(first)

    states, second = pl.pallas_call(
        functools.partial(score_kernel, sizes),
        out_shape=(pltpu.HBM(state.shape, f32), pltpu.VMEM(sums.shape, f32)),
        in_specs=[HBM] * 2, out_specs=(HBM, VMEM),
        scratch_shapes=[
            scratch(sums), pltpu.VMEM((SEEN, vr, LANES), f32), scratch(state), pltpu.VMEM((8, feat), f32), sem((4,)),
        ],
        compiler_params=params, name="score",
    )(first, packed)
    second = exchanged(second)

    lines = vocab * tiles
    lines = -(-(lines + (kernel + 2) * tiles) // devices) * devices
    parts = struct((lines // 16, 8, LANES), f32)
    blocks, keep, send = pl.pallas_call(
        functools.partial(back_kernel, sizes),
        out_shape=(pltpu.HBM((rows * half, feat), f32), pltpu.VMEM(parts.shape, f32), pltpu.VMEM(parts.shape, f32)),
        in_specs=[HBM] * 9, out_specs=(HBM, VMEM, VMEM),
        scratch_shapes=[
            scratch(sums), scratch(sums), scratch(pack), scratch(state), scratch(marks), scratch(embed),
            pltpu.VMEM((8, feat), f32), pltpu.VMEM((half // RUNS, RUNS, WIDE), f32),
            pltpu.VMEM((rows * half, feat), f32), pltpu.VMEM((half, half), bf16), pltpu.VMEM((10, vr, LANES), f32),
            pltpu.VMEM((kernel + 2, RUNS, feat), f32), pltpu.VMEM((lines // 8, 8, LANES), f32),
            scratch(wide_conv), scratch(wide_emb), scratch(wide_cot), scratch(wide_emb),
            sem((5, max(6, rows * pairs))),
        ],
        compiler_params=params, name="back",
    )(first, second, packed, states, mark, embed, conv, emb, cot)

    mine, other = summed_over_devices(keep, send)
    table, taps_grad, bias_grad, scorer_grad = pl.pallas_call(
        functools.partial(finish_kernel, feat),
        out_shape=(
            pltpu.HBM((vocab * tiles // 8, 8, LANES), f32), struct((kernel, feat), f32), struct((feat,), f32),
            struct((feat,), f32),
        ),
        in_specs=[VMEM, VMEM], out_specs=(HBM, VMEM, VMEM, VMEM), scratch_shapes=[sem((2,))],
        compiler_params=pltpu.CompilerParams(vmem_limit_bytes=8 * 1024 * 1024), name="finish",
    )(mine, other)
    table = table.reshape(vocab // 8, tiles, 8, LANES).transpose(0, 2, 1, 3).reshape(vocab, feat)
    return blocks.reshape(rows, half, feat), table, taps_grad, bias_grad, scorer_grad


def solution(mesh):
    placed = (P("rows", "seq"), P("rows"), P(), P(), P(), P(), P("rows", "seq", None))
    return jax.shard_map(
        on_device,
        mesh=mesh,
        in_specs=placed,
        out_specs=(P("rows", "seq", None), P(), P(), P(), P()),
        check_vma=False,
    )
```
